512 devices in a mesh: lon: 16 (over z), lat: 8 (over x, y_lo), ens: 4 (over y_hi, core).
Axes of the slice: x: 4, y: 4 (y_hi: 2, y_lo: 2; y = y_hi * 2 + y_lo), z: 16, core: 2. Of those that a mesh axis runs over, the one named last changes fastest.
Arguments:
- field: bfloat16 [4, 128, 1024, 128], P('ens', 'lat', 'lon'), may hold values from -6 to 6
- cotangent: bfloat16 [4, 128, 1024, 128], P('ens', 'lat', 'lon'), may hold values from -6 to 6
- land_mask: int32 [128, 1024], P('lat', 'lon'), may hold values from 0 to 1, as said below
- kernel_taps: float32 [49, 128], replicated, may hold values from -0.875 to 0.875
- norm_gain: float32 [128], replicated, may hold values from 0.1 to 1.9
- norm_shift: float32 [128], replicated, may hold values from -3 to 3
- up_weight: bfloat16 [128, 256], replicated, may hold values from -0.5 to 0.5
- down_weight: bfloat16 [256, 128], replicated, may hold values from -0.375 to 0.375
Outputs:
- output: bfloat16 [4, 128, 1024, 128], P('ens', 'lat', 'lon')
- field_grad: bfloat16 [4, 128, 1024, 128], P('ens', 'lat', 'lon')
- kernel_grad: float32 [49, 128], replicated
- norm_grad: float32 [2, 128], replicated
- up_grad: float32 [128, 256], replicated
- down_grad: float32 [256, 128], replicated
The draws below stay inside these ranges and needn't reach their ends.
Inputs may be any that keep to these rules, and one draw needn't show every extreme that they name: `land_mask`: 1 marks an ocean cell and 0 a land cell; the share of ocean differs from tile to tile.
All inputs are finite; a program needn't handle non-finite values.
Results may differ from the reference program's by a relative error of at most 0.0062.
Values may be sent and summed in bfloat16 or wider, within the bound.
A program may use at most 64 MiB of HBM per device.

```python
import math
import jax
import jax.numpy as jnp
from jax import lax

CHANNELS = 128
HIDDEN_SIZE = 256
KERNEL = 7
DILATION = 2
REACH = 6
TILE_LAT = 16
TILE_LON = 64
MEMBERS = 4
GRID_LAT = 128
GRID_LON = 1024


def draw_land_mask(key, part):
    level_key = jax.random.fold_in(key, 11)
    cell_key = jax.random.fold_in(key, 23)
    levels = jax.random.randint(level_key, (GRID_LAT // TILE_LAT, GRID_LON // TILE_LON), 0, 5)
    spread = jnp.repeat(jnp.repeat(levels, TILE_LAT, 0), TILE_LON, 1)
    cells = jax.random.randint(cell_key, (GRID_LAT, GRID_LON), 0, 4)
    return (cells < spread).astype(jnp.int32)


def block_scale(rng, extent, split, least, top_value):
    def one(position, parts):
        heights = jax.random.uniform(jax.random.fold_in(jax.random.fold_in(rng, 6), position), (parts,), jnp.float32, least / len(split), top_value / len(split))
        return jnp.repeat(jnp.exp(heights), extent[position] // parts).reshape((-1,) + (1,) * (len(extent) - position - 1))

    gain = one(*split[0])
    for cut in split[1:]:
        gain = gain * one(*cut)
    return gain


def bell_draw(key, dims, width, most, shards=(), held_as=jnp.bfloat16):
    values = width * jax.random.normal(key, dims, jnp.float32)
    if shards:
        values = values * block_scale(key, dims, shards, -0.22, 0.18)
    return jnp.clip(values, -most, most).astype(held_as)


def setup_inputs(seed: int = 0) -> dict:
    arg_keys = jax.random.split(jax.random.key(seed), 9)
    return {
        "field": bell_draw(arg_keys[0], (MEMBERS, GRID_LAT, GRID_LON, CHANNELS), 1.0, 6.0, ((0, 4), (1, 8), (2, 16))),
        "cotangent": bell_draw(arg_keys[1], (MEMBERS, GRID_LAT, GRID_LON, CHANNELS), 1.0, 6.0, ((0, 4), (1, 8), (2, 16))),
        "land_mask": draw_land_mask(jax.random.fold_in(arg_keys[8], 71), 0),
        "kernel_taps": bell_draw(arg_keys[3], (KERNEL * KERNEL, CHANNELS), (KERNEL * KERNEL) ** -0.5, 0.875, (), jnp.float32),
        "norm_gain": jnp.clip(1.0 + 0.18 * jax.random.normal(arg_keys[4], (CHANNELS,), jnp.float32), 0.1, 1.9),
        "norm_shift": bell_draw(arg_keys[5], (CHANNELS,), 0.5, 3.0, (), jnp.float32),
        "up_weight": bell_draw(arg_keys[6], (CHANNELS, HIDDEN_SIZE), CHANNELS ** -0.5, 0.5),
        "down_weight": bell_draw(arg_keys[7], (HIDDEN_SIZE, CHANNELS), HIDDEN_SIZE ** -0.5, 0.375),
    }


def extend(masked):
    top_rows = masked[GRID_LAT - REACH:][::-1, ::-1]
    lower = jnp.zeros((REACH, GRID_LON, masked.shape[2]), masked.dtype)
    tall = jnp.concatenate([lower, masked, top_rows], 0)
    return jnp.concatenate([tall[:, GRID_LON - REACH:], tall, tall[:, :REACH]], 1)

def depthwise(widened, kernel_taps):
    rows = widened.shape[0] - 2 * REACH
    cols = widened.shape[1] - 2 * REACH
    total = jnp.zeros((rows, cols, widened.shape[2]), jnp.float32)
    for row_tap in range(KERNEL):
        for col_tap in range(KERNEL):
            window = widened[DILATION * row_tap:DILATION * row_tap + rows, DILATION * col_tap:DILATION * col_tap + cols]
            total = total + kernel_taps[row_tap * KERNEL + col_tap] * window
    return total

def member_pass(state, upstream_in, land_mask, kernel_taps, norm_gain, norm_shift, up_weight, down_weight):
    sea = land_mask.astype(jnp.float32)[:, :, None]
    masked = (state.astype(jnp.float32) * sea).astype(jnp.bfloat16)
    masked_wide = masked.astype(jnp.float32)
    widened, extend_back = jax.vjp(extend, masked_wide)
    mixed, conv_back = jax.vjp(depthwise, widened, kernel_taps)
    centered = mixed - lax.optimization_barrier(jnp.mean(mixed, -1, keepdims=True))
    rstd = lax.rsqrt(lax.optimization_barrier(jnp.mean(centered * centered, -1, keepdims=True)) + 1e-06)
    unit = centered * rstd
    normed = (unit * norm_gain + norm_shift).astype(jnp.bfloat16)
    cells = GRID_LAT * GRID_LON
    flat_norm = normed.reshape(cells, CHANNELS)
    pre = jnp.dot(flat_norm, up_weight, preferred_element_type=jnp.float32)
    slope = math.sqrt(2.0 / math.pi)
    tanh_val = jnp.tanh(slope * (pre + 0.044715 * pre * pre * pre))
    activated = (0.5 * pre * (1.0 + tanh_val)).astype(jnp.bfloat16)
    product = jnp.dot(activated, down_weight, preferred_element_type=jnp.float32).reshape(GRID_LAT, GRID_LON, CHANNELS)
    output = ((state.astype(jnp.float32) + product) * sea).astype(jnp.bfloat16)
    upstream = (upstream_in.astype(jnp.float32) * sea).astype(jnp.bfloat16)
    flat_up = upstream.reshape(cells, CHANNELS)
    down_part = jnp.dot(activated.T, flat_up, preferred_element_type=jnp.float32)
    act_grad = jnp.dot(flat_up, down_weight.T, preferred_element_type=jnp.float32)
    deriv = 0.5 * (1.0 + tanh_val) + 0.5 * pre * (1.0 - tanh_val * tanh_val) * slope * (1.0 + 3.0 * 0.044715 * pre * pre)
    pre_grad = (act_grad * deriv).astype(jnp.bfloat16)
    up_part = jnp.dot(flat_norm.T, pre_grad, preferred_element_type=jnp.float32)
    norm_in_grad = jnp.dot(pre_grad, up_weight.T, preferred_element_type=jnp.float32).reshape(GRID_LAT, GRID_LON, CHANNELS)
    norm_part = jnp.stack([lax.optimization_barrier(jnp.sum(norm_in_grad * unit, (0, 1))), lax.optimization_barrier(jnp.sum(norm_in_grad, (0, 1)))])
    scaled = norm_in_grad * norm_gain
    mixed_grad = rstd * (scaled - lax.optimization_barrier(jnp.mean(scaled, -1, keepdims=True)) - unit * lax.optimization_barrier(jnp.mean(scaled * unit, -1, keepdims=True)))
    extended_grad, kernel_part = conv_back(mixed_grad)
    masked_grad = extend_back(extended_grad)[0]
    field_grad = ((upstream_in.astype(jnp.float32) + masked_grad) * sea).astype(jnp.bfloat16)
    return (output, field_grad, kernel_part, norm_part, up_part, down_part)

def reference(field, cotangent, land_mask, kernel_taps, norm_gain, norm_shift, up_weight, down_weight):

    def one_member(pair):
        return member_pass(pair[0], pair[1], land_mask, kernel_taps, norm_gain, norm_shift, up_weight, down_weight)
    output, field_grad, kernel_part, norm_part, up_part, down_part = lax.map(one_member, (field, cotangent))
    factor = 1.0 / math.sqrt(MEMBERS * GRID_LAT * GRID_LON)
    return (output, field_grad, lax.optimization_barrier(jnp.sum(kernel_part, 0)) * factor, lax.optimization_barrier(jnp.sum(norm_part, 0)) * factor, lax.optimization_barrier(jnp.sum(up_part, 0)) * factor, lax.optimization_barrier(jnp.sum(down_part, 0)) * factor)
```

```python
import functools
import math

import jax
import jax.numpy as jnp
from jax import lax
from jax.experimental import pallas as pl
from jax.experimental.pallas import tpu as pltpu
from jax.sharding import PartitionSpec as P

KERNEL = 7
REACH = 6
TAPS = KERNEL * KERNEL
MESH = pl.DeviceIdType.MESH
F32 = jnp.float32
BF16 = jnp.bfloat16
SLOPE = math.sqrt(2.0 / math.pi)
CUBIC = 0.044715

SOUTH, CENTER, NORTH = 0, 1, 2
WEST, MIDDLE, EAST = 0, 1, 2


def rdot(a, b):
    return lax.dot_general(a, b, (((1,), (1,)), ((), ())), preferred_element_type=F32)


def tdot(a, b):
    return lax.dot_general(a, b, (((0,), (0,)), ((), ())), preferred_element_type=F32)


def phases_of(blocks):
    count = blocks.shape[0]
    sub = lax.broadcasted_iota(jnp.int32, (count - 1, 8, 128), 1)
    out = []
    for shift in (2, 4, 6):
        rolled = pltpu.roll(blocks, 8 - shift, 1)
        out.append(jnp.where(sub < 8 - shift, rolled[: count - 1], rolled[1:]))
    return out


def region(ref, rows, cols):
    return ref.at[pl.ds(*rows), pl.ds(*cols)]


DST_ROWS = {SOUTH: (0, 6), CENTER: (6, 16), NORTH: (22, 6)}
DST_COLS = {WEST: (0, 1), MIDDLE: (1, 8), EAST: (9, 1)}
REGIONS = [(r, c) for r in range(3) for c in range(3) if (r, c) != (CENTER, MIDDLE)]


class Grid:
    def __init__(self, nlon, nlat, nens):
        self.nlon, self.nlat, self.nens = nlon, nlat, nens
        self.lon = lax.axis_index("lon")
        self.lat = lax.axis_index("lat")
        self.ens = lax.axis_index("ens")
        self.north = self.lat == nlat - 1
        self.plane = self.lat * nens + self.ens
        self.planes = nlat * nens


def halo_start(g, src, dst, src_rows, src_cols, ssem, rsem, only_rows):
    for rr, cc in REGIONS:
        if rr not in only_rows:
            continue
        here = region(src, src_rows[rr], src_cols[cc])
        land_c = 2 - cc
        step = cc - 1
        east = lax.rem(g.lon + step + g.nlon, g.nlon)

        def send(lat, lon, land_r, here=here, rr=rr, cc=cc, land_c=land_c):
            pltpu.make_async_remote_copy(
                src_ref=here,
                dst_ref=region(dst, DST_ROWS[land_r], DST_COLS[land_c]),
                send_sem=ssem.at[rr * 3 + cc],
                recv_sem=rsem.at[land_r * 3 + land_c],
                device_id={"lon": lon, "lat": lat},
                device_id_type=MESH,
            ).start()

        if rr == CENTER:
            send(g.lat, east, CENTER)
        elif rr == SOUTH:

            @pl.when(g.lat > 0)
            def _(send=send, east=east):
                send(g.lat - 1, east, NORTH)

        else:
            across = lax.rem(2 * g.nlon - 1 - g.lon - step, g.nlon)

            @pl.when(jnp.logical_not(g.north))
            def _(send=send, east=east):
                send(g.lat + 1, east, SOUTH)

            @pl.when(jnp.logical_and(g.north, across != g.lon))
            def _(send=send, across=across):
                send(g.lat, across, NORTH)

            if cc != MIDDLE:

                @pl.when(jnp.logical_and(g.north, across == g.lon))
                def _(here=here, land_c=land_c):
                    pltpu.make_async_copy(
                        here,
                        region(dst, DST_ROWS[NORTH], DST_COLS[land_c]),
                        rsem.at[NORTH * 3 + land_c],
                    ).start()


def halo_wait_recv(g, dst, rsem, row):
    for cc in range(3):
        if (row, cc) == (CENTER, MIDDLE):
            continue
        part = region(dst, DST_ROWS[row], DST_COLS[cc])
        wait = pltpu.make_async_copy(part, part, rsem.at[row * 3 + cc]).wait
        if row == SOUTH:
            pl.when(g.lat > 0)(wait)
        else:
            wait()


def halo_wait_send(g, src, src_rows, src_cols, ssem):
    for rr, cc in REGIONS:
        here = region(src, src_rows[rr], src_cols[cc])
        wait = pltpu.make_async_copy(here, here, ssem.at[rr * 3 + cc]).wait
        if rr == CENTER:
            wait()
        elif rr == SOUTH:
            pl.when(g.lat > 0)(wait)
        elif cc == MIDDLE:
            wait()
        else:
            across = lax.rem(2 * g.nlon - 1 - g.lon - (cc - 1), g.nlon)
            pl.when(jnp.logical_or(jnp.logical_not(g.north), across != g.lon))(wait)


def plane_send(g, src_of, dst, ssem, rsem):
    def one(k, carry):
        peer = lax.rem(g.plane + k, g.planes)
        pltpu.make_async_remote_copy(
            src_ref=src_of(peer),
            dst_ref=dst.at[g.plane],
            send_sem=ssem,
            recv_sem=rsem,
            device_id={"lat": peer // g.nens, "ens": lax.rem(peer, g.nens)},
            device_id_type=MESH,
        ).start()
        return carry

    lax.fori_loop(1, g.planes, one, 0)


def lon_send(g, buf, ssem, rsem):
    def one(k, carry):
        pltpu.make_async_remote_copy(
            src_ref=buf.at[g.lon],
            dst_ref=buf.at[g.lon],
            send_sem=ssem,
            recv_sem=rsem,
            device_id={"lon": lax.rem(g.lon + k, g.nlon)},
            device_id_type=MESH,
        ).start()
        return carry

    lax.fori_loop(1, g.nlon, one, 0)


def bulk_wait(buf, count, sem):
    part = buf.at[pl.ds(0, count)]
    pltpu.make_async_copy(part, part, sem).wait()


FWD_ROWS = {SOUTH: (6, 6), CENTER: (6, 16), NORTH: (16, 6)}
FWD_COLS = {WEST: (1, 1), MIDDLE: (1, 8), EAST: (8, 1)}
BWD_ROWS = {SOUTH: (0, 6), CENTER: (6, 16), NORTH: (22, 6)}
BWD_COLS = {WEST: (0, 1), MIDDLE: (1, 8), EAST: (9, 1)}


def kernel(
    sizes,
    field, cotangent, mask, taps, gain, shift, up, down,
    output, field_grad, kernel_grad, norm_grad, up_grad, down_grad,
    ext, sea, ep, kt, ups, mixed, normed, active, pregrad, nacc, mp, kacc, eg, egs, rb,
    pay1, ra1, zb1, gb1, pay2, ra2, zb2, gb2,
    fs, fr, bs, br, ar_s, ar_r,
):
    g = Grid(*sizes)
    factor = 1.0 / math.sqrt(1024 * g.nlon * g.nlat * g.nens)

    barrier = pltpu.get_barrier_semaphore()

    def greet(**where):
        pl.semaphore_signal(barrier, inc=1, device_id=where, device_id_type=MESH)

    def greet_plane(k, carry):
        peer = lax.rem(g.plane + k, g.planes)
        greet(lat=peer // g.nens, ens=lax.rem(peer, g.nens))
        return carry

    def greet_lon(k, carry):
        greet(lon=lax.rem(g.lon + k, g.nlon))
        return carry

    east = lax.rem(g.lon + 1, g.nlon)
    west = lax.rem(g.lon + g.nlon - 1, g.nlon)

    @pl.when(g.lat > 0)
    def _():
        greet(lat=g.lat - 1, lon=east)
        greet(lat=g.lat - 1, lon=west)

    @pl.when(g.lat < g.nlat - 1)
    def _():
        greet(lat=g.lat + 1, lon=east)
        greet(lat=g.lat + 1, lon=west)

    lax.fori_loop(1, g.planes, greet_plane, 0)
    lax.fori_loop(1, g.nlon, greet_lon, 0)

    eye = (
        lax.broadcasted_iota(jnp.int32, (64, 64), 0) == lax.broadcasted_iota(jnp.int32, (64, 64), 1)
    )
    ones = jnp.ones((64, 128), BF16)

    def mask_row(r, carry):
        marks = jnp.broadcast_to(mask[pl.ds(r, 1), :].astype(F32), (64, 64))
        spread = jnp.where(eye, marks, 0.0).astype(BF16)
        wide = jnp.dot(spread, ones, preferred_element_type=F32).reshape(8, 8, 128)
        sea[r] = wide
        ext[r + REACH, 1:9] = (field[r].astype(F32) * wide).astype(BF16)
        return carry

    lax.fori_loop(0, 16, mask_row, 0)

    count = g.planes + g.nlon - 2
    count = count + 2 * (g.lat > 0).astype(jnp.int32) + 2 * (g.lat < g.nlat - 1).astype(jnp.int32)
    pl.semaphore_wait(barrier, count)
    halo_start(g, ext, ext, FWD_ROWS, FWD_COLS, fs, fr, (NORTH, SOUTH, CENTER))

    def upstream_row(r, carry):
        wide = cotangent[r].astype(F32) * sea[r]
        ups[pl.ds(pl.multiple_of(r * 64, 64), 64), :] = wide.reshape(64, 128).astype(BF16)
        return carry

    lax.fori_loop(0, 16, upstream_row, 0)
    for t in range(TAPS):
        kt[t] = jnp.broadcast_to(taps[t : t + 1, :], (8, 128))
    nacc[...] = jnp.zeros_like(nacc)
    kacc[...] = jnp.zeros_like(kacc)

    def widen_row(r, carry):
        blocks = ext[r].astype(F32)
        ep[0, r] = blocks
        for k, moved in enumerate(phases_of(blocks)):
            ep[k + 1, r, 0:9] = moved
        return carry

    halo_wait_recv(g, ext, fr, CENTER)
    lax.fori_loop(REACH, 16 + REACH, widen_row, 0)

    halo_wait_recv(g, ext, fr, SOUTH)

    @pl.when(g.lat == 0)
    def _():
        ext[0:REACH] = jnp.zeros((REACH, 10, 8, 128), BF16)

    lax.fori_loop(0, REACH, widen_row, 0)

    def conv_row(r, carry):
        total = jnp.zeros((8, 8, 128), F32)
        for i in range(KERNEL):
            for j in range(KERNEL):
                off = 2 + 2 * j
                ph, skip = (off % 8) // 2, off // 8
                total = total + kt[i * KERNEL + j][None] * ep[ph, r + 2 * i, skip : skip + 8]
        mixed[pl.ds(pl.multiple_of(r * 64, 64), 64), :] = total.reshape(64, 128)
        return carry

    gain_row = gain[...]
    shift_row = shift[...]

    def group(q, carry):
        lax.fori_loop(4 * q, 4 * q + 4, conv_row, 0)
        cells = pl.ds(pl.multiple_of(q * 256, 256), 256)
        x = mixed[cells, :]
        centered = x - jnp.mean(x, -1, keepdims=True)
        rstd = lax.rsqrt(jnp.mean(centered * centered, -1, keepdims=True) + 1e-06)
        unit = centered * rstd
        norm = (unit * gain_row + shift_row).astype(BF16)
        normed[cells, :] = norm
        pre = jnp.dot(norm, up[...], preferred_element_type=F32)
        square = pre * pre
        tanh_val = jnp.tanh(SLOPE * (pre + CUBIC * pre * square))
        half = 0.5 * (1.0 + tanh_val)
        act = (pre * half).astype(BF16)
        active[cells, :] = act
        product = jnp.dot(act, down[...], preferred_element_type=F32).reshape(4, 8, 8, 128)
        rows = pl.ds(4 * q, 4)
        output[rows] = ((field[rows].astype(F32) + product) * sea[rows]).astype(BF16)
        act_grad = rdot(ups[cells, :], down[...])
        deriv = half + 0.5 * pre * (1.0 - tanh_val * tanh_val) * SLOPE * (1.0 + 3.0 * CUBIC * square)
        pre_grad = (act_grad * deriv).astype(BF16)
        pregrad[cells, :] = pre_grad
        nig = rdot(pre_grad, up[...])
        scaled = nig * gain_row
        nacc[0] += jnp.sum((nig * unit).reshape(32, 8, 128), 0)
        nacc[1] += jnp.sum(nig.reshape(32, 8, 128), 0)
        mg = rstd * (
            scaled
            - jnp.mean(scaled, -1, keepdims=True)
            - unit * jnp.mean(scaled * unit, -1, keepdims=True)
        )
        mp[0, rows, 1:9] = mg.reshape(4, 8, 8, 128)
        return carry

    zero_block = jnp.zeros((1, 8, 128), F32)

    def spread_row(r, carry):
        mp[0, r, 0:1] = zero_block
        blocks = jnp.concatenate([zero_block, mp[0, r, 1:9], zero_block], 0)
        for k, moved in enumerate(phases_of(blocks)):
            mp[k + 1, r] = moved
        return carry

    lax.fori_loop(0, 2, group, 0)
    halo_wait_recv(g, ext, fr, NORTH)

    flip = (
        lax.broadcasted_iota(jnp.int32, (80, 80), 0)
        + lax.broadcasted_iota(jnp.int32, (80, 80), 1)
        == 79
    ).astype(F32).astype(BF16)

    @pl.when(jnp.logical_not(g.north))
    def _():
        lax.fori_loop(16 + REACH, 16 + 2 * REACH, widen_row, 0)

    @pl.when(g.north)
    def _():
        def turn_row(k, carry):
            row = ext[16 + REACH + k].astype(F32).reshape(80, 128).astype(BF16)
            turned = jnp.dot(flip, row, preferred_element_type=F32).reshape(10, 8, 128)
            r = 16 + 2 * REACH - 1 - k
            ep[0, r] = turned
            for s, moved in enumerate(phases_of(turned)):
                ep[s + 1, r, 0:9] = moved
            return carry

        lax.fori_loop(0, REACH, turn_row, 0)

    lax.fori_loop(2, 4, group, 0)
    lax.fori_loop(0, 16, spread_row, 0)

    def eg_row(p, first, last):
        lo = jnp.zeros((9, 8, 128), F32)
        hi = jnp.zeros((9, 8, 128), F32)
        for i in range(first, last + 1):
            for j in range(KERNEL):
                off = 14 - 2 * j
                ph, skip = (off % 8) // 2, off // 8
                term = kt[i * KERNEL + j][None] * mp[ph, p - 2 * i]
                if skip:
                    lo = lo + term
                else:
                    hi = hi + term
        return jnp.concatenate([lo, zero_block], 0) + jnp.concatenate([zero_block, hi], 0)

    def eg_halo(start, first, last):
        def one(p, carry):
            egs[p] = eg_row(p, first, last).astype(BF16)
            return carry

        lax.fori_loop(start, start + 2, one, 0)

    def eg_center(start, stop, first, last):
        def one(p, carry):
            value = eg_row(p, first, last)
            eg[p - REACH] = value[1:9]
            egs[p, 0:1] = value[0:1].astype(BF16)
            egs[p, 9:10] = value[9:10].astype(BF16)
            return carry

        lax.fori_loop(start, stop, one, 0)

    for m in range(3):
        eg_halo(22 + 2 * m, 4 + m, 6)
    halo_start(g, egs, rb, BWD_ROWS, BWD_COLS, bs, br, (NORTH,))
    for m in range(3):
        eg_halo(2 * m, 0, m)
    halo_start(g, egs, rb, BWD_ROWS, BWD_COLS, bs, br, (SOUTH,))

    chunk = 512 // g.planes
    per = 128 // chunk
    up_part = tdot(normed[...], pregrad[...]).astype(BF16)
    pay1[0:per] = up_part[:, 0:128].reshape(per, chunk, 128)
    pay1[per : 2 * per] = up_part[:, 128:256].reshape(per, chunk, 128)
    down_part = tdot(active[...], ups[...]).astype(BF16)
    pay1[2 * per : 4 * per] = down_part.reshape(2 * per, chunk, 128)
    ra1[g.plane] = pay1[g.plane]
    plane_send(g, lambda peer: pay1.at[peer], ra1, ar_s.at[0], ar_r.at[0])

    for m in range(3, 6):
        eg_center(2 * m, 2 * m + 2, 0, m)
    eg_center(12, 16, 0, 6)
    for m in range(3):
        eg_center(16 + 2 * m, 18 + 2 * m, 1 + m, 6)
    halo_start(g, egs, rb, BWD_ROWS, BWD_COLS, bs, br, (CENTER,))

    def tap_row(r, carry):
        grad = mp[0, r, 1:9]
        for i in range(KERNEL):
            for j in range(KERNEL):
                off = 2 + 2 * j
                ph, skip = (off % 8) // 2, off // 8
                kacc[i * KERNEL + j] += jnp.sum(grad * ep[ph, r + 2 * i, skip : skip + 8], 0)
        return carry

    lax.fori_loop(0, 16, tap_row, 0)

    small = 64 // g.planes
    pay2[...] = jnp.zeros_like(pay2)
    for t in range(TAPS + 2):
        value = kacc[t] if t < TAPS else nacc[t - TAPS]
        pay2[t // small, t % small : t % small + 1] = jnp.sum(value, 0, keepdims=True)
    ra2[g.plane] = pay2[g.plane]
    plane_send(g, lambda peer: pay2.at[peer], ra2, ar_s.at[1], ar_r.at[1])

    bulk_wait(ra1, g.planes - 1, ar_r.at[0])
    zb1[g.lon] = jnp.sum(ra1[...].astype(F32), 0).astype(BF16)
    lon_send(g, zb1, ar_s.at[2], ar_r.at[2])
    bulk_wait(ra2, g.planes - 1, ar_r.at[1])
    zb2[g.lon] = jnp.sum(ra2[...], 0)
    lon_send(g, zb2, ar_s.at[3], ar_r.at[3])

    halo_wait_recv(g, rb, br, CENTER)

    def edge_row(r, carry):
        eg[r, 0:1] += rb[r + REACH, 0:1].astype(F32)
        eg[r, 7:8] += rb[r + REACH, 9:10].astype(F32)
        return carry

    lax.fori_loop(0, 16, edge_row, 0)
    halo_wait_recv(g, rb, br, SOUTH)

    def fold_in(r, row):
        eg[r] += row[1:9]
        eg[r, 0:1] += row[0:1]
        eg[r, 7:8] += row[9:10]

    @pl.when(g.lat > 0)
    def _():
        def one(k, carry):
            fold_in(k, rb[k].astype(F32))
            return carry

        lax.fori_loop(0, REACH, one, 0)

    halo_wait_recv(g, rb, br, NORTH)

    @pl.when(jnp.logical_not(g.north))
    def _():
        def one(k, carry):
            fold_in(10 + k, rb[22 + k].astype(F32))
            return carry

        lax.fori_loop(0, REACH, one, 0)

    @pl.when(g.north)
    def _():
        def one(k, carry):
            row = rb[22 + k].astype(F32).reshape(80, 128).astype(BF16)
            fold_in(15 - k, jnp.dot(flip, row, preferred_element_type=F32).reshape(10, 8, 128))
            return carry

        lax.fori_loop(0, REACH, one, 0)

    def last_row(r, carry):
        field_grad[r] = ((cotangent[r].astype(F32) + eg[r]) * sea[r]).astype(BF16)
        return carry

    lax.fori_loop(0, 16, last_row, 0)

    bulk_wait(zb1, g.nlon - 1, ar_r.at[2])
    gb1[g.plane] = jnp.sum(zb1[...].astype(F32), 0).astype(BF16)
    plane_send(g, lambda peer: gb1.at[g.plane], gb1, ar_s.at[4], ar_r.at[4])
    bulk_wait(zb2, g.nlon - 1, ar_r.at[3])
    gb2[g.plane] = jnp.sum(zb2[...], 0)
    plane_send(g, lambda peer: gb2.at[g.plane], gb2, ar_s.at[5], ar_r.at[5])

    bulk_wait(gb1, g.planes - 1, ar_r.at[4])
    up_grad[:, 0:128] = gb1[0:per].astype(F32).reshape(128, 128) * factor
    up_grad[:, 128:256] = gb1[per : 2 * per].astype(F32).reshape(128, 128) * factor
    down_grad[...] = gb1[2 * per : 4 * per].astype(F32).reshape(256, 128) * factor
    bulk_wait(gb2, g.planes - 1, ar_r.at[5])
    for t in range(TAPS + 2):
        value = gb2[t // small, t % small : t % small + 1] * factor
        if t < TAPS:
            kernel_grad[t : t + 1, :] = value
        else:
            norm_grad[t - TAPS : t - TAPS + 1, :] = value

    halo_wait_send(g, ext, FWD_ROWS, FWD_COLS, fs)
    halo_wait_send(g, egs, BWD_ROWS, BWD_COLS, bs)
    bulk_wait(pay1, g.planes - 1, ar_s.at[0])
    bulk_wait(pay2, g.planes - 1, ar_s.at[1])
    bulk_wait(zb1, g.nlon - 1, ar_s.at[2])
    bulk_wait(zb2, g.nlon - 1, ar_s.at[3])
    bulk_wait(gb1, g.planes - 1, ar_s.at[4])
    bulk_wait(gb2, g.planes - 1, ar_s.at[5])


def shards(sizes, field, cotangent, land_mask, kernel_taps, norm_gain, norm_shift, up_weight, down_weight):
    planes = sizes[1] * sizes[2]
    chunk, small = 512 // planes, 64 // planes
    tile = (16, 8, 8, 128)
    vmem = pl.BlockSpec(memory_space=pltpu.VMEM)
    dma = pltpu.SemaphoreType.DMA
    out = pl.pallas_call(
        functools.partial(kernel, sizes),
        out_shape=(
            jax.ShapeDtypeStruct(tile, BF16),
            jax.ShapeDtypeStruct(tile, BF16),
            jax.ShapeDtypeStruct((TAPS, 128), F32),
            jax.ShapeDtypeStruct((2, 128), F32),
            jax.ShapeDtypeStruct((128, 256), F32),
            jax.ShapeDtypeStruct((256, 128), F32),
        ),
        in_specs=[vmem] * 8,
        out_specs=(vmem,) * 6,
        scratch_shapes=[
            pltpu.VMEM((28, 10, 8, 128), BF16),
            pltpu.VMEM(tile, F32),
            pltpu.VMEM((4, 28, 10, 8, 128), F32),
            pltpu.VMEM((TAPS, 8, 128), F32),
            pltpu.VMEM((1024, 128), BF16),
            pltpu.VMEM((1024, 128), F32),
            pltpu.VMEM((1024, 128), BF16),
            pltpu.VMEM((1024, 256), BF16),
            pltpu.VMEM((1024, 256), BF16),
            pltpu.VMEM((2, 8, 128), F32),
            pltpu.VMEM((4, 16, 9, 8, 128), F32),
            pltpu.VMEM((TAPS, 8, 128), F32),
            pltpu.VMEM(tile, F32),
            pltpu.VMEM((28, 10, 8, 128), BF16),
            pltpu.VMEM((28, 10, 8, 128), BF16),
            pltpu.VMEM((planes, chunk, 128), BF16),
            pltpu.VMEM((planes, chunk, 128), BF16),
            pltpu.VMEM((sizes[0], chunk, 128), BF16),
            pltpu.VMEM((planes, chunk, 128), BF16),
            pltpu.VMEM((planes, small, 128), F32),
            pltpu.VMEM((planes, small, 128), F32),
            pltpu.VMEM((sizes[0], small, 128), F32),
            pltpu.VMEM((planes, small, 128), F32),
            dma((9,)),
            dma((9,)),
            dma((9,)),
            dma((9,)),
            dma((6,)),
            dma((6,)),
        ],
        compiler_params=pltpu.CompilerParams(
            collective_id=0, has_side_effects=True, vmem_limit_bytes=48 * 1024 * 1024
        ),
        name="ocean_block",
    )(
        field.reshape(tile),
        cotangent.reshape(tile),
        land_mask,
        kernel_taps,
        norm_gain.reshape(1, 128),
        norm_shift.reshape(1, 128),
        up_weight,
        down_weight,
    )
    return (out[0].reshape(field.shape), out[1].reshape(field.shape)) + tuple(out[2:])


def solution(mesh):
    sizes = (mesh.shape["lon"], mesh.shape["lat"], mesh.shape["ens"])
    tiles = P("ens", "lat", "lon", None)
    in_specs = (tiles, tiles, P("lat", "lon"), P(), P(), P(), P(), P())
    out_specs = (tiles, tiles, P(), P(), P(), P())
    return jax.shard_map(
        functools.partial(shards, sizes),
        mesh=mesh,
        in_specs=in_specs,
        out_specs=out_specs,
        check_vma=False,
    )
```

```python
import functools
import math

import jax
import jax.numpy as jnp
from jax import lax
from jax.experimental import pallas as pl
from jax.experimental.pallas import tpu as pltpu
from jax.sharding import PartitionSpec as P

KERNEL = 7
REACH = 6
TAPS = KERNEL * KERNEL
MESH = pl.DeviceIdType.MESH
F32 = jnp.float32
BF16 = jnp.bfloat16
SLOPE = math.sqrt(2.0 / math.pi)
CUBIC = 0.044715

SOUTH, CENTER, NORTH = 0, 1, 2
WEST, MIDDLE, EAST = 0, 1, 2


def rdot(a, b):
    return lax.dot_general(a, b, (((1,), (1,)), ((), ())), preferred_element_type=F32)


def tdot(a, b):
    return lax.dot_general(a, b, (((0,), (0,)), ((), ())), preferred_element_type=F32)


def phases_of(blocks):
    count = blocks.shape[0]
    sub = lax.broadcasted_iota(jnp.int32, (count - 1, 8, 128), 1)
    out = []
    for shift in (2, 4, 6):
        rolled = pltpu.roll(blocks, 8 - shift, 1)
        out.append(jnp.where(sub < 8 - shift, rolled[: count - 1], rolled[1:]))
    return out


def region(ref, rows, cols):
    return ref.at[pl.ds(*rows), pl.ds(*cols)]


DST_ROWS = {SOUTH: (0, 6), CENTER: (6, 16), NORTH: (22, 6)}
DST_COLS = {WEST: (0, 1), MIDDLE: (1, 8), EAST: (9, 1)}
REGIONS = [(r, c) for r in range(3) for c in range(3) if (r, c) != (CENTER, MIDDLE)]


class Grid:
    def __init__(self, nlon, nlat, nens):
        self.nlon, self.nlat, self.nens = nlon, nlat, nens
        self.lon = lax.axis_index("lon")
        self.lat = lax.axis_index("lat")
        self.ens = lax.axis_index("ens")
        self.north = self.lat == nlat - 1
        self.plane = self.lat * nens + self.ens
        self.planes = nlat * nens
        self.owners = min(8, self.planes)
        across, along = nlat // 2, nens // 2 * 2
        y = self.ens // 2 * 2 + lax.rem(self.lat, 2)
        core = lax.rem(self.ens, 2)
        xs = [lax.rem(self.lat // 2 + d, across) for d in range(across)]
        ys = [lax.rem(y + d, along) for d in range(along)]
        steps = [(dx, dy, dc) for dx in range(across) for dy in range(along) for dc in range(2)][1:]
        steps.sort(key=lambda s: -min(s[0], across - s[0]) - min(s[1], along - s[1]))
        self.peers = []
        for dx, dy, dc in steps:
            lat = xs[dx] * 2 + lax.rem(ys[dy], 2)
            ens = ys[dy] // 2 * 2 + (1 - core if dc else core)
            self.peers.append((lat, ens))
        far = sorted(range(1, nlon), key=lambda k: -min(k, nlon - k))
        self.lons = [lax.rem(self.lon + k, nlon) for k in far]


def halo_start(g, src, dst, src_rows, src_cols, ssem, rsem, only_rows):
    for rr, cc in sorted(REGIONS, key=lambda rc: only_rows.index(rc[0]) if rc[0] in only_rows else 9):
        if rr not in only_rows:
            continue
        here = region(src, src_rows[rr], src_cols[cc])
        land_c = 2 - cc
        step = cc - 1
        east = lax.rem(g.lon + step + g.nlon, g.nlon)

        def send(lat, lon, land_r, here=here, rr=rr, cc=cc, land_c=land_c):
            pltpu.make_async_remote_copy(
                src_ref=here,
                dst_ref=region(dst, DST_ROWS[land_r], DST_COLS[land_c]),
                send_sem=ssem.at[rr * 3 + cc],
                recv_sem=rsem.at[land_r * 3 + land_c],
                device_id={"lon": lon, "lat": lat},
                device_id_type=MESH,
            ).start()

        if rr == CENTER:
            send(g.lat, east, CENTER)
        elif rr == SOUTH:

            @pl.when(g.lat > 0)
            def _(send=send, east=east):
                send(g.lat - 1, east, NORTH)

        else:
            across = lax.rem(2 * g.nlon - 1 - g.lon - step, g.nlon)

            @pl.when(jnp.logical_not(g.north))
            def _(send=send, east=east):
                send(g.lat + 1, east, SOUTH)

            @pl.when(jnp.logical_and(g.north, across != g.lon))
            def _(send=send, across=across):
                send(g.lat, across, NORTH)

            if cc != MIDDLE:

                @pl.when(jnp.logical_and(g.north, across == g.lon))
                def _(here=here, land_c=land_c):
                    pltpu.make_async_copy(
                        here,
                        region(dst, DST_ROWS[NORTH], DST_COLS[land_c]),
                        rsem.at[NORTH * 3 + land_c],
                    ).start()


def halo_wait_recv(g, dst, rsem, row):
    for cc in range(3):
        if (row, cc) == (CENTER, MIDDLE):
            continue
        part = region(dst, DST_ROWS[row], DST_COLS[cc])
        wait = pltpu.make_async_copy(part, part, rsem.at[row * 3 + cc]).wait
        if row == SOUTH:
            pl.when(g.lat > 0)(wait)
        else:
            wait()


def halo_wait_send(g, src, src_rows, src_cols, ssem):
    for rr, cc in REGIONS:
        here = region(src, src_rows[rr], src_cols[cc])
        wait = pltpu.make_async_copy(here, here, ssem.at[rr * 3 + cc]).wait
        if rr == CENTER:
            wait()
        elif rr == SOUTH:
            pl.when(g.lat > 0)(wait)
        elif cc == MIDDLE:
            wait()
        else:
            across = lax.rem(2 * g.nlon - 1 - g.lon - (cc - 1), g.nlon)
            pl.when(jnp.logical_or(jnp.logical_not(g.north), across != g.lon))(wait)


def plane_send(g, src_of, dst, ssem, rsem):
    for lat, ens in g.peers:
        pltpu.make_async_remote_copy(
            src_ref=src_of(lat * g.nens + ens),
            dst_ref=dst.at[g.plane],
            send_sem=ssem,
            recv_sem=rsem,
            device_id={"lat": lat, "ens": ens},
            device_id_type=MESH,
        ).start()


def owner_send(g, src, dst, ssem, rsem):
    for o in range(g.owners):

        @pl.when(g.plane != o)
        def _(o=o):
            pltpu.make_async_remote_copy(
                src_ref=src.at[o],
                dst_ref=dst.at[g.plane],
                send_sem=ssem,
                recv_sem=rsem,
                device_id={"lat": o // g.nens, "ens": o % g.nens},
                device_id_type=MESH,
            ).start()


def lon_send(g, buf, ssem, rsem):
    for lon in g.lons:
        pltpu.make_async_remote_copy(
            src_ref=buf.at[g.lon],
            dst_ref=buf.at[g.lon],
            send_sem=ssem,
            recv_sem=rsem,
            device_id={"lon": lon},
            device_id_type=MESH,
        ).start()


def bulk_wait(buf, count, sem):
    part = buf.at[pl.ds(0, count)]
    pltpu.make_async_copy(part, part, sem).wait()


FWD_ROWS = {SOUTH: (6, 6), CENTER: (6, 16), NORTH: (16, 6)}
FWD_COLS = {WEST: (1, 1), MIDDLE: (1, 8), EAST: (8, 1)}
BWD_ROWS = {SOUTH: (0, 6), CENTER: (6, 16), NORTH: (22, 6)}
BWD_COLS = {WEST: (0, 1), MIDDLE: (1, 8), EAST: (9, 1)}


def kernel(
    sizes,
    field_h, cotangent_h, mask_h, taps_h, gain_h, shift_h, up_h, down_h,
    output, field_grad, kernel_grad, norm_grad, up_grad, down_grad,
    field, cotangent, mask, taps, gain, shift, up, down,
    ext, sea, ep, kt, ups, mixed, normed, active, pregrad, mp, kacc, uacc, dacc, eg, egs, rb,
    pay1, ra1, zb1, gb1, pay2, ra2, zb2, gb2,
    ins, fs, fr, bs, br, ar_s, ar_r,
):
    g = Grid(*sizes)
    factor = 1.0 / math.sqrt(1024 * g.nlon * g.nlat * g.nens)
    owner = g.plane < g.owners

    loads = {}
    for k, (name, src, dst) in enumerate(
        (
            ("mask", mask_h, mask),
            ("field", field_h, field),
            ("cotangent", cotangent_h, cotangent),
            ("taps", taps_h, taps),
            ("gain", gain_h, gain),
            ("shift", shift_h, shift),
            ("up", up_h, up),
            ("down", down_h, down),
        )
    ):
        loads[name] = pltpu.make_async_copy(src, dst, ins.at[k])
        loads[name].start()

    barrier = pltpu.get_barrier_semaphore()

    def greet(**where):
        pl.semaphore_signal(barrier, inc=1, device_id=where, device_id_type=MESH)

    for lon in g.lons:
        greet(lon=lon)

    east = lax.rem(g.lon + 1, g.nlon)
    west = lax.rem(g.lon + g.nlon - 1, g.nlon)

    @pl.when(g.lat > 0)
    def _():
        greet(lat=g.lat - 1, lon=east)
        greet(lat=g.lat - 1, lon=west)

    @pl.when(g.lat < g.nlat - 1)
    def _():
        greet(lat=g.lat + 1, lon=east)
        greet(lat=g.lat + 1, lon=west)

    for lat, ens in g.peers:
        greet(lat=lat, ens=ens)

    eye = (
        lax.broadcasted_iota(jnp.int32, (64, 64), 0) == lax.broadcasted_iota(jnp.int32, (64, 64), 1)
    )
    ones = jnp.ones((64, 128), BF16)
    loads["mask"].wait()
    loads["field"].wait()
    for r in range(16):
        marks = jnp.broadcast_to(mask[r : r + 1, :].astype(F32), (64, 64))
        spread = jnp.where(eye, marks, 0.0).astype(BF16)
        wide = jnp.dot(spread, ones, preferred_element_type=F32).reshape(8, 8, 128)
        sea[r] = wide
        ext[r + REACH, 1:9] = (field[r].astype(F32) * wide).astype(BF16)

    count = g.planes + g.nlon - 2
    count = count + 2 * (g.lat > 0).astype(jnp.int32) + 2 * (g.lat < g.nlat - 1).astype(jnp.int32)
    pl.semaphore_wait(barrier, count)
    halo_start(g, ext, ext, FWD_ROWS, FWD_COLS, fs, fr, (CENTER, NORTH, SOUTH))

    loads["cotangent"].wait()
    for name in ("taps", "gain", "shift", "up", "down"):
        loads[name].wait()

    def upstream_row(r, carry):
        wide = cotangent[r].astype(F32) * sea[r]
        ups[pl.ds(pl.multiple_of(r * 64, 64), 64), :] = wide.reshape(64, 128).astype(BF16)
        return carry

    lax.fori_loop(0, 16, upstream_row, 0, unroll=4)
    for t in range(TAPS):
        kt[t] = jnp.broadcast_to(taps[t : t + 1, :], (8, 128))
    kacc[...] = jnp.zeros_like(kacc)

    def widen_row(r, carry):
        blocks = ext[r].astype(F32)
        ep[0, r] = blocks
        for k, moved in enumerate(phases_of(blocks)):
            ep[k + 1, r, 0:9] = moved
        return carry

    halo_wait_recv(g, ext, fr, CENTER)
    lax.fori_loop(REACH, 16 + REACH, widen_row, 0)

    halo_wait_recv(g, ext, fr, SOUTH)

    @pl.when(g.lat == 0)
    def _():
        ext[0:REACH] = jnp.zeros((REACH, 10, 8, 128), BF16)

    lax.fori_loop(0, REACH, widen_row, 0)

    def conv_row(r, carry):
        total = jnp.zeros((8, 8, 128), F32)
        for i in range(KERNEL):
            for j in range(KERNEL):
                off = 2 + 2 * j
                ph, skip = (off % 8) // 2, off // 8
                total = total + kt[i * KERNEL + j][None] * ep[ph, r + 2 * i, skip : skip + 8]
        mixed[pl.ds(pl.multiple_of(r * 64, 64), 64), :] = total.reshape(64, 128)
        return carry

    gain_row = gain[...]
    shift_row = shift[...]

    def group(first, many):
        lax.fori_loop(first, first + many, conv_row, 0)
        cells = slice(64 * first, 64 * (first + many))
        rows = slice(first, first + many)
        x = mixed[cells, :]
        centered = x - jnp.mean(x, -1, keepdims=True)
        rstd = lax.rsqrt(jnp.mean(centered * centered, -1, keepdims=True) + 1e-06)
        unit = centered * rstd
        norm = (unit * gain_row + shift_row).astype(BF16)
        normed[cells, :] = norm
        pre = jnp.dot(norm, up[...], preferred_element_type=F32)
        square = pre * pre
        tanh_val = jnp.tanh(pre * (SLOPE + (SLOPE * CUBIC) * square))
        half = 0.5 + 0.5 * tanh_val
        gated = pre * half
        act = gated.astype(BF16)
        active[cells, :] = act
        product = jnp.dot(act, down[...], preferred_element_type=F32).reshape(many, 8, 8, 128)
        output[rows] = ((field[rows].astype(F32) + product) * sea[rows]).astype(BF16)
        act_grad = rdot(ups[cells, :], down[...])
        deriv = half + gated * (1.0 - tanh_val) * (SLOPE + (3.0 * SLOPE * CUBIC) * square)
        pre_grad = (act_grad * deriv).astype(BF16)
        pregrad[cells, :] = pre_grad
        nig = rdot(pre_grad, up[...])
        scaled = nig * gain_row
        kacc[TAPS] += jnp.sum((nig * unit).reshape(8 * many, 8, 128), 0)
        kacc[TAPS + 1] += jnp.sum(nig.reshape(8 * many, 8, 128), 0)
        mg = rstd * (
            scaled
            - jnp.mean(scaled, -1, keepdims=True)
            - unit * jnp.mean(scaled * unit, -1, keepdims=True)
        )
        mp[0, rows, 1:9] = mg.reshape(many, 8, 8, 128)

    zero_block = jnp.zeros((1, 8, 128), F32)

    def spread_row(r, carry):
        mp[0, r, 0:1] = zero_block
        blocks = jnp.concatenate([zero_block, mp[0, r, 1:9], zero_block], 0)
        for k, moved in enumerate(phases_of(blocks)):
            mp[k + 1, r] = moved
        return carry

    def tap_row(r, carry):
        grad = mp[0, r, 1:9]
        for i in range(KERNEL):
            for j in range(KERNEL):
                off = 2 + 2 * j
                ph, skip = (off % 8) // 2, off // 8
                kacc[i * KERNEL + j] += jnp.sum(grad * ep[ph, r + 2 * i, skip : skip + 8], 0)
        return carry

    group(0, 5)
    group(5, 5)
    lax.fori_loop(0, 10, tap_row, 0)
    lax.fori_loop(0, 10, spread_row, 0)
    uacc[...] = tdot(normed[0:640, :], pregrad[0:640, :])
    dacc[...] = tdot(active[0:640, :], ups[0:640, :])
    halo_wait_recv(g, ext, fr, NORTH)

    flip = (
        lax.broadcasted_iota(jnp.int32, (80, 80), 0)
        + lax.broadcasted_iota(jnp.int32, (80, 80), 1)
        == 79
    ).astype(F32).astype(BF16)

    @pl.when(jnp.logical_not(g.north))
    def _():
        lax.fori_loop(16 + REACH, 16 + 2 * REACH, widen_row, 0)

    @pl.when(g.north)
    def _():
        for k in range(REACH):
            row = ext[16 + REACH + k].astype(F32).reshape(80, 128).astype(BF16)
            turned = jnp.dot(flip, row, preferred_element_type=F32).reshape(10, 8, 128)
            r = 16 + 2 * REACH - 1 - k
            ep[0, r] = turned
            for s, moved in enumerate(phases_of(turned)):
                ep[s + 1, r, 0:9] = moved

    group(10, 6)
    lax.fori_loop(10, 16, spread_row, 0)

    def eg_row(p, first, last):
        lo = jnp.zeros((9, 8, 128), F32)
        hi = jnp.zeros((9, 8, 128), F32)
        for i in range(first, last + 1):
            for j in range(KERNEL):
                off = 14 - 2 * j
                ph, skip = (off % 8) // 2, off // 8
                term = kt[i * KERNEL + j][None] * mp[ph, p - 2 * i]
                if skip:
                    lo = lo + term
                else:
                    hi = hi + term
        return jnp.concatenate([lo, zero_block], 0) + jnp.concatenate([zero_block, hi], 0)

    def eg_halo(start, first, last):
        def one(p, carry):
            egs[p] = eg_row(p, first, last).astype(BF16)
            return carry

        lax.fori_loop(start, start + 2, one, 0)

    def eg_center(start, stop, first, last):
        def one(p, carry):
            value = eg_row(p, first, last)
            eg[p - REACH] = value[1:9]
            egs[p, 0:1] = value[0:1].astype(BF16)
            egs[p, 9:10] = value[9:10].astype(BF16)
            return carry

        lax.fori_loop(start, stop, one, 0)

    for m in range(3):
        eg_halo(22 + 2 * m, 4 + m, 6)
    halo_start(g, egs, rb, BWD_ROWS, BWD_COLS, bs, br, (NORTH,))

    chunk = 512 // g.planes
    per = 128 // chunk
    up_part = (uacc[...] + tdot(normed[640:1024, :], pregrad[640:1024, :])).astype(BF16)
    pay1[0:per] = up_part[:, 0:128].reshape(per, chunk, 128)
    pay1[per : 2 * per] = up_part[:, 128:256].reshape(per, chunk, 128)
    down_part = (dacc[...] + tdot(active[640:1024, :], ups[640:1024, :])).astype(BF16)
    pay1[2 * per : 4 * per] = down_part.reshape(2 * per, chunk, 128)
    ra1[g.plane] = pay1[g.plane]
    plane_send(g, lambda peer: pay1.at[peer], ra1, ar_s.at[0], ar_r.at[0])

    lax.fori_loop(10, 16, tap_row, 0)
    small = 64 // g.owners
    pay2[...] = jnp.sum(kacc[...], 1).reshape(g.owners, small, 128)

    @pl.when(owner)
    def _():
        ra2[g.plane] = pay2[g.plane]

    owner_send(g, pay2, ra2, ar_s.at[1], ar_r.at[1])

    for m in range(3):
        eg_halo(2 * m, 0, m)
    halo_start(g, egs, rb, BWD_ROWS, BWD_COLS, bs, br, (SOUTH,))
    for m in range(3, 6):
        eg_center(2 * m, 2 * m + 2, 0, m)
    eg_center(12, 16, 0, 6)
    for m in range(3):
        eg_center(16 + 2 * m, 18 + 2 * m, 1 + m, 6)
    halo_start(g, egs, rb, BWD_ROWS, BWD_COLS, bs, br, (CENTER,))

    bulk_wait(ra1, g.planes - 1, ar_r.at[0])
    zb1[g.lon] = jnp.sum(ra1[...].astype(F32), 0).astype(BF16)
    lon_send(g, zb1, ar_s.at[2], ar_r.at[2])

    @pl.when(owner)
    def _():
        bulk_wait(ra2, g.planes - 1, ar_r.at[1])
        zb2[g.lon] = jnp.sum(ra2[...], 0)
        lon_send(g, zb2, ar_s.at[3], ar_r.at[3])

    halo_wait_recv(g, rb, br, CENTER)

    def edge_row(r, carry):
        eg[r, 0:1] += rb[r + REACH, 0:1].astype(F32)
        eg[r, 7:8] += rb[r + REACH, 9:10].astype(F32)
        return carry

    lax.fori_loop(0, 16, edge_row, 0)
    halo_wait_recv(g, rb, br, SOUTH)

    def fold_in(r, row):
        eg[r] += row[1:9]
        eg[r, 0:1] += row[0:1]
        eg[r, 7:8] += row[9:10]

    @pl.when(g.lat > 0)
    def _():
        def one(k, carry):
            fold_in(k, rb[k].astype(F32))
            return carry

        lax.fori_loop(0, REACH, one, 0)

    halo_wait_recv(g, rb, br, NORTH)

    @pl.when(jnp.logical_not(g.north))
    def _():
        def one(k, carry):
            fold_in(10 + k, rb[22 + k].astype(F32))
            return carry

        lax.fori_loop(0, REACH, one, 0)

    @pl.when(g.north)
    def _():
        for k in range(REACH):
            row = rb[22 + k].astype(F32).reshape(80, 128).astype(BF16)
            fold_in(15 - k, jnp.dot(flip, row, preferred_element_type=F32).reshape(10, 8, 128))

    def last_row(r, carry):
        field_grad[r] = ((cotangent[r].astype(F32) + eg[r]) * sea[r]).astype(BF16)
        return carry

    lax.fori_loop(0, 16, last_row, 0, unroll=2)

    bulk_wait(zb1, g.nlon - 1, ar_r.at[2])
    gb1[g.plane] = jnp.sum(zb1[...].astype(F32), 0).astype(BF16)
    plane_send(g, lambda peer: gb1.at[g.plane], gb1, ar_s.at[4], ar_r.at[4])

    @pl.when(owner)
    def _():
        bulk_wait(zb2, g.nlon - 1, ar_r.at[3])
        gb2[g.plane] = jnp.sum(zb2[...], 0)
        plane_send(g, lambda peer: gb2.at[g.plane], gb2, ar_s.at[5], ar_r.at[5])

    bulk_wait(gb1, g.planes - 1, ar_r.at[4])
    up_grad[:, 0:128] = gb1[0:per].astype(F32).reshape(128, 128) * factor
    up_grad[:, 128:256] = gb1[per : 2 * per].astype(F32).reshape(128, 128) * factor
    down_grad[...] = gb1[2 * per : 4 * per].astype(F32).reshape(256, 128) * factor

    @pl.when(owner)
    def _():
        bulk_wait(gb2, g.owners - 1, ar_r.at[5])

    @pl.when(jnp.logical_not(owner))
    def _():
        bulk_wait(gb2, g.owners, ar_r.at[5])

    small_sums = gb2[...].reshape(64, 128) * factor
    kernel_grad[...] = small_sums[0:TAPS]
    norm_grad[...] = small_sums[TAPS : TAPS + 2]

    halo_wait_send(g, ext, FWD_ROWS, FWD_COLS, fs)
    halo_wait_send(g, egs, BWD_ROWS, BWD_COLS, bs)
    bulk_wait(pay1, g.planes - 1, ar_s.at[0])
    bulk_wait(zb1, g.nlon - 1, ar_s.at[2])
    bulk_wait(gb1, g.planes - 1, ar_s.at[4])

    @pl.when(owner)
    def _():
        bulk_wait(pay2, g.owners - 1, ar_s.at[1])
        bulk_wait(zb2, g.nlon - 1, ar_s.at[3])
        bulk_wait(ra2, g.planes - 1, ar_s.at[5])

    @pl.when(jnp.logical_not(owner))
    def _():
        bulk_wait(pay2, g.owners, ar_s.at[1])


def write_out(*refs):
    sems = refs[-1]
    half = len(refs) // 2
    copies = [
        pltpu.make_async_copy(src, dst, sems.at[k])
        for k, (src, dst) in enumerate(zip(refs[:half], refs[half:-1]))
    ]
    for copy in copies:
        copy.start()
    for copy in copies:
        copy.wait()


def shards(sizes, field, cotangent, land_mask, kernel_taps, norm_gain, norm_shift, up_weight, down_weight):
    planes = sizes[1] * sizes[2]
    owners = min(8, planes)
    chunk, small = 512 // planes, 64 // owners
    tile = (16, 8, 8, 128)
    vmem = pl.BlockSpec(memory_space=pltpu.VMEM)
    hbm = pl.BlockSpec(memory_space=pltpu.HBM)
    dma = pltpu.SemaphoreType.DMA
    results = (
        jax.ShapeDtypeStruct(tile, BF16),
        jax.ShapeDtypeStruct(tile, BF16),
        jax.ShapeDtypeStruct((TAPS, 128), F32),
        jax.ShapeDtypeStruct((2, 128), F32),
        jax.ShapeDtypeStruct((128, 256), F32),
        jax.ShapeDtypeStruct((256, 128), F32),
    )
    held = pl.pallas_call(
        functools.partial(kernel, sizes),
        out_shape=results,
        in_specs=[hbm] * 8,
        out_specs=(vmem,) * 6,
        scratch_shapes=[
            pltpu.VMEM(tile, BF16),
            pltpu.VMEM(tile, BF16),
            pltpu.VMEM((16, 64), jnp.int32),
            pltpu.VMEM((TAPS, 128), F32),
            pltpu.VMEM((1, 128), F32),
            pltpu.VMEM((1, 128), F32),
            pltpu.VMEM((128, 256), BF16),
            pltpu.VMEM((256, 128), BF16),
            pltpu.VMEM((28, 10, 8, 128), BF16),
            pltpu.VMEM(tile, F32),
            pltpu.VMEM((4, 28, 10, 8, 128), F32),
            pltpu.VMEM((TAPS, 8, 128), F32),
            pltpu.VMEM((1024, 128), BF16),
            pltpu.VMEM((1024, 128), F32),
            pltpu.VMEM((1024, 128), BF16),
            pltpu.VMEM((1024, 256), BF16),
            pltpu.VMEM((1024, 256), BF16),
            pltpu.VMEM((4, 16, 9, 8, 128), F32),
            pltpu.VMEM((64, 8, 128), F32),
            pltpu.VMEM((128, 256), F32),
            pltpu.VMEM((256, 128), F32),
            pltpu.VMEM(tile, F32),
            pltpu.VMEM((28, 10, 8, 128), BF16),
            pltpu.VMEM((28, 10, 8, 128), BF16),
            pltpu.VMEM((planes, chunk, 128), BF16),
            pltpu.VMEM((planes, chunk, 128), BF16),
            pltpu.VMEM((sizes[0], chunk, 128), BF16),
            pltpu.VMEM((planes, chunk, 128), BF16),
            pltpu.VMEM((owners, small, 128), F32),
            pltpu.VMEM((planes, small, 128), F32),
            pltpu.VMEM((sizes[0], small, 128), F32),
            pltpu.VMEM((owners, small, 128), F32),
            dma((8,)),
            dma((9,)),
            dma((9,)),
            dma((9,)),
            dma((9,)),
            dma((6,)),
            dma((6,)),
        ],
        compiler_params=pltpu.CompilerParams(
            collective_id=0, has_side_effects=True, vmem_limit_bytes=48 * 1024 * 1024
        ),
        name="ocean_block",
    )(
        *(
            pltpu.with_memory_space_constraint(x, pltpu.HBM)
            for x in (
                field.reshape(tile),
                cotangent.reshape(tile),
                land_mask,
                kernel_taps,
                norm_gain.reshape(1, 128),
                norm_shift.reshape(1, 128),
                up_weight,
                down_weight,
            )
        )
    )
    out = pl.pallas_call(
        write_out,
        out_shape=results,
        in_specs=[vmem] * 6,
        out_specs=(hbm,) * 6,
        scratch_shapes=[dma((6,))],
        compiler_params=pltpu.CompilerParams(vmem_limit_bytes=8 * 1024 * 1024),
        name="write_out",
    )(*held)
    return (out[0].reshape(field.shape), out[1].reshape(field.shape)) + tuple(out[2:])


def solution(mesh):
    sizes = (mesh.shape["lon"], mesh.shape["lat"], mesh.shape["ens"])
    tiles = P("ens", "lat", "lon", None)
    in_specs = (tiles, tiles, P("lat", "lon"), P(), P(), P(), P(), P())
    out_specs = (tiles, tiles, P(), P(), P(), P())
    return jax.shard_map(
        functools.partial(shards, sizes),
        mesh=mesh,
        in_specs=in_specs,
        out_specs=out_specs,
        check_vma=False,
    )
```

```python
import functools
import math

import jax
import jax.numpy as jnp
from jax import lax
from jax.experimental import pallas as pl
from jax.experimental.pallas import tpu as pltpu
from jax.sharding import PartitionSpec as P

KERNEL = 7
REACH = 6
TAPS = KERNEL * KERNEL
MESH = pl.DeviceIdType.MESH
F32 = jnp.float32
BF16 = jnp.bfloat16
SLOPE = math.sqrt(2.0 / math.pi)
CUBIC = 0.044715

SOUTH, CENTER, NORTH = 0, 1, 2
WEST, MIDDLE, EAST = 0, 1, 2


def rdot(a, b):
    return lax.dot_general(a, b, (((1,), (1,)), ((), ())), preferred_element_type=F32)


def tdot(a, b):
    return lax.dot_general(a, b, (((0,), (0,)), ((), ())), preferred_element_type=F32)


def phases_of(blocks):
    count = blocks.shape[0]
    sub = lax.broadcasted_iota(jnp.int32, (count - 1, 8, 128), 1)
    out = []
    for shift in (2, 4, 6):
        rolled = pltpu.roll(blocks, 8 - shift, 1)
        out.append(jnp.where(sub < 8 - shift, rolled[: count - 1], rolled[1:]))
    return out


def region(ref, rows, cols):
    return ref.at[pl.ds(*rows), pl.ds(*cols)]


DST_ROWS = {SOUTH: (0, 6), CENTER: (6, 16), NORTH: (22, 6)}
DST_COLS = {WEST: (0, 1), MIDDLE: (1, 8), EAST: (9, 1)}
REGIONS = [(r, c) for r in range(3) for c in range(3) if (r, c) != (CENTER, MIDDLE)]


class Grid:
    def __init__(self, nlon, nlat, nens):
        self.nlon, self.nlat, self.nens = nlon, nlat, nens
        self.lon = lax.axis_index("lon")
        self.lat = lax.axis_index("lat")
        self.ens = lax.axis_index("ens")
        self.north = self.lat == nlat - 1
        self.plane = self.lat * nens + self.ens
        self.planes = nlat * nens
        self.owners = min(8, self.planes)
        self.relays = (nlat - 3, 1) if nlat == 8 else ()
        across, along = nlat // 2, nens // 2 * 2
        y = self.ens // 2 * 2 + lax.rem(self.lat, 2)
        core = lax.rem(self.ens, 2)
        xs = [lax.rem(self.lat // 2 + d, across) for d in range(across)]
        ys = [lax.rem(y + d, along) for d in range(along)]
        steps = [(dx, dy, dc) for dx in range(across) for dy in range(along) for dc in range(2)][1:]
        steps.sort(key=lambda s: -min(s[0], across - s[0]) - min(s[1], along - s[1]))
        self.peers = []
        for dx, dy, dc in steps:
            lat = xs[dx] * 2 + lax.rem(ys[dy], 2)
            ens = ys[dy] // 2 * 2 + (1 - core if dc else core)
            self.peers.append((lat, ens))
        far = sorted(range(1, nlon), key=lambda k: -min(k, nlon - k))
        self.lons = [lax.rem(self.lon + k, nlon) for k in far]


def halo_start(g, src, dst, src_rows, src_cols, ssem, rsem, only_rows):
    for rr, cc in sorted(REGIONS, key=lambda rc: only_rows.index(rc[0]) if rc[0] in only_rows else 9):
        if rr not in only_rows:
            continue
        here = region(src, src_rows[rr], src_cols[cc])
        land_c = 2 - cc
        step = cc - 1
        east = lax.rem(g.lon + step + g.nlon, g.nlon)

        def send(lat, lon, land_r, here=here, rr=rr, cc=cc, land_c=land_c):
            pltpu.make_async_remote_copy(
                src_ref=here,
                dst_ref=region(dst, DST_ROWS[land_r], DST_COLS[land_c]),
                send_sem=ssem.at[rr * 3 + cc],
                recv_sem=rsem.at[land_r * 3 + land_c],
                device_id={"lon": lon, "lat": lat},
                device_id_type=MESH,
            ).start()

        if rr == CENTER:
            send(g.lat, east, CENTER)
        elif rr == SOUTH:

            @pl.when(g.lat > 0)
            def _(send=send, east=east):
                send(g.lat - 1, east, NORTH)

        else:

            @pl.when(jnp.logical_not(g.north))
            def _(send=send, east=east):
                send(g.lat + 1, east, SOUTH)


def across(g, step):
    return lax.rem(2 * g.nlon - 1 - g.lon - step, g.nlon)


def fold_sends(g, here, dst, dst_row, count, cols, ssem, rsem, first_row):
    for cc in (MIDDLE, EAST, WEST):
        lon = across(g, cc - 1)
        part = here.at[pl.ds(first_row, count), pl.ds(*cols[cc])]
        land = dst.at[pl.ds(dst_row, count), pl.ds(*DST_COLS[2 - cc])]
        arrived = rsem.at[NORTH * 3 + 2 - cc]

        def go(part=part, land=land, arrived=arrived, lon=lon, cc=cc):
            pltpu.make_async_remote_copy(
                src_ref=part,
                dst_ref=land,
                send_sem=ssem(cc),
                recv_sem=arrived,
                device_id={"lon": lon, "lat": g.nlat - 1},
                device_id_type=MESH,
            ).start()

        yield cc, lon, part, land, arrived, go


def fold_start(g, src, dst, src_rows, src_cols, ssem, rsem, relay, rsems):
    row, total = src_rows[NORTH]
    own = total - 2 * len(g.relays)
    for cc, lon, part, land, arrived, go in fold_sends(
        g, src, dst, DST_ROWS[NORTH][0], own, src_cols, lambda cc: ssem.at[NORTH * 3 + cc], rsem, row
    ):
        if cc == MIDDLE:
            for q, lat in enumerate(g.relays):
                low, high = src_cols[WEST][0], src_cols[EAST][0] + 1
                pltpu.make_async_remote_copy(
                    src_ref=src.at[pl.ds(row + own + 2 * q, 2), pl.ds(low, high - low)],
                    dst_ref=relay.at[pl.ds(0, 2), pl.ds(low, high - low)],
                    send_sem=rsems.at[q],
                    recv_sem=rsems.at[2],
                    device_id={"lat": lat},
                    device_id_type=MESH,
                ).start()
            go()
        else:
            pl.when(lon != g.lon)(go)

            @pl.when(lon == g.lon)
            def _(part=part, land=land, arrived=arrived):
                pltpu.make_async_copy(part, land, arrived).start()


def fold_pass_on(g, dst, src_cols, rsem, relay, rsems):
    low, high = src_cols[WEST][0], src_cols[EAST][0] + 1
    part = relay.at[pl.ds(0, 2), pl.ds(low, high - low)]
    for q, lat in enumerate(g.relays):

        @pl.when(g.lat == lat)
        def _(q=q):
            pltpu.make_async_copy(part, part, rsems.at[2]).wait()
            row = DST_ROWS[NORTH][0] + 6 - 2 * len(g.relays) + 2 * q
            for cc, lon, _, _, _, go in fold_sends(
                g, relay, dst, row, 2, src_cols, lambda cc: rsems.at[3 + cc], rsem, 0
            ):
                go()


def fold_wait_send(g, src, src_rows, src_cols, ssem, relay, rsems):
    row, total = src_rows[NORTH]
    own = total - 2 * len(g.relays)
    low, high = src_cols[WEST][0], src_cols[EAST][0] + 1
    whole = relay.at[pl.ds(0, 2), pl.ds(low, high - low)]

    @pl.when(g.north)
    def _():
        for cc in range(3):
            part = src.at[pl.ds(row, own), pl.ds(*src_cols[cc])]
            wait = pltpu.make_async_copy(part, part, ssem.at[NORTH * 3 + cc]).wait
            if cc == MIDDLE:
                wait()
            else:
                pl.when(across(g, cc - 1) != g.lon)(wait)
        for q in range(len(g.relays)):
            pltpu.make_async_copy(whole, whole, rsems.at[q]).wait()

    for lat in g.relays:

        @pl.when(g.lat == lat)
        def _():
            for cc in range(3):
                part = relay.at[pl.ds(0, 2), pl.ds(*src_cols[cc])]
                pltpu.make_async_copy(part, part, rsems.at[3 + cc]).wait()


def halo_wait_recv(g, dst, rsem, row):
    for cc in range(3):
        if (row, cc) == (CENTER, MIDDLE):
            continue
        part = region(dst, DST_ROWS[row], DST_COLS[cc])
        wait = pltpu.make_async_copy(part, part, rsem.at[row * 3 + cc]).wait
        if row == SOUTH:
            pl.when(g.lat > 0)(wait)
        else:
            wait()


def halo_wait_send(g, src, src_rows, src_cols, ssem):
    for rr, cc in REGIONS:
        here = region(src, src_rows[rr], src_cols[cc])
        wait = pltpu.make_async_copy(here, here, ssem.at[rr * 3 + cc]).wait
        if rr == CENTER:
            wait()
        elif rr == SOUTH:
            pl.when(g.lat > 0)(wait)
        else:
            pl.when(jnp.logical_not(g.north))(wait)


def plane_send(g, src_of, dst, ssem, rsem):
    for lat, ens in g.peers:
        pltpu.make_async_remote_copy(
            src_ref=src_of(lat * g.nens + ens),
            dst_ref=dst.at[g.plane],
            send_sem=ssem,
            recv_sem=rsem,
            device_id={"lat": lat, "ens": ens},
            device_id_type=MESH,
        ).start()


def owner_send(g, src, dst, ssem, rsem):
    for o in range(g.owners):

        @pl.when(g.plane != o)
        def _(o=o):
            pltpu.make_async_remote_copy(
                src_ref=src.at[o],
                dst_ref=dst.at[g.plane],
                send_sem=ssem,
                recv_sem=rsem,
                device_id={"lat": o // g.nens, "ens": o % g.nens},
                device_id_type=MESH,
            ).start()


def lon_send(g, buf, ssem, rsem):
    for lon in g.lons:
        pltpu.make_async_remote_copy(
            src_ref=buf.at[g.lon],
            dst_ref=buf.at[g.lon],
            send_sem=ssem,
            recv_sem=rsem,
            device_id={"lon": lon},
            device_id_type=MESH,
        ).start()


def bulk_wait(buf, count, sem):
    part = buf.at[pl.ds(0, count)]
    pltpu.make_async_copy(part, part, sem).wait()


FWD_ROWS = {SOUTH: (6, 6), CENTER: (6, 16), NORTH: (16, 6)}
FWD_COLS = {WEST: (1, 1), MIDDLE: (1, 8), EAST: (8, 1)}
BWD_ROWS = {SOUTH: (0, 6), CENTER: (6, 16), NORTH: (22, 6)}
BWD_COLS = {WEST: (0, 1), MIDDLE: (1, 8), EAST: (9, 1)}


def kernel(
    sizes,
    field_h, cotangent_h, mask_h, taps_h, gain_h, shift_h, up_h, down_h,
    output, field_grad, kernel_grad, norm_grad, up_grad, down_grad,
    field, cotangent, mask, taps, gain, shift, up, down,
    ext, sea, ep, kt, ups, mixed, normed, active, pregrad, mp, kacc, uacc, dacc, eg, egs, rb,
    pay1, ra1, zb1, gb1, pay2, ra2, zb2, gb2,
    relay_f, relay_b, ins, fs, fr, bs, br, ar_s, ar_r, rf, rb_s,
):
    g = Grid(*sizes)
    factor = 1.0 / math.sqrt(1024 * g.nlon * g.nlat * g.nens)
    owner = g.plane < g.owners

    loads = {}
    for k, (name, src, dst) in enumerate(
        (
            ("mask", mask_h, mask),
            ("field", field_h, field),
            ("cotangent", cotangent_h, cotangent),
            ("taps", taps_h, taps),
            ("gain", gain_h, gain),
            ("shift", shift_h, shift),
            ("up", up_h, up),
            ("down", down_h, down),
        )
    ):
        loads[name] = pltpu.make_async_copy(src, dst, ins.at[k])
        loads[name].start()

    barrier = pltpu.get_barrier_semaphore()

    def greet(**where):
        pl.semaphore_signal(barrier, inc=1, device_id=where, device_id_type=MESH)

    for lon in g.lons:
        greet(lon=lon)

    relay_here = jnp.int32(0)
    for lat in g.relays:
        relay_here = relay_here + (g.lat == lat).astype(jnp.int32)

        @pl.when(g.north)
        def _(lat=lat):
            for step in (0, 1, -1):
                greet(lat=lat, lon=across(g, step))

    east = lax.rem(g.lon + 1, g.nlon)
    west = lax.rem(g.lon + g.nlon - 1, g.nlon)

    @pl.when(g.lat > 0)
    def _():
        greet(lat=g.lat - 1, lon=east)
        greet(lat=g.lat - 1, lon=west)

    @pl.when(g.lat < g.nlat - 1)
    def _():
        greet(lat=g.lat + 1, lon=east)
        greet(lat=g.lat + 1, lon=west)

    for lat, ens in g.peers:
        greet(lat=lat, ens=ens)

    eye = (
        lax.broadcasted_iota(jnp.int32, (64, 64), 0) == lax.broadcasted_iota(jnp.int32, (64, 64), 1)
    )
    ones = jnp.ones((64, 128), BF16)
    loads["mask"].wait()
    loads["field"].wait()
    for r in range(16):
        marks = jnp.broadcast_to(mask[r : r + 1, :].astype(F32), (64, 64))
        spread = jnp.where(eye, marks, 0.0).astype(BF16)
        wide = jnp.dot(spread, ones, preferred_element_type=F32).reshape(8, 8, 128)
        sea[r] = wide
        ext[r + REACH, 1:9] = (field[r].astype(F32) * wide).astype(BF16)

    count = g.planes + g.nlon - 2
    count = count + 2 * (g.lat > 0).astype(jnp.int32) + 2 * (g.lat < g.nlat - 1).astype(jnp.int32)
    pl.semaphore_wait(barrier, count + 3 * relay_here)
    halo_start(g, ext, ext, FWD_ROWS, FWD_COLS, fs, fr, (CENTER, NORTH, SOUTH))

    @pl.when(g.north)
    def _():
        fold_start(g, ext, ext, FWD_ROWS, FWD_COLS, fs, fr, relay_f, rf)


    loads["cotangent"].wait()
    for name in ("taps", "gain", "shift", "up", "down"):
        loads[name].wait()

    def upstream_row(r, carry):
        wide = cotangent[r].astype(F32) * sea[r]
        ups[pl.ds(pl.multiple_of(r * 64, 64), 64), :] = wide.reshape(64, 128).astype(BF16)
        return carry

    lax.fori_loop(0, 16, upstream_row, 0, unroll=4)
    for t in range(TAPS):
        kt[t] = jnp.broadcast_to(taps[t : t + 1, :], (8, 128))
    kacc[...] = jnp.zeros_like(kacc)

    def widen_row(r, carry):
        blocks = ext[r].astype(F32)
        ep[0, r] = blocks
        for k, moved in enumerate(phases_of(blocks)):
            ep[k + 1, r, 0:9] = moved
        return carry

    halo_wait_recv(g, ext, fr, CENTER)
    fold_pass_on(g, ext, FWD_COLS, fr, relay_f, rf)
    lax.fori_loop(REACH, 16 + REACH, widen_row, 0)

    halo_wait_recv(g, ext, fr, SOUTH)

    @pl.when(g.lat == 0)
    def _():
        ext[0:REACH] = jnp.zeros((REACH, 10, 8, 128), BF16)

    lax.fori_loop(0, REACH, widen_row, 0)

    def conv_row(r, carry):
        total = jnp.zeros((8, 8, 128), F32)
        for i in range(KERNEL):
            for j in range(KERNEL):
                off = 2 + 2 * j
                ph, skip = (off % 8) // 2, off // 8
                total = total + kt[i * KERNEL + j][None] * ep[ph, r + 2 * i, skip : skip + 8]
        mixed[pl.ds(pl.multiple_of(r * 64, 64), 64), :] = total.reshape(64, 128)
        return carry

    gain_row = gain[...]
    shift_row = shift[...]

    def group(first, many):
        lax.fori_loop(first, first + many, conv_row, 0)
        cells = slice(64 * first, 64 * (first + many))
        rows = slice(first, first + many)
        x = mixed[cells, :]
        centered = x - jnp.mean(x, -1, keepdims=True)
        rstd = lax.rsqrt(jnp.mean(centered * centered, -1, keepdims=True) + 1e-06)
        unit = centered * rstd
        norm = (unit * gain_row + shift_row).astype(BF16)
        normed[cells, :] = norm
        pre = jnp.dot(norm, up[...], preferred_element_type=F32)
        square = pre * pre
        tanh_val = jnp.tanh(pre * (SLOPE + (SLOPE * CUBIC) * square))
        half = 0.5 + 0.5 * tanh_val
        gated = pre * half
        act = gated.astype(BF16)
        active[cells, :] = act
        product = jnp.dot(act, down[...], preferred_element_type=F32).reshape(many, 8, 8, 128)
        output[rows] = ((field[rows].astype(F32) + product) * sea[rows]).astype(BF16)
        act_grad = rdot(ups[cells, :], down[...])
        deriv = half + gated * (1.0 - tanh_val) * (SLOPE + (3.0 * SLOPE * CUBIC) * square)
        pre_grad = (act_grad * deriv).astype(BF16)
        pregrad[cells, :] = pre_grad
        nig = rdot(pre_grad, up[...])
        scaled = nig * gain_row
        kacc[TAPS] += jnp.sum((nig * unit).reshape(8 * many, 8, 128), 0)
        kacc[TAPS + 1] += jnp.sum(nig.reshape(8 * many, 8, 128), 0)
        mg = rstd * (
            scaled
            - jnp.mean(scaled, -1, keepdims=True)
            - unit * jnp.mean(scaled * unit, -1, keepdims=True)
        )
        mp[0, rows, 1:9] = mg.reshape(many, 8, 8, 128)

    zero_block = jnp.zeros((1, 8, 128), F32)

    def spread_row(r, carry):
        mp[0, r, 0:1] = zero_block
        blocks = jnp.concatenate([zero_block, mp[0, r, 1:9], zero_block], 0)
        for k, moved in enumerate(phases_of(blocks)):
            mp[k + 1, r] = moved
        return carry

    def tap_row(r, carry):
        grad = mp[0, r, 1:9]
        for i in range(KERNEL):
            for j in range(KERNEL):
                off = 2 + 2 * j
                ph, skip = (off % 8) // 2, off // 8
                kacc[i * KERNEL + j] += jnp.sum(grad * ep[ph, r + 2 * i, skip : skip + 8], 0)
        return carry

    group(0, 5)
    group(5, 5)
    lax.fori_loop(0, 10, tap_row, 0)
    lax.fori_loop(0, 10, spread_row, 0)
    uacc[...] = tdot(normed[0:640, :], pregrad[0:640, :])
    dacc[...] = tdot(active[0:640, :], ups[0:640, :])
    halo_wait_recv(g, ext, fr, NORTH)

    flip = (
        lax.broadcasted_iota(jnp.int32, (80, 80), 0)
        + lax.broadcasted_iota(jnp.int32, (80, 80), 1)
        == 79
    ).astype(F32).astype(BF16)

    @pl.when(jnp.logical_not(g.north))
    def _():
        lax.fori_loop(16 + REACH, 16 + 2 * REACH, widen_row, 0)

    @pl.when(g.north)
    def _():
        for k in range(REACH):
            row = ext[16 + REACH + k].astype(F32).reshape(80, 128).astype(BF16)
            turned = jnp.dot(flip, row, preferred_element_type=F32).reshape(10, 8, 128)
            r = 16 + 2 * REACH - 1 - k
            ep[0, r] = turned
            for s, moved in enumerate(phases_of(turned)):
                ep[s + 1, r, 0:9] = moved

    group(10, 6)
    lax.fori_loop(10, 16, spread_row, 0)

    def eg_row(p, first, last):
        lo = jnp.zeros((9, 8, 128), F32)
        hi = jnp.zeros((9, 8, 128), F32)
        for i in range(first, last + 1):
            for j in range(KERNEL):
                off = 14 - 2 * j
                ph, skip = (off % 8) // 2, off // 8
                term = kt[i * KERNEL + j][None] * mp[ph, p - 2 * i]
                if skip:
                    lo = lo + term
                else:
                    hi = hi + term
        return jnp.concatenate([lo, zero_block], 0) + jnp.concatenate([zero_block, hi], 0)

    def eg_halo(start, first, last):
        def one(p, carry):
            egs[p] = eg_row(p, first, last).astype(BF16)
            return carry

        lax.fori_loop(start, start + 2, one, 0)

    def eg_center(start, stop, first, last):
        def one(p, carry):
            value = eg_row(p, first, last)
            eg[p - REACH] = value[1:9]
            egs[p, 0:1] = value[0:1].astype(BF16)
            egs[p, 9:10] = value[9:10].astype(BF16)
            return carry

        lax.fori_loop(start, stop, one, 0)

    for m in range(3):
        eg_halo(22 + 2 * m, 4 + m, 6)
    halo_start(g, egs, rb, BWD_ROWS, BWD_COLS, bs, br, (NORTH,))

    @pl.when(g.north)
    def _():
        fold_start(g, egs, rb, BWD_ROWS, BWD_COLS, bs, br, relay_b, rb_s)


    chunk = 512 // g.planes
    per = 128 // chunk
    up_part = (uacc[...] + tdot(normed[640:1024, :], pregrad[640:1024, :])).astype(BF16)
    pay1[0:per] = up_part[:, 0:128].reshape(per, chunk, 128)
    pay1[per : 2 * per] = up_part[:, 128:256].reshape(per, chunk, 128)
    down_part = (dacc[...] + tdot(active[640:1024, :], ups[640:1024, :])).astype(BF16)
    pay1[2 * per : 4 * per] = down_part.reshape(2 * per, chunk, 128)
    ra1[g.plane] = pay1[g.plane]
    plane_send(g, lambda peer: pay1.at[peer], ra1, ar_s.at[0], ar_r.at[0])

    lax.fori_loop(10, 16, tap_row, 0)
    small = 64 // g.owners
    pay2[...] = jnp.sum(kacc[...], 1).reshape(g.owners, small, 128)

    @pl.when(owner)
    def _():
        ra2[g.plane] = pay2[g.plane]

    owner_send(g, pay2, ra2, ar_s.at[1], ar_r.at[1])

    for m in range(3):
        eg_halo(2 * m, 0, m)
    halo_start(g, egs, rb, BWD_ROWS, BWD_COLS, bs, br, (SOUTH,))
    for m in range(3, 6):
        eg_center(2 * m, 2 * m + 2, 0, m)
    eg_center(12, 16, 0, 6)
    for m in range(3):
        eg_center(16 + 2 * m, 18 + 2 * m, 1 + m, 6)
    halo_start(g, egs, rb, BWD_ROWS, BWD_COLS, bs, br, (CENTER,))
    fold_pass_on(g, rb, BWD_COLS, br, relay_b, rb_s)

    bulk_wait(ra1, g.planes - 1, ar_r.at[0])
    zb1[g.lon] = jnp.sum(ra1[...].astype(F32), 0).astype(BF16)
    lon_send(g, zb1, ar_s.at[2], ar_r.at[2])

    @pl.when(owner)
    def _():
        bulk_wait(ra2, g.planes - 1, ar_r.at[1])
        zb2[g.lon] = jnp.sum(ra2[...], 0)
        lon_send(g, zb2, ar_s.at[3], ar_r.at[3])

    halo_wait_recv(g, rb, br, CENTER)

    def edge_row(r, carry):
        eg[r, 0:1] += rb[r + REACH, 0:1].astype(F32)
        eg[r, 7:8] += rb[r + REACH, 9:10].astype(F32)
        return carry

    lax.fori_loop(0, 16, edge_row, 0)
    halo_wait_recv(g, rb, br, SOUTH)

    def fold_in(r, row):
        eg[r] += row[1:9]
        eg[r, 0:1] += row[0:1]
        eg[r, 7:8] += row[9:10]

    @pl.when(g.lat > 0)
    def _():
        def one(k, carry):
            fold_in(k, rb[k].astype(F32))
            return carry

        lax.fori_loop(0, REACH, one, 0)

    halo_wait_recv(g, rb, br, NORTH)

    @pl.when(jnp.logical_not(g.north))
    def _():
        def one(k, carry):
            fold_in(10 + k, rb[22 + k].astype(F32))
            return carry

        lax.fori_loop(0, REACH, one, 0)

    @pl.when(g.north)
    def _():
        for k in range(REACH):
            row = rb[22 + k].astype(F32).reshape(80, 128).astype(BF16)
            fold_in(15 - k, jnp.dot(flip, row, preferred_element_type=F32).reshape(10, 8, 128))

    def last_row(r, carry):
        field_grad[r] = ((cotangent[r].astype(F32) + eg[r]) * sea[r]).astype(BF16)
        return carry

    lax.fori_loop(0, 16, last_row, 0, unroll=2)

    bulk_wait(zb1, g.nlon - 1, ar_r.at[2])
    gb1[g.plane] = jnp.sum(zb1[...].astype(F32), 0).astype(BF16)
    plane_send(g, lambda peer: gb1.at[g.plane], gb1, ar_s.at[4], ar_r.at[4])

    @pl.when(owner)
    def _():
        bulk_wait(zb2, g.nlon - 1, ar_r.at[3])
        gb2[g.plane] = jnp.sum(zb2[...], 0)
        plane_send(g, lambda peer: gb2.at[g.plane], gb2, ar_s.at[5], ar_r.at[5])

    bulk_wait(gb1, g.planes - 1, ar_r.at[4])
    up_grad[:, 0:128] = gb1[0:per].astype(F32).reshape(128, 128) * factor
    up_grad[:, 128:256] = gb1[per : 2 * per].astype(F32).reshape(128, 128) * factor
    down_grad[...] = gb1[2 * per : 4 * per].astype(F32).reshape(256, 128) * factor

    @pl.when(owner)
    def _():
        bulk_wait(gb2, g.owners - 1, ar_r.at[5])

    @pl.when(jnp.logical_not(owner))
    def _():
        bulk_wait(gb2, g.owners, ar_r.at[5])

    small_sums = gb2[...].reshape(64, 128) * factor
    kernel_grad[...] = small_sums[0:TAPS]
    norm_grad[...] = small_sums[TAPS : TAPS + 2]

    halo_wait_send(g, ext, FWD_ROWS, FWD_COLS, fs)
    halo_wait_send(g, egs, BWD_ROWS, BWD_COLS, bs)
    fold_wait_send(g, ext, FWD_ROWS, FWD_COLS, fs, relay_f, rf)
    fold_wait_send(g, egs, BWD_ROWS, BWD_COLS, bs, relay_b, rb_s)
    bulk_wait(pay1, g.planes - 1, ar_s.at[0])
    bulk_wait(zb1, g.nlon - 1, ar_s.at[2])
    bulk_wait(gb1, g.planes - 1, ar_s.at[4])

    @pl.when(owner)
    def _():
        bulk_wait(pay2, g.owners - 1, ar_s.at[1])
        bulk_wait(zb2, g.nlon - 1, ar_s.at[3])
        bulk_wait(ra2, g.planes - 1, ar_s.at[5])

    @pl.when(jnp.logical_not(owner))
    def _():
        bulk_wait(pay2, g.owners, ar_s.at[1])


def write_out(*refs):
    sems = refs[-1]
    half = len(refs) // 2
    copies = [
        pltpu.make_async_copy(src, dst, sems.at[k])
        for k, (src, dst) in enumerate(zip(refs[:half], refs[half:-1]))
    ]
    for copy in copies:
        copy.start()
    for copy in copies:
        copy.wait()


def shards(sizes, field, cotangent, land_mask, kernel_taps, norm_gain, norm_shift, up_weight, down_weight):
    planes = sizes[1] * sizes[2]
    owners = min(8, planes)
    chunk, small = 512 // planes, 64 // owners
    tile = (16, 8, 8, 128)
    vmem = pl.BlockSpec(memory_space=pltpu.VMEM)
    hbm = pl.BlockSpec(memory_space=pltpu.HBM)
    dma = pltpu.SemaphoreType.DMA
    results = (
        jax.ShapeDtypeStruct(tile, BF16),
        jax.ShapeDtypeStruct(tile, BF16),
        jax.ShapeDtypeStruct((TAPS, 128), F32),
        jax.ShapeDtypeStruct((2, 128), F32),
        jax.ShapeDtypeStruct((128, 256), F32),
        jax.ShapeDtypeStruct((256, 128), F32),
    )
    held = pl.pallas_call(
        functools.partial(kernel, sizes),
        out_shape=results,
        in_specs=[hbm] * 8,
        out_specs=(vmem,) * 6,
        scratch_shapes=[
            pltpu.VMEM(tile, BF16),
            pltpu.VMEM(tile, BF16),
            pltpu.VMEM((16, 64), jnp.int32),
            pltpu.VMEM((TAPS, 128), F32),
            pltpu.VMEM((1, 128), F32),
            pltpu.VMEM((1, 128), F32),
            pltpu.VMEM((128, 256), BF16),
            pltpu.VMEM((256, 128), BF16),
            pltpu.VMEM((28, 10, 8, 128), BF16),
            pltpu.VMEM(tile, F32),
            pltpu.VMEM((4, 28, 10, 8, 128), F32),
            pltpu.VMEM((TAPS, 8, 128), F32),
            pltpu.VMEM((1024, 128), BF16),
            pltpu.VMEM((1024, 128), F32),
            pltpu.VMEM((1024, 128), BF16),
            pltpu.VMEM((1024, 256), BF16),
            pltpu.VMEM((1024, 256), BF16),
            pltpu.VMEM((4, 16, 9, 8, 128), F32),
            pltpu.VMEM((64, 8, 128), F32),
            pltpu.VMEM((128, 256), F32),
            pltpu.VMEM((256, 128), F32),
            pltpu.VMEM(tile, F32),
            pltpu.VMEM((28, 10, 8, 128), BF16),
            pltpu.VMEM((28, 10, 8, 128), BF16),
            pltpu.VMEM((planes, chunk, 128), BF16),
            pltpu.VMEM((planes, chunk, 128), BF16),
            pltpu.VMEM((sizes[0], chunk, 128), BF16),
            pltpu.VMEM((planes, chunk, 128), BF16),
            pltpu.VMEM((owners, small, 128), F32),
            pltpu.VMEM((planes, small, 128), F32),
            pltpu.VMEM((sizes[0], small, 128), F32),
            pltpu.VMEM((owners, small, 128), F32),
            pltpu.VMEM((2, 10, 8, 128), BF16),
            pltpu.VMEM((2, 10, 8, 128), BF16),
            dma((8,)),
            dma((9,)),
            dma((9,)),
            dma((9,)),
            dma((9,)),
            dma((6,)),
            dma((6,)),
            dma((6,)),
            dma((6,)),
        ],
        compiler_params=pltpu.CompilerParams(
            collective_id=0, has_side_effects=True, vmem_limit_bytes=48 * 1024 * 1024
        ),
        name="ocean_block",
    )(
        *(
            pltpu.with_memory_space_constraint(x, pltpu.HBM)
            for x in (
                field.reshape(tile),
                cotangent.reshape(tile),
                land_mask,
                kernel_taps,
                norm_gain.reshape(1, 128),
                norm_shift.reshape(1, 128),
                up_weight,
                down_weight,
            )
        )
    )
    out = pl.pallas_call(
        write_out,
        out_shape=results,
        in_specs=[vmem] * 6,
        out_specs=(hbm,) * 6,
        scratch_shapes=[dma((6,))],
        compiler_params=pltpu.CompilerParams(vmem_limit_bytes=8 * 1024 * 1024),
        name="write_out",
    )(*held)
    return (out[0].reshape(field.shape), out[1].reshape(field.shape)) + tuple(out[2:])


def solution(mesh):
    sizes = (mesh.shape["lon"], mesh.shape["lat"], mesh.shape["ens"])
    tiles = P("ens", "lat", "lon", None)
    in_specs = (tiles, tiles, P("lat", "lon"), P(), P(), P(), P(), P())
    out_specs = (tiles, tiles, P(), P(), P(), P())
    return jax.shard_map(
        functools.partial(shards, sizes),
        mesh=mesh,
        in_specs=in_specs,
        out_specs=out_specs,
        check_vma=False,
    )
```

```python
import functools
import math

import jax
import jax.numpy as jnp
from jax import lax
from jax.experimental import pallas as pl
from jax.experimental.pallas import tpu as pltpu
from jax.sharding import PartitionSpec as P

KERNEL = 7
REACH = 6
TAPS = KERNEL * KERNEL
MESH = pl.DeviceIdType.MESH
F32 = jnp.float32
BF16 = jnp.bfloat16
SLOPE = math.sqrt(2.0 / math.pi)
CUBIC = 0.044715

SOUTH, CENTER, NORTH = 0, 1, 2
WEST, MIDDLE, EAST = 0, 1, 2


def rdot(a, b):
    return lax.dot_general(a, b, (((1,), (1,)), ((), ())), preferred_element_type=F32)


def tdot(a, b):
    return lax.dot_general(a, b, (((0,), (0,)), ((), ())), preferred_element_type=F32)


def phases_of(blocks):
    count = blocks.shape[0]
    sub = lax.broadcasted_iota(jnp.int32, (count - 1, 8, 128), 1)
    out = []
    for shift in (2, 4, 6):
        rolled = pltpu.roll(blocks, 8 - shift, 1)
        out.append(jnp.where(sub < 8 - shift, rolled[: count - 1], rolled[1:]))
    return out


def region(ref, rows, cols):
    return ref.at[pl.ds(*rows), pl.ds(*cols)]


DST_ROWS = {SOUTH: (0, 6), CENTER: (6, 16), NORTH: (22, 6)}
DST_COLS = {WEST: (0, 1), MIDDLE: (1, 8), EAST: (9, 1)}
REGIONS = [(r, c) for r in range(3) for c in range(3) if (r, c) != (CENTER, MIDDLE)]


class Grid:
    def __init__(self, nlon, nlat, nens):
        self.nlon, self.nlat, self.nens = nlon, nlat, nens
        self.lon = lax.axis_index("lon")
        self.lat = lax.axis_index("lat")
        self.ens = lax.axis_index("ens")
        self.north = self.lat == nlat - 1
        self.plane = self.lat * nens + self.ens
        self.planes = nlat * nens
        if nlat == 8 and nens == 4:
            self.owner_at = [(lat, ens) for lat in (0, 2, 4, 6) for ens in (0, 2)]
            self.owner = (lax.rem(self.lat, 2) + lax.rem(self.ens, 2)) == 0
            self.owned = self.lat // 2 * 2 + self.ens // 2
        else:
            self.owner_at = [(p // nens, p % nens) for p in range(min(8, self.planes))]
            self.owner = self.plane < len(self.owner_at)
            self.owned = self.plane
        self.owners = len(self.owner_at)
        self.relays = ((nlat - 3, 2), (1, 2)) if nlat == 8 else ()
        self.relayed = sum(rows for _, rows in self.relays)
        across, along = nlat // 2, nens // 2 * 2
        y = self.ens // 2 * 2 + lax.rem(self.lat, 2)
        core = lax.rem(self.ens, 2)
        xs = [lax.rem(self.lat // 2 + d, across) for d in range(across)]
        ys = [lax.rem(y + d, along) for d in range(along)]
        steps = [(dx, dy, dc) for dx in range(across) for dy in range(along) for dc in range(2)][1:]
        steps.sort(key=lambda s: -min(s[0], across - s[0]) - min(s[1], along - s[1]))
        self.peers = []
        for dx, dy, dc in steps:
            lat = xs[dx] * 2 + lax.rem(ys[dy], 2)
            ens = ys[dy] // 2 * 2 + (1 - core if dc else core)
            self.peers.append((lat, ens))
        far = sorted(range(1, nlon), key=lambda k: -min(k, nlon - k))
        self.lons = [lax.rem(self.lon + k, nlon) for k in far]


def halo_start(g, src, dst, src_rows, src_cols, ssem, rsem, only_rows):
    for rr, cc in sorted(REGIONS, key=lambda rc: only_rows.index(rc[0]) if rc[0] in only_rows else 9):
        if rr not in only_rows:
            continue
        here = region(src, src_rows[rr], src_cols[cc])
        land_c = 2 - cc
        step = cc - 1
        east = lax.rem(g.lon + step + g.nlon, g.nlon)

        def send(lat, lon, land_r, here=here, rr=rr, cc=cc, land_c=land_c):
            pltpu.make_async_remote_copy(
                src_ref=here,
                dst_ref=region(dst, DST_ROWS[land_r], DST_COLS[land_c]),
                send_sem=ssem.at[rr * 3 + cc],
                recv_sem=rsem.at[land_r * 3 + land_c],
                device_id={"lon": lon, "lat": lat},
                device_id_type=MESH,
            ).start()

        if rr == CENTER:
            send(g.lat, east, CENTER)
        elif rr == SOUTH:

            @pl.when(g.lat > 0)
            def _(send=send, east=east):
                send(g.lat - 1, east, NORTH)

        else:

            @pl.when(jnp.logical_not(g.north))
            def _(send=send, east=east):
                send(g.lat + 1, east, SOUTH)


def across(g, step):
    return lax.rem(2 * g.nlon - 1 - g.lon - step, g.nlon)


def fold_sends(g, here, dst, dst_row, count, cols, ssem, rsem, first_row):
    for cc in (MIDDLE, EAST, WEST):
        lon = across(g, cc - 1)
        part = here.at[pl.ds(first_row, count), pl.ds(*cols[cc])]
        land = dst.at[pl.ds(dst_row, count), pl.ds(*DST_COLS[2 - cc])]
        arrived = rsem.at[NORTH * 3 + 2 - cc]

        def go(part=part, land=land, arrived=arrived, lon=lon, cc=cc):
            pltpu.make_async_remote_copy(
                src_ref=part,
                dst_ref=land,
                send_sem=ssem(cc),
                recv_sem=arrived,
                device_id={"lon": lon, "lat": g.nlat - 1},
                device_id_type=MESH,
            ).start()

        yield cc, lon, part, land, arrived, go


def relay_part(g, relay, src_cols, rows):
    low, high = src_cols[WEST][0], src_cols[EAST][0] + 1
    return relay.at[pl.ds(0, rows), pl.ds(low, high - low)]


def fold_start(g, src, dst, src_rows, src_cols, ssem, rsem, relay, rsems):
    row, total = src_rows[NORTH]
    low, high = src_cols[WEST][0], src_cols[EAST][0] + 1
    own = total - g.relayed
    first = row + own
    for q, (lat, rows) in enumerate(g.relays):
        pltpu.make_async_remote_copy(
            src_ref=src.at[pl.ds(first, rows), pl.ds(low, high - low)],
            dst_ref=relay_part(g, relay, src_cols, rows),
            send_sem=rsems.at[q],
            recv_sem=rsems.at[3],
            device_id={"lat": lat},
            device_id_type=MESH,
        ).start()
        first += rows
    for cc, lon, part, land, arrived, go in fold_sends(
        g, src, dst, DST_ROWS[NORTH][0], own, src_cols, lambda cc: ssem.at[NORTH * 3 + cc], rsem, row
    ):
        if cc == MIDDLE:
            go()
        else:
            pl.when(lon != g.lon)(go)

            @pl.when(lon == g.lon)
            def _(part=part, land=land, arrived=arrived):
                pltpu.make_async_copy(part, land, arrived).start()


def fold_pass_on(g, dst, src_cols, rsem, relay, rsems):
    first = DST_ROWS[NORTH][0] + DST_ROWS[NORTH][1] - g.relayed
    for lat, rows in g.relays:

        @pl.when(g.lat == lat)
        def _(first=first, rows=rows):
            part = relay_part(g, relay, src_cols, rows)
            pltpu.make_async_copy(part, part, rsems.at[3]).wait()
            for cc, lon, _, _, _, go in fold_sends(
                g, relay, dst, first, rows, src_cols, lambda cc: rsems.at[4 + cc], rsem, 0
            ):
                go()

        first += rows


def fold_wait_send(g, src, src_rows, src_cols, ssem, relay, rsems):
    row, total = src_rows[NORTH]
    own = total - g.relayed

    @pl.when(g.north)
    def _():
        for cc in range(3):
            part = src.at[pl.ds(row, own), pl.ds(*src_cols[cc])]
            wait = pltpu.make_async_copy(part, part, ssem.at[NORTH * 3 + cc]).wait
            if cc == MIDDLE:
                wait()
            else:
                pl.when(across(g, cc - 1) != g.lon)(wait)
        for q, (_, rows) in enumerate(g.relays):
            whole = relay_part(g, relay, src_cols, rows)
            pltpu.make_async_copy(whole, whole, rsems.at[q]).wait()

    for lat, rows in g.relays:

        @pl.when(g.lat == lat)
        def _(rows=rows):
            for cc in range(3):
                part = relay.at[pl.ds(0, rows), pl.ds(*src_cols[cc])]
                pltpu.make_async_copy(part, part, rsems.at[4 + cc]).wait()


def halo_wait_recv(g, dst, rsem, row):
    for cc in range(3):
        if (row, cc) == (CENTER, MIDDLE):
            continue
        part = region(dst, DST_ROWS[row], DST_COLS[cc])
        wait = pltpu.make_async_copy(part, part, rsem.at[row * 3 + cc]).wait
        if row == SOUTH:
            pl.when(g.lat > 0)(wait)
        else:
            wait()


def halo_wait_send(g, src, src_rows, src_cols, ssem):
    for rr, cc in REGIONS:
        here = region(src, src_rows[rr], src_cols[cc])
        wait = pltpu.make_async_copy(here, here, ssem.at[rr * 3 + cc]).wait
        if rr == CENTER:
            wait()
        elif rr == SOUTH:
            pl.when(g.lat > 0)(wait)
        else:
            pl.when(jnp.logical_not(g.north))(wait)


def plane_send(g, src_of, dst, ssem, rsem, slot=None):
    slot = g.plane if slot is None else slot
    for lat, ens in g.peers:
        pltpu.make_async_remote_copy(
            src_ref=src_of(lat * g.nens + ens),
            dst_ref=dst.at[slot],
            send_sem=ssem,
            recv_sem=rsem,
            device_id={"lat": lat, "ens": ens},
            device_id_type=MESH,
        ).start()


def owner_send(g, src, dst, ssem, rsem):
    for o, (lat, ens) in enumerate(g.owner_at):

        @pl.when(g.plane != lat * g.nens + ens)
        def _(o=o, lat=lat, ens=ens):
            pltpu.make_async_remote_copy(
                src_ref=src.at[o],
                dst_ref=dst.at[g.plane],
                send_sem=ssem,
                recv_sem=rsem,
                device_id={"lat": lat, "ens": ens},
                device_id_type=MESH,
            ).start()


def lon_send(g, buf, ssem, rsem):
    for lon in g.lons:
        pltpu.make_async_remote_copy(
            src_ref=buf.at[g.lon],
            dst_ref=buf.at[g.lon],
            send_sem=ssem,
            recv_sem=rsem,
            device_id={"lon": lon},
            device_id_type=MESH,
        ).start()


def bulk_wait(buf, count, sem):
    part = buf.at[pl.ds(0, count)]
    pltpu.make_async_copy(part, part, sem).wait()


FWD_ROWS = {SOUTH: (6, 6), CENTER: (6, 16), NORTH: (16, 6)}
FWD_COLS = {WEST: (1, 1), MIDDLE: (1, 8), EAST: (8, 1)}
BWD_ROWS = {SOUTH: (0, 6), CENTER: (6, 16), NORTH: (22, 6)}
BWD_COLS = {WEST: (0, 1), MIDDLE: (1, 8), EAST: (9, 1)}


def kernel(
    sizes,
    field_h, cotangent_h, mask_h, taps_h, gain_h, shift_h, up_h, down_h,
    output, field_grad, kernel_grad, norm_grad, up_grad, down_grad,
    field, cotangent, mask, taps, gain, shift, up, down,
    ext, sea, ep, kt, ups, mixed, normed, active, pregrad, mp, kacc, uacc, dacc, eg, egs, rb,
    pay1, ra1, zb1, gb1, pay2, ra2, zb2, gb2,
    relay_f, relay_b, ins, fs, fr, bs, br, ar_s, ar_r, rf, rb_s,
):
    g = Grid(*sizes)
    factor = 1.0 / math.sqrt(1024 * g.nlon * g.nlat * g.nens)
    owner = g.owner

    loads = {}
    for k, (name, src, dst) in enumerate(
        (
            ("mask", mask_h, mask),
            ("field", field_h, field),
            ("cotangent", cotangent_h, cotangent),
            ("taps", taps_h, taps),
            ("gain", gain_h, gain),
            ("shift", shift_h, shift),
            ("up", up_h, up),
            ("down", down_h, down),
        )
    ):
        loads[name] = pltpu.make_async_copy(src, dst, ins.at[k])
        loads[name].start()

    barrier = pltpu.get_barrier_semaphore()

    def greet(**where):
        pl.semaphore_signal(barrier, inc=1, device_id=where, device_id_type=MESH)

    for lon in g.lons:
        greet(lon=lon)

    east = lax.rem(g.lon + 1, g.nlon)
    west = lax.rem(g.lon + g.nlon - 1, g.nlon)

    @pl.when(g.lat > 0)
    def _():
        greet(lat=g.lat - 1, lon=east)
        greet(lat=g.lat - 1, lon=west)

    @pl.when(g.lat < g.nlat - 1)
    def _():
        greet(lat=g.lat + 1, lon=east)
        greet(lat=g.lat + 1, lon=west)

    for lat, ens in g.peers:
        greet(lat=lat, ens=ens)

    eye = (
        lax.broadcasted_iota(jnp.int32, (64, 64), 0) == lax.broadcasted_iota(jnp.int32, (64, 64), 1)
    )
    ones = jnp.ones((64, 128), BF16)
    loads["mask"].wait()
    loads["field"].wait()
    for r in range(16):
        marks = jnp.broadcast_to(mask[r : r + 1, :].astype(F32), (64, 64))
        spread = jnp.where(eye, marks, 0.0).astype(BF16)
        wide = jnp.dot(spread, ones, preferred_element_type=F32).reshape(8, 8, 128)
        sea[r] = wide
        ext[r + REACH, 1:9] = (field[r].astype(F32) * wide).astype(BF16)

    count = g.planes + g.nlon - 2
    count = count + 2 * (g.lat > 0).astype(jnp.int32) + 2 * (g.lat < g.nlat - 1).astype(jnp.int32)
    pl.semaphore_wait(barrier, count)

    @pl.when(g.north)
    def _():
        fold_start(g, ext, ext, FWD_ROWS, FWD_COLS, fs, fr, relay_f, rf)

    halo_start(g, ext, ext, FWD_ROWS, FWD_COLS, fs, fr, (CENTER, NORTH, SOUTH))


    loads["cotangent"].wait()
    for name in ("taps", "gain", "shift", "up", "down"):
        loads[name].wait()

    def upstream_row(r, carry):
        wide = cotangent[r].astype(F32) * sea[r]
        ups[pl.ds(pl.multiple_of(r * 64, 64), 64), :] = wide.reshape(64, 128).astype(BF16)
        return carry

    lax.fori_loop(0, 16, upstream_row, 0, unroll=4)
    for t in range(TAPS):
        kt[t] = jnp.broadcast_to(taps[t : t + 1, :], (8, 128))
    kacc[...] = jnp.zeros_like(kacc)

    def widen_row(r, carry):
        blocks = ext[r].astype(F32)
        ep[0, r] = blocks
        for k, moved in enumerate(phases_of(blocks)):
            ep[k + 1, r, 0:9] = moved
        return carry

    fold_pass_on(g, ext, FWD_COLS, fr, relay_f, rf)
    halo_wait_recv(g, ext, fr, CENTER)
    lax.fori_loop(REACH, 16 + REACH, widen_row, 0)

    def conv_row(r, carry):
        total = jnp.zeros((8, 8, 128), F32)
        for i in range(KERNEL):
            for j in range(KERNEL):
                off = 2 + 2 * j
                ph, skip = (off % 8) // 2, off // 8
                total = total + kt[i * KERNEL + j][None] * ep[ph, r + 2 * i, skip : skip + 8]
        mixed[pl.ds(pl.multiple_of(r * 64, 64), 64), :] = total.reshape(64, 128)
        return carry

    gain_row = gain[...]
    shift_row = shift[...]

    def group(first, many):
        lax.fori_loop(first, first + many, conv_row, 0)
        cells = slice(64 * first, 64 * (first + many))
        rows = slice(first, first + many)
        x = mixed[cells, :]
        centered = x - jnp.mean(x, -1, keepdims=True)
        rstd = lax.rsqrt(jnp.mean(centered * centered, -1, keepdims=True) + 1e-06)
        unit = centered * rstd
        norm = (unit * gain_row + shift_row).astype(BF16)
        normed[cells, :] = norm
        pre = jnp.dot(norm, up[...], preferred_element_type=F32)
        square = pre * pre
        tanh_val = jnp.tanh(pre * (SLOPE + (SLOPE * CUBIC) * square))
        half = 0.5 + 0.5 * tanh_val
        gated = pre * half
        act = gated.astype(BF16)
        active[cells, :] = act
        product = jnp.dot(act, down[...], preferred_element_type=F32).reshape(many, 8, 8, 128)
        output[rows] = ((field[rows].astype(F32) + product) * sea[rows]).astype(BF16)
        act_grad = rdot(ups[cells, :], down[...])
        deriv = half + gated * (1.0 - tanh_val) * (SLOPE + (3.0 * SLOPE * CUBIC) * square)
        pre_grad = (act_grad * deriv).astype(BF16)
        pregrad[cells, :] = pre_grad
        nig = rdot(pre_grad, up[...])
        scaled = nig * gain_row
        kacc[TAPS] += jnp.sum((nig * unit).reshape(8 * many, 8, 128), 0)
        kacc[TAPS + 1] += jnp.sum(nig.reshape(8 * many, 8, 128), 0)
        mg = rstd * (
            scaled
            - jnp.mean(scaled, -1, keepdims=True)
            - unit * jnp.mean(scaled * unit, -1, keepdims=True)
        )
        mp[0, rows, 1:9] = mg.reshape(many, 8, 8, 128)

    zero_block = jnp.zeros((1, 8, 128), F32)

    def spread_row(r, carry):
        mp[0, r, 0:1] = zero_block
        blocks = jnp.concatenate([zero_block, mp[0, r, 1:9], zero_block], 0)
        for k, moved in enumerate(phases_of(blocks)):
            mp[k + 1, r] = moved
        return carry

    def tap_row(r, carry):
        grad = mp[0, r, 1:9]
        for i in range(KERNEL):
            for j in range(KERNEL):
                off = 2 + 2 * j
                ph, skip = (off % 8) // 2, off // 8
                kacc[i * KERNEL + j] += jnp.sum(grad * ep[ph, r + 2 * i, skip : skip + 8], 0)
        return carry

    group(6, 4)
    halo_wait_recv(g, ext, fr, SOUTH)

    @pl.when(g.lat == 0)
    def _():
        ext[0:REACH] = jnp.zeros((REACH, 10, 8, 128), BF16)

    lax.fori_loop(0, REACH, widen_row, 0)

    group(0, 6)
    lax.fori_loop(0, 10, tap_row, 0)
    lax.fori_loop(0, 10, spread_row, 0)
    uacc[...] = tdot(normed[0:640, :], pregrad[0:640, :])
    dacc[...] = tdot(active[0:640, :], ups[0:640, :])
    halo_wait_recv(g, ext, fr, NORTH)

    flip = (
        lax.broadcasted_iota(jnp.int32, (80, 80), 0)
        + lax.broadcasted_iota(jnp.int32, (80, 80), 1)
        == 79
    ).astype(F32).astype(BF16)

    @pl.when(jnp.logical_not(g.north))
    def _():
        lax.fori_loop(16 + REACH, 16 + 2 * REACH, widen_row, 0)

    @pl.when(g.north)
    def _():
        for k in range(REACH):
            row = ext[16 + REACH + k].astype(F32).reshape(80, 128).astype(BF16)
            turned = jnp.dot(flip, row, preferred_element_type=F32).reshape(10, 8, 128)
            r = 16 + 2 * REACH - 1 - k
            ep[0, r] = turned
            for s, moved in enumerate(phases_of(turned)):
                ep[s + 1, r, 0:9] = moved

    group(10, 6)
    lax.fori_loop(10, 16, spread_row, 0)

    def eg_row(p, first, last):
        lo = jnp.zeros((9, 8, 128), F32)
        hi = jnp.zeros((9, 8, 128), F32)
        for i in range(first, last + 1):
            for j in range(KERNEL):
                off = 14 - 2 * j
                ph, skip = (off % 8) // 2, off // 8
                term = kt[i * KERNEL + j][None] * mp[ph, p - 2 * i]
                if skip:
                    lo = lo + term
                else:
                    hi = hi + term
        return jnp.concatenate([lo, zero_block], 0) + jnp.concatenate([zero_block, hi], 0)

    def eg_halo(start, first, last):
        def one(p, carry):
            egs[p] = eg_row(p, first, last).astype(BF16)
            return carry

        lax.fori_loop(start, start + 2, one, 0)

    def eg_center(start, stop, first, last):
        def one(p, carry):
            value = eg_row(p, first, last)
            eg[p - REACH] = value[1:9]
            egs[p, 0:1] = value[0:1].astype(BF16)
            egs[p, 9:10] = value[9:10].astype(BF16)
            return carry

        lax.fori_loop(start, stop, one, 0)

    for m in range(3):
        eg_halo(22 + 2 * m, 4 + m, 6)
    halo_start(g, egs, rb, BWD_ROWS, BWD_COLS, bs, br, (NORTH,))

    @pl.when(g.north)
    def _():
        fold_start(g, egs, rb, BWD_ROWS, BWD_COLS, bs, br, relay_b, rb_s)


    chunk = 512 // g.planes
    per = 128 // chunk
    up_part = (uacc[...] + tdot(normed[640:1024, :], pregrad[640:1024, :])).astype(BF16)
    pay1[0:per] = up_part[:, 0:128].reshape(per, chunk, 128)
    pay1[per : 2 * per] = up_part[:, 128:256].reshape(per, chunk, 128)
    down_part = (dacc[...] + tdot(active[640:1024, :], ups[640:1024, :])).astype(BF16)
    pay1[2 * per : 4 * per] = down_part.reshape(2 * per, chunk, 128)
    ra1[g.plane] = pay1[g.plane]
    plane_send(g, lambda peer: pay1.at[peer], ra1, ar_s.at[0], ar_r.at[0])

    lax.fori_loop(10, 16, tap_row, 0)
    small = 64 // g.owners
    pay2[...] = jnp.sum(kacc[...], 1).reshape(g.owners, small, 128).astype(BF16)

    @pl.when(owner)
    def _():
        ra2[g.plane] = pay2[g.owned]

    owner_send(g, pay2, ra2, ar_s.at[1], ar_r.at[1])

    for m in range(3):
        eg_halo(2 * m, 0, m)
    halo_start(g, egs, rb, BWD_ROWS, BWD_COLS, bs, br, (SOUTH,))
    for m in range(3, 6):
        eg_center(2 * m, 2 * m + 2, 0, m)
    eg_center(12, 16, 0, 6)
    for m in range(3):
        eg_center(16 + 2 * m, 18 + 2 * m, 1 + m, 6)
    halo_start(g, egs, rb, BWD_ROWS, BWD_COLS, bs, br, (CENTER,))
    fold_pass_on(g, rb, BWD_COLS, br, relay_b, rb_s)

    bulk_wait(ra1, g.planes - 1, ar_r.at[0])
    zb1[g.lon] = jnp.sum(ra1[...].astype(F32), 0).astype(BF16)
    lon_send(g, zb1, ar_s.at[2], ar_r.at[2])

    @pl.when(owner)
    def _():
        bulk_wait(ra2, g.planes - 1, ar_r.at[1])
        zb2[g.lon] = jnp.sum(ra2[...].astype(F32), 0).astype(BF16)
        lon_send(g, zb2, ar_s.at[3], ar_r.at[3])

    bulk_wait(zb1, g.nlon - 1, ar_r.at[2])
    gb1[g.plane] = jnp.sum(zb1[...].astype(F32), 0).astype(BF16)
    plane_send(g, lambda peer: gb1.at[g.plane], gb1, ar_s.at[4], ar_r.at[4])

    @pl.when(owner)
    def _():
        bulk_wait(zb2, g.nlon - 1, ar_r.at[3])
        gb2[g.owned] = jnp.sum(zb2[...].astype(F32), 0).astype(BF16)
        plane_send(g, lambda peer: gb2.at[g.owned], gb2, ar_s.at[5], ar_r.at[5], g.owned)

    halo_wait_recv(g, rb, br, CENTER)

    def edge_row(r, carry):
        eg[r, 0:1] += rb[r + REACH, 0:1].astype(F32)
        eg[r, 7:8] += rb[r + REACH, 9:10].astype(F32)
        return carry

    lax.fori_loop(0, 16, edge_row, 0)
    halo_wait_recv(g, rb, br, SOUTH)

    def fold_in(r, row):
        eg[r] += row[1:9]
        eg[r, 0:1] += row[0:1]
        eg[r, 7:8] += row[9:10]

    @pl.when(g.lat > 0)
    def _():
        def one(k, carry):
            fold_in(k, rb[k].astype(F32))
            return carry

        lax.fori_loop(0, REACH, one, 0)

    halo_wait_recv(g, rb, br, NORTH)

    @pl.when(jnp.logical_not(g.north))
    def _():
        def one(k, carry):
            fold_in(10 + k, rb[22 + k].astype(F32))
            return carry

        lax.fori_loop(0, REACH, one, 0)

    @pl.when(g.north)
    def _():
        for k in range(REACH):
            row = rb[22 + k].astype(F32).reshape(80, 128).astype(BF16)
            fold_in(15 - k, jnp.dot(flip, row, preferred_element_type=F32).reshape(10, 8, 128))

    def last_row(r, carry):
        field_grad[r] = ((cotangent[r].astype(F32) + eg[r]) * sea[r]).astype(BF16)
        return carry

    lax.fori_loop(0, 16, last_row, 0, unroll=2)

    bulk_wait(gb1, g.planes - 1, ar_r.at[4])
    up_grad[:, 0:128] = gb1[0:per].astype(F32).reshape(128, 128) * factor
    up_grad[:, 128:256] = gb1[per : 2 * per].astype(F32).reshape(128, 128) * factor
    down_grad[...] = gb1[2 * per : 4 * per].astype(F32).reshape(256, 128) * factor

    @pl.when(owner)
    def _():
        bulk_wait(gb2, g.owners - 1, ar_r.at[5])

    @pl.when(jnp.logical_not(owner))
    def _():
        bulk_wait(gb2, g.owners, ar_r.at[5])

    small_sums = gb2[...].astype(F32).reshape(64, 128) * factor
    kernel_grad[...] = small_sums[0:TAPS]
    norm_grad[...] = small_sums[TAPS : TAPS + 2]

    halo_wait_send(g, ext, FWD_ROWS, FWD_COLS, fs)
    halo_wait_send(g, egs, BWD_ROWS, BWD_COLS, bs)
    fold_wait_send(g, ext, FWD_ROWS, FWD_COLS, fs, relay_f, rf)
    fold_wait_send(g, egs, BWD_ROWS, BWD_COLS, bs, relay_b, rb_s)
    bulk_wait(pay1, g.planes - 1, ar_s.at[0])
    bulk_wait(zb1, g.nlon - 1, ar_s.at[2])
    bulk_wait(gb1, g.planes - 1, ar_s.at[4])

    @pl.when(owner)
    def _():
        bulk_wait(pay2, g.owners - 1, ar_s.at[1])
        bulk_wait(zb2, g.nlon - 1, ar_s.at[3])
        bulk_wait(ra2, g.planes - 1, ar_s.at[5])

    @pl.when(jnp.logical_not(owner))
    def _():
        bulk_wait(pay2, g.owners, ar_s.at[1])


def write_out(*refs):
    sems = refs[-1]
    half = len(refs) // 2
    copies = [
        pltpu.make_async_copy(src, dst, sems.at[k])
        for k, (src, dst) in enumerate(zip(refs[:half], refs[half:-1]))
    ]
    for copy in copies:
        copy.start()
    for copy in copies:
        copy.wait()


def shards(sizes, field, cotangent, land_mask, kernel_taps, norm_gain, norm_shift, up_weight, down_weight):
    planes = sizes[1] * sizes[2]
    owners = min(8, planes)
    chunk, small = 512 // planes, 64 // owners
    tile = (16, 8, 8, 128)
    vmem = pl.BlockSpec(memory_space=pltpu.VMEM)
    hbm = pl.BlockSpec(memory_space=pltpu.HBM)
    dma = pltpu.SemaphoreType.DMA
    results = (
        jax.ShapeDtypeStruct(tile, BF16),
        jax.ShapeDtypeStruct(tile, BF16),
        jax.ShapeDtypeStruct((TAPS, 128), F32),
        jax.ShapeDtypeStruct((2, 128), F32),
        jax.ShapeDtypeStruct((128, 256), F32),
        jax.ShapeDtypeStruct((256, 128), F32),
    )
    held = pl.pallas_call(
        functools.partial(kernel, sizes),
        out_shape=results,
        in_specs=[hbm] * 8,
        out_specs=(vmem,) * 6,
        scratch_shapes=[
            pltpu.VMEM(tile, BF16),
            pltpu.VMEM(tile, BF16),
            pltpu.VMEM((16, 64), jnp.int32),
            pltpu.VMEM((TAPS, 128), F32),
            pltpu.VMEM((1, 128), F32),
            pltpu.VMEM((1, 128), F32),
            pltpu.VMEM((128, 256), BF16),
            pltpu.VMEM((256, 128), BF16),
            pltpu.VMEM((28, 10, 8, 128), BF16),
            pltpu.VMEM(tile, F32),
            pltpu.VMEM((4, 28, 10, 8, 128), F32),
            pltpu.VMEM((TAPS, 8, 128), F32),
            pltpu.VMEM((1024, 128), BF16),
            pltpu.VMEM((1024, 128), F32),
            pltpu.VMEM((1024, 128), BF16),
            pltpu.VMEM((1024, 256), BF16),
            pltpu.VMEM((1024, 256), BF16),
            pltpu.VMEM((4, 16, 9, 8, 128), F32),
            pltpu.VMEM((64, 8, 128), F32),
            pltpu.VMEM((128, 256), F32),
            pltpu.VMEM((256, 128), F32),
            pltpu.VMEM(tile, F32),
            pltpu.VMEM((28, 10, 8, 128), BF16),
            pltpu.VMEM((28, 10, 8, 128), BF16),
            pltpu.VMEM((planes, chunk, 128), BF16),
            pltpu.VMEM((planes, chunk, 128), BF16),
            pltpu.VMEM((sizes[0], chunk, 128), BF16),
            pltpu.VMEM((planes, chunk, 128), BF16),
            pltpu.VMEM((owners, small, 128), BF16),
            pltpu.VMEM((planes, small, 128), BF16),
            pltpu.VMEM((sizes[0], small, 128), BF16),
            pltpu.VMEM((owners, small, 128), BF16),
            pltpu.VMEM((2, 10, 8, 128), BF16),
            pltpu.VMEM((2, 10, 8, 128), BF16),
            dma((8,)),
            dma((9,)),
            dma((9,)),
            dma((9,)),
            dma((9,)),
            dma((6,)),
            dma((6,)),
            dma((7,)),
            dma((7,)),
        ],
        compiler_params=pltpu.CompilerParams(
            collective_id=0, has_side_effects=True, vmem_limit_bytes=48 * 1024 * 1024
        ),
        name="ocean_block",
    )(
        *(
            pltpu.with_memory_space_constraint(x, pltpu.HBM)
            for x in (
                field.reshape(tile),
                cotangent.reshape(tile),
                land_mask,
                kernel_taps,
                norm_gain.reshape(1, 128),
                norm_shift.reshape(1, 128),
                up_weight,
                down_weight,
            )
        )
    )
    out = pl.pallas_call(
        write_out,
        out_shape=results,
        in_specs=[vmem] * 6,
        out_specs=(hbm,) * 6,
        scratch_shapes=[dma((6,))],
        compiler_params=pltpu.CompilerParams(vmem_limit_bytes=8 * 1024 * 1024),
        name="write_out",
    )(*held)
    return (out[0].reshape(field.shape), out[1].reshape(field.shape)) + tuple(out[2:])


def solution(mesh):
    sizes = (mesh.shape["lon"], mesh.shape["lat"], mesh.shape["ens"])
    tiles = P("ens", "lat", "lon", None)
    in_specs = (tiles, tiles, P("lat", "lon"), P(), P(), P(), P(), P())
    out_specs = (tiles, tiles, P(), P(), P(), P())
    return jax.shard_map(
        functools.partial(shards, sizes),
        mesh=mesh,
        in_specs=in_specs,
        out_specs=out_specs,
        check_vma=False,
    )
```

```python
import functools
import math

import jax
import jax.numpy as jnp
from jax import lax
from jax.experimental import pallas as pl
from jax.experimental.pallas import tpu as pltpu
from jax.sharding import PartitionSpec as P

KERNEL = 7
REACH = 6
TAPS = KERNEL * KERNEL
MESH = pl.DeviceIdType.MESH
F32 = jnp.float32
BF16 = jnp.bfloat16
SLOPE = math.sqrt(2.0 / math.pi)
CUBIC = 0.044715

SOUTH, CENTER, NORTH = 0, 1, 2
WEST, MIDDLE, EAST = 0, 1, 2


def rdot(a, b):
    return lax.dot_general(a, b, (((1,), (1,)), ((), ())), preferred_element_type=F32)


def tdot(a, b):
    return lax.dot_general(a, b, (((0,), (0,)), ((), ())), preferred_element_type=F32)


def phases_of(blocks):
    count = blocks.shape[0]
    sub = lax.broadcasted_iota(jnp.int32, (count - 1, 8, 128), 1)
    out = []
    for shift in (2, 4, 6):
        rolled = pltpu.roll(blocks, 8 - shift, 1)
        out.append(jnp.where(sub < 8 - shift, rolled[: count - 1], rolled[1:]))
    return out


def region(ref, rows, cols):
    return ref.at[pl.ds(*rows), pl.ds(*cols)]


DST_ROWS = {SOUTH: (0, 6), CENTER: (6, 16), NORTH: (22, 6)}
DST_COLS = {WEST: (0, 1), MIDDLE: (1, 8), EAST: (9, 1)}
REGIONS = [(r, c) for r in range(3) for c in range(3) if (r, c) != (CENTER, MIDDLE)]


class Grid:
    def __init__(self, nlon, nlat, nens):
        self.nlon, self.nlat, self.nens = nlon, nlat, nens
        self.lon = lax.axis_index("lon")
        self.lat = lax.axis_index("lat")
        self.ens = lax.axis_index("ens")
        self.north = self.lat == nlat - 1
        self.plane = self.lat * nens + self.ens
        self.planes = nlat * nens
        if nlat == 8 and nens == 4:
            self.owner_at = [(lat, ens) for lat in (0, 2, 4, 6) for ens in (0, 2)]
            self.owner = (lax.rem(self.lat, 2) + lax.rem(self.ens, 2)) == 0
            self.owned = self.lat // 2 * 2 + self.ens // 2
        else:
            self.owner_at = [(p // nens, p % nens) for p in range(min(8, self.planes))]
            self.owner = self.plane < len(self.owner_at)
            self.owned = self.plane
        self.owners = len(self.owner_at)
        self.relays = ((nlat - 3, 2), (1, 2)) if nlat == 8 else ()
        self.relayed = sum(rows for _, rows in self.relays)
        across, along = nlat // 2, nens // 2 * 2
        y = self.ens // 2 * 2 + lax.rem(self.lat, 2)
        core = lax.rem(self.ens, 2)
        hop = lambda d: {"lon": lax.rem(self.lon + d + nlon, nlon)}
        x, low, high = self.lat // 2, lax.rem(self.lat, 2), self.ens // 2
        self.first = [hop(d) for d in (1, -1, 2, -2)]
        self.lon_rounds = [[hop(d), hop(-d)] for d in (2, 4) if 2 * d <= nlon]
        twin = {"ens": high * 2 + (1 - core)}
        beside = {"lat": x * 2 + (1 - low)}
        self.plane_rounds = [[twin], [beside]]
        if along == 4:
            self.plane_rounds.insert(1, [{"ens": (1 - high) * 2 + core}])
        if across == 4:
            ring = [{"lat": lax.rem(x + d, 4) * 2 + low} for d in (1, 3)]
            self.plane_rounds += [ring, ring]
        for near in self.plane_rounds[: 3 if along == 4 else 2] + self.plane_rounds[3:4]:
            self.first += near
        xs = [lax.rem(self.lat // 2 + d, across) for d in range(across)]
        ys = [lax.rem(y + d, along) for d in range(along)]
        steps = [(dx, dy, dc) for dx in range(across) for dy in range(along) for dc in range(2)][1:]
        steps.sort(key=lambda s: -min(s[0], across - s[0]) - min(s[1], along - s[1]))
        self.peers = []
        for dx, dy, dc in steps:
            lat = xs[dx] * 2 + lax.rem(ys[dy], 2)
            ens = ys[dy] // 2 * 2 + (1 - core if dc else core)
            self.peers.append((lat, ens))
        far = sorted(range(1, nlon), key=lambda k: -min(k, nlon - k))
        self.lons = [lax.rem(self.lon + k, nlon) for k in far]


def halo_start(g, src, dst, src_rows, src_cols, ssem, rsem, only_rows):
    for rr, cc in sorted(REGIONS, key=lambda rc: only_rows.index(rc[0]) if rc[0] in only_rows else 9):
        if rr not in only_rows:
            continue
        here = region(src, src_rows[rr], src_cols[cc])
        land_c = 2 - cc
        step = cc - 1
        east = lax.rem(g.lon + step + g.nlon, g.nlon)

        def send(lat, lon, land_r, here=here, rr=rr, cc=cc, land_c=land_c):
            pltpu.make_async_remote_copy(
                src_ref=here,
                dst_ref=region(dst, DST_ROWS[land_r], DST_COLS[land_c]),
                send_sem=ssem.at[rr * 3 + cc],
                recv_sem=rsem.at[land_r * 3 + land_c],
                device_id={"lon": lon, "lat": lat},
                device_id_type=MESH,
            ).start()

        if rr == CENTER:
            send(g.lat, east, CENTER)
        elif rr == SOUTH:

            @pl.when(g.lat > 0)
            def _(send=send, east=east):
                send(g.lat - 1, east, NORTH)

        else:

            @pl.when(jnp.logical_not(g.north))
            def _(send=send, east=east):
                send(g.lat + 1, east, SOUTH)


def across(g, step):
    return lax.rem(2 * g.nlon - 1 - g.lon - step, g.nlon)


def fold_sends(g, here, dst, dst_row, count, cols, ssem, rsem, first_row):
    for cc in (MIDDLE, EAST, WEST):
        lon = across(g, cc - 1)
        part = here.at[pl.ds(first_row, count), pl.ds(*cols[cc])]
        land = dst.at[pl.ds(dst_row, count), pl.ds(*DST_COLS[2 - cc])]
        arrived = rsem.at[NORTH * 3 + 2 - cc]

        def go(part=part, land=land, arrived=arrived, lon=lon, cc=cc):
            pltpu.make_async_remote_copy(
                src_ref=part,
                dst_ref=land,
                send_sem=ssem(cc),
                recv_sem=arrived,
                device_id={"lon": lon, "lat": g.nlat - 1},
                device_id_type=MESH,
            ).start()

        yield cc, lon, part, land, arrived, go


def relay_part(g, relay, src_cols, rows):
    low, high = src_cols[WEST][0], src_cols[EAST][0] + 1
    return relay.at[pl.ds(0, rows), pl.ds(low, high - low)]


def relay_send(g, src, src_rows, src_cols, relay, rsems):
    low, high = src_cols[WEST][0], src_cols[EAST][0] + 1
    first = sum(src_rows[NORTH]) - g.relayed
    for q, (lat, rows) in enumerate(g.relays):
        pltpu.make_async_remote_copy(
            src_ref=src.at[pl.ds(first, rows), pl.ds(low, high - low)],
            dst_ref=relay_part(g, relay, src_cols, rows),
            send_sem=rsems.at[q],
            recv_sem=rsems.at[3],
            device_id={"lat": lat},
            device_id_type=MESH,
        ).start()
        first += rows


def fold_own(g, src, dst, src_rows, src_cols, ssem, rsem):
    row, total = src_rows[NORTH]
    for cc, lon, part, land, arrived, go in fold_sends(
        g,
        src,
        dst,
        DST_ROWS[NORTH][0],
        total - g.relayed,
        src_cols,
        lambda cc: ssem.at[NORTH * 3 + cc],
        rsem,
        row,
    ):
        if cc == MIDDLE:
            go()
        else:
            pl.when(lon != g.lon)(go)

            @pl.when(lon == g.lon)
            def _(part=part, land=land, arrived=arrived):
                pltpu.make_async_copy(part, land, arrived).start()


def fold_pass_on(g, dst, src_cols, rsem, relay, rsems):
    first = DST_ROWS[NORTH][0] + DST_ROWS[NORTH][1] - g.relayed
    for lat, rows in g.relays:

        @pl.when(g.lat == lat)
        def _(first=first, rows=rows):
            part = relay_part(g, relay, src_cols, rows)
            pltpu.make_async_copy(part, part, rsems.at[3]).wait()
            for cc, lon, _, _, _, go in fold_sends(
                g, relay, dst, first, rows, src_cols, lambda cc: rsems.at[4 + cc], rsem, 0
            ):
                go()

        first += rows


def fold_wait_send(g, src, src_rows, src_cols, ssem, relay, rsems):
    row, total = src_rows[NORTH]
    own = total - g.relayed

    @pl.when(g.north)
    def _():
        for cc in range(3):
            part = src.at[pl.ds(row, own), pl.ds(*src_cols[cc])]
            wait = pltpu.make_async_copy(part, part, ssem.at[NORTH * 3 + cc]).wait
            if cc == MIDDLE:
                wait()
            else:
                pl.when(across(g, cc - 1) != g.lon)(wait)
        for q, (_, rows) in enumerate(g.relays):
            whole = relay_part(g, relay, src_cols, rows)
            pltpu.make_async_copy(whole, whole, rsems.at[q]).wait()

    for lat, rows in g.relays:

        @pl.when(g.lat == lat)
        def _(rows=rows):
            for cc in range(3):
                part = relay.at[pl.ds(0, rows), pl.ds(*src_cols[cc])]
                pltpu.make_async_copy(part, part, rsems.at[4 + cc]).wait()


def halo_wait_recv(g, dst, rsem, row):
    for cc in range(3):
        if (row, cc) == (CENTER, MIDDLE):
            continue
        part = region(dst, DST_ROWS[row], DST_COLS[cc])
        wait = pltpu.make_async_copy(part, part, rsem.at[row * 3 + cc]).wait
        if row == SOUTH:
            pl.when(g.lat > 0)(wait)
        else:
            wait()


def halo_wait_send(g, src, src_rows, src_cols, ssem):
    for rr, cc in REGIONS:
        here = region(src, src_rows[rr], src_cols[cc])
        wait = pltpu.make_async_copy(here, here, ssem.at[rr * 3 + cc]).wait
        if rr == CENTER:
            wait()
        elif rr == SOUTH:
            pl.when(g.lat > 0)(wait)
        else:
            pl.when(jnp.logical_not(g.north))(wait)


def plane_send(g, src_of, dst, ssem, rsem, slot=None):
    slot = g.plane if slot is None else slot
    for lat, ens in g.peers:
        pltpu.make_async_remote_copy(
            src_ref=src_of(lat * g.nens + ens),
            dst_ref=dst.at[slot],
            send_sem=ssem,
            recv_sem=rsem,
            device_id={"lat": lat, "ens": ens},
            device_id_type=MESH,
        ).start()


def owner_send(g, src, dst, ssem, rsem):
    for o, (lat, ens) in enumerate(g.owner_at):

        @pl.when(g.plane != lat * g.nens + ens)
        def _(o=o, lat=lat, ens=ens):
            pltpu.make_async_remote_copy(
                src_ref=src.at[o],
                dst_ref=dst.at[g.plane],
                send_sem=ssem,
                recv_sem=rsem,
                device_id={"lat": lat, "ens": ens},
                device_id_type=MESH,
            ).start()


def lon_send(g, buf, ssem, rsem):
    for lon in g.lons:
        pltpu.make_async_remote_copy(
            src_ref=buf.at[g.lon],
            dst_ref=buf.at[g.lon],
            send_sem=ssem,
            recv_sem=rsem,
            device_id={"lon": lon},
            device_id_type=MESH,
        ).start()


def bulk_wait(buf, count, sem):
    part = buf.at[pl.ds(0, count)]
    pltpu.make_async_copy(part, part, sem).wait()


FWD_ROWS = {SOUTH: (6, 6), CENTER: (6, 16), NORTH: (16, 6)}
FWD_COLS = {WEST: (1, 1), MIDDLE: (1, 8), EAST: (8, 1)}
BWD_ROWS = {SOUTH: (0, 6), CENTER: (6, 16), NORTH: (22, 6)}
BWD_COLS = {WEST: (0, 1), MIDDLE: (1, 8), EAST: (9, 1)}


def kernel(
    sizes,
    field_h, cotangent_h, mask_h, taps_h, gain_h, shift_h, up_h, down_h,
    output, field_grad, kernel_grad, norm_grad, up_grad, down_grad,
    field, cotangent, mask, taps, gain, shift, up, down,
    ext, sea, ep, kt, ups, mixed, normed, active, pregrad, mp, kacc, uacc, dacc, eg, egs, rb,
    pay1, ra1, zb1, gb1, pay2, ra2, zb2, gb2,
    relay_f, relay_b, ins, fs, fr, bs, br, ar_s, ar_r, rf, rb_s, lon_sem, plane_sem,
):
    g = Grid(*sizes)
    factor = 1.0 / math.sqrt(1024 * g.nlon * g.nlat * g.nens)
    owner = g.owner

    loads = {}
    for k, (name, src, dst) in enumerate(
        (
            ("mask", mask_h, mask),
            ("field", field_h, field),
            ("cotangent", cotangent_h, cotangent),
            ("taps", taps_h, taps),
            ("gain", gain_h, gain),
            ("shift", shift_h, shift),
            ("up", up_h, up),
            ("down", down_h, down),
        )
    ):
        loads[name] = pltpu.make_async_copy(src, dst, ins.at[k])
        loads[name].start()

    barrier = pltpu.get_barrier_semaphore()

    def greet(**where):
        pl.semaphore_signal(barrier, inc=1, device_id=where, device_id_type=MESH)

    for where in g.first:
        greet(**where)
    east = lax.rem(g.lon + 1, g.nlon)
    west = lax.rem(g.lon + g.nlon - 1, g.nlon)

    @pl.when(g.lat > 0)
    def _():
        for lon in (east, west, g.lon):
            greet(lat=g.lat - 1, lon=lon)

    @pl.when(g.lat < g.nlat - 1)
    def _():
        for lon in (east, west, g.lon):
            greet(lat=g.lat + 1, lon=lon)

    relay = jnp.int32(0)
    for lat, _ in g.relays:
        relay = relay + (g.lat == lat).astype(jnp.int32)

        @pl.when(g.north)
        def _(lat=lat):
            for where in g.first[:4]:
                greet(lat=lat, **where)

    def tell(rounds, sem, k):
        for where in rounds[k]:
            pl.semaphore_signal(sem.at[k], inc=1, device_id=where, device_id_type=MESH)

    def hear(rounds, sem, k):
        pl.semaphore_wait(sem.at[k], len(rounds[k]))

    eye = (
        lax.broadcasted_iota(jnp.int32, (64, 64), 0) == lax.broadcasted_iota(jnp.int32, (64, 64), 1)
    )
    ones = jnp.ones((64, 128), BF16)
    loads["mask"].wait()
    loads["field"].wait()
    for r in range(16):
        marks = jnp.broadcast_to(mask[r : r + 1, :].astype(F32), (64, 64))
        spread = jnp.where(eye, marks, 0.0).astype(BF16)
        wide = jnp.dot(spread, ones, preferred_element_type=F32).reshape(8, 8, 128)
        sea[r] = wide
        ext[r + REACH, 1:9] = (field[r].astype(F32) * wide).astype(BF16)

    sides = (g.lat > 0).astype(jnp.int32) + (g.lat < g.nlat - 1).astype(jnp.int32)
    pl.semaphore_wait(barrier, len(g.first) + 3 * sides + 4 * relay)
    tell(g.lon_rounds, lon_sem, 0)
    tell(g.plane_rounds, plane_sem, 0)

    @pl.when(g.north)
    def _():
        relay_send(g, ext, FWD_ROWS, FWD_COLS, relay_f, rf)

    halo_start(g, ext, ext, FWD_ROWS, FWD_COLS, fs, fr, (CENTER, NORTH, SOUTH))


    loads["cotangent"].wait()
    for name in ("taps", "gain", "shift", "up", "down"):
        loads[name].wait()

    def upstream_row(r, carry):
        wide = cotangent[r].astype(F32) * sea[r]
        ups[pl.ds(pl.multiple_of(r * 64, 64), 64), :] = wide.reshape(64, 128).astype(BF16)
        return carry

    lax.fori_loop(0, 16, upstream_row, 0, unroll=4)
    for t in range(TAPS):
        kt[t] = jnp.broadcast_to(taps[t : t + 1, :], (8, 128))
    kacc[...] = jnp.zeros_like(kacc)

    def widen_row(r, carry):
        blocks = ext[r].astype(F32)
        ep[0, r] = blocks
        for k, moved in enumerate(phases_of(blocks)):
            ep[k + 1, r, 0:9] = moved
        return carry

    hear(g.lon_rounds, lon_sem, 0)
    tell(g.lon_rounds, lon_sem, 1)
    hear(g.plane_rounds, plane_sem, 0)
    tell(g.plane_rounds, plane_sem, 1)
    halo_wait_recv(g, ext, fr, CENTER)
    lax.fori_loop(REACH, 16 + REACH, widen_row, 0)

    def conv_row(r, carry):
        total = jnp.zeros((8, 8, 128), F32)
        for i in range(KERNEL):
            for j in range(KERNEL):
                off = 2 + 2 * j
                ph, skip = (off % 8) // 2, off // 8
                total = total + kt[i * KERNEL + j][None] * ep[ph, r + 2 * i, skip : skip + 8]
        mixed[pl.ds(pl.multiple_of(r * 64, 64), 64), :] = total.reshape(64, 128)
        return carry

    gain_row = gain[...]
    shift_row = shift[...]

    def conv_pair(start, taps_i, more):
        def one(r, carry):
            cells = pl.ds(pl.multiple_of(r * 64, 64), 64)
            total = mixed[cells, :].reshape(8, 8, 128) if more else jnp.zeros((8, 8, 128), F32)
            for i in taps_i:
                for j in range(KERNEL):
                    off = 2 + 2 * j
                    ph, skip = (off % 8) // 2, off // 8
                    total = total + kt[i * KERNEL + j][None] * ep[ph, r + 2 * i, skip : skip + 8]
            mixed[cells, :] = total.reshape(64, 128)
            return carry

        lax.fori_loop(start, start + 2, one, 0)

    def group(first, many, conv=True):
        if conv:
            lax.fori_loop(first, first + many, conv_row, 0)
        cells = slice(64 * first, 64 * (first + many))
        rows = slice(first, first + many)
        x = mixed[cells, :]
        centered = x - jnp.mean(x, -1, keepdims=True)
        rstd = lax.rsqrt(jnp.mean(centered * centered, -1, keepdims=True) + 1e-06)
        unit = centered * rstd
        norm = (unit * gain_row + shift_row).astype(BF16)
        normed[cells, :] = norm
        pre = jnp.dot(norm, up[...], preferred_element_type=F32)
        square = pre * pre
        tanh_val = jnp.tanh(pre * (SLOPE + (SLOPE * CUBIC) * square))
        half = 0.5 + 0.5 * tanh_val
        gated = pre * half
        act = gated.astype(BF16)
        active[cells, :] = act
        product = jnp.dot(act, down[...], preferred_element_type=F32).reshape(many, 8, 8, 128)
        output[rows] = ((field[rows].astype(F32) + product) * sea[rows]).astype(BF16)
        act_grad = rdot(ups[cells, :], down[...])
        deriv = half + gated * (1.0 - tanh_val) * (SLOPE + (3.0 * SLOPE * CUBIC) * square)
        pre_grad = (act_grad * deriv).astype(BF16)
        pregrad[cells, :] = pre_grad
        nig = rdot(pre_grad, up[...])
        scaled = nig * gain_row
        kacc[TAPS] += jnp.sum((nig * unit).reshape(8 * many, 8, 128), 0)
        kacc[TAPS + 1] += jnp.sum(nig.reshape(8 * many, 8, 128), 0)
        mg = rstd * (
            scaled
            - jnp.mean(scaled, -1, keepdims=True)
            - unit * jnp.mean(scaled * unit, -1, keepdims=True)
        )
        mp[0, rows, 1:9] = mg.reshape(many, 8, 8, 128)

    zero_block = jnp.zeros((1, 8, 128), F32)

    def spread_row(r, carry):
        mp[0, r, 0:1] = zero_block
        blocks = jnp.concatenate([zero_block, mp[0, r, 1:9], zero_block], 0)
        for k, moved in enumerate(phases_of(blocks)):
            mp[k + 1, r] = moved
        return carry

    def tap_row(r, carry):
        grad = mp[0, r, 1:9]
        for i in range(KERNEL):
            for j in range(KERNEL):
                off = 2 + 2 * j
                ph, skip = (off % 8) // 2, off // 8
                kacc[i * KERNEL + j] += jnp.sum(grad * ep[ph, r + 2 * i, skip : skip + 8], 0)
        return carry

    hear(g.plane_rounds, plane_sem, 1)
    tell(g.plane_rounds, plane_sem, 2)
    crossing = jnp.logical_or(g.north, relay > 0)

    @pl.when(crossing)
    def _():
        hear(g.lon_rounds, lon_sem, 1)

    @pl.when(g.north)
    def _():
        fold_own(g, ext, ext, FWD_ROWS, FWD_COLS, fs, fr)

    fold_pass_on(g, ext, FWD_COLS, fr, relay_f, rf)
    group(6, 4)
    hear(g.plane_rounds, plane_sem, 2)
    tell(g.plane_rounds, plane_sem, 3)
    halo_wait_recv(g, ext, fr, SOUTH)

    @pl.when(g.lat == 0)
    def _():
        ext[0:REACH] = jnp.zeros((REACH, 10, 8, 128), BF16)

    lax.fori_loop(0, REACH, widen_row, 0)

    hear(g.plane_rounds, plane_sem, 3)
    tell(g.plane_rounds, plane_sem, 4)
    group(0, 6)
    lax.fori_loop(0, 10, tap_row, 0)
    lax.fori_loop(0, 10, spread_row, 0)
    uacc[...] = tdot(normed[0:640, :], pregrad[0:640, :])
    dacc[...] = tdot(active[0:640, :], ups[0:640, :])
    for m in range(3):
        conv_pair(10 + 2 * m, range(6 - m), False)
    halo_wait_recv(g, ext, fr, NORTH)

    flip = (
        lax.broadcasted_iota(jnp.int32, (80, 80), 0)
        + lax.broadcasted_iota(jnp.int32, (80, 80), 1)
        == 79
    ).astype(F32).astype(BF16)

    @pl.when(jnp.logical_not(g.north))
    def _():
        lax.fori_loop(16 + REACH, 16 + 2 * REACH, widen_row, 0)

    @pl.when(g.north)
    def _():
        for k in range(REACH):
            row = ext[16 + REACH + k].astype(F32).reshape(80, 128).astype(BF16)
            turned = jnp.dot(flip, row, preferred_element_type=F32).reshape(10, 8, 128)
            r = 16 + 2 * REACH - 1 - k
            ep[0, r] = turned
            for s, moved in enumerate(phases_of(turned)):
                ep[s + 1, r, 0:9] = moved

    for m in range(3):
        conv_pair(10 + 2 * m, range(6 - m, KERNEL), True)
    group(10, 6, False)
    def eg_row(p, first, last):
        lo = jnp.zeros((9, 8, 128), F32)
        hi = jnp.zeros((9, 8, 128), F32)
        for i in range(first, last + 1):
            for j in range(KERNEL):
                off = 14 - 2 * j
                ph, skip = (off % 8) // 2, off // 8
                term = kt[i * KERNEL + j][None] * mp[ph, p - 2 * i]
                if skip:
                    lo = lo + term
                else:
                    hi = hi + term
        return jnp.concatenate([lo, zero_block], 0) + jnp.concatenate([zero_block, hi], 0)

    def eg_halo(start, first, last):
        def one(p, carry):
            egs[p] = eg_row(p, first, last).astype(BF16)
            return carry

        lax.fori_loop(start, start + 2, one, 0)

    def eg_center(start, stop, first, last):
        def one(p, carry):
            value = eg_row(p, first, last)
            eg[p - REACH] = value[1:9]
            egs[p, 0:1] = value[0:1].astype(BF16)
            egs[p, 9:10] = value[9:10].astype(BF16)
            return carry

        lax.fori_loop(start, stop, one, 0)

    chunk = 512 // g.planes
    per = 128 // chunk
    up_part = (uacc[...] + tdot(normed[640:1024, :], pregrad[640:1024, :])).astype(BF16)
    pay1[0:per] = up_part[:, 0:128].reshape(per, chunk, 128)
    pay1[per : 2 * per] = up_part[:, 128:256].reshape(per, chunk, 128)
    down_part = (dacc[...] + tdot(active[640:1024, :], ups[640:1024, :])).astype(BF16)
    pay1[2 * per : 4 * per] = down_part.reshape(2 * per, chunk, 128)
    ra1[g.plane] = pay1[g.plane]
    hear(g.plane_rounds, plane_sem, 4)
    plane_send(g, lambda peer: pay1.at[peer], ra1, ar_s.at[0], ar_r.at[0])

    lax.fori_loop(10, 16, tap_row, 0)
    small = 64 // g.owners
    pay2[...] = jnp.sum(kacc[...], 1).reshape(g.owners, small, 128).astype(BF16)

    @pl.when(owner)
    def _():
        ra2[g.plane] = pay2[g.owned]

    owner_send(g, pay2, ra2, ar_s.at[1], ar_r.at[1])

    lax.fori_loop(10, 16, spread_row, 0)

    for m in range(3):
        eg_halo(22 + 2 * m, 4 + m, 6)
    halo_start(g, egs, rb, BWD_ROWS, BWD_COLS, bs, br, (NORTH,))

    @pl.when(g.north)
    def _():
        relay_send(g, egs, BWD_ROWS, BWD_COLS, relay_b, rb_s)
        fold_own(g, egs, rb, BWD_ROWS, BWD_COLS, bs, br)


    for m in range(3):
        eg_halo(2 * m, 0, m)
    halo_start(g, egs, rb, BWD_ROWS, BWD_COLS, bs, br, (SOUTH,))
    for m in range(3, 6):
        eg_center(2 * m, 2 * m + 2, 0, m)
    eg_center(12, 16, 0, 6)
    for m in range(3):
        eg_center(16 + 2 * m, 18 + 2 * m, 1 + m, 6)
    halo_start(g, egs, rb, BWD_ROWS, BWD_COLS, bs, br, (CENTER,))
    fold_pass_on(g, rb, BWD_COLS, br, relay_b, rb_s)

    @pl.when(jnp.logical_not(crossing))
    def _():
        hear(g.lon_rounds, lon_sem, 1)

    bulk_wait(ra1, g.planes - 1, ar_r.at[0])
    zb1[g.lon] = jnp.sum(ra1[...].astype(F32), 0).astype(BF16)
    lon_send(g, zb1, ar_s.at[2], ar_r.at[2])

    @pl.when(owner)
    def _():
        bulk_wait(ra2, g.planes - 1, ar_r.at[1])
        zb2[g.lon] = jnp.sum(ra2[...].astype(F32), 0).astype(BF16)
        lon_send(g, zb2, ar_s.at[3], ar_r.at[3])

    bulk_wait(zb1, g.nlon - 1, ar_r.at[2])
    gb1[g.plane] = jnp.sum(zb1[...].astype(F32), 0).astype(BF16)
    plane_send(g, lambda peer: gb1.at[g.plane], gb1, ar_s.at[4], ar_r.at[4])

    @pl.when(owner)
    def _():
        bulk_wait(zb2, g.nlon - 1, ar_r.at[3])
        gb2[g.owned] = jnp.sum(zb2[...].astype(F32), 0).astype(BF16)
        plane_send(g, lambda peer: gb2.at[g.owned], gb2, ar_s.at[5], ar_r.at[5], g.owned)

    halo_wait_recv(g, rb, br, CENTER)

    def edge_row(r, carry):
        eg[r, 0:1] += rb[r + REACH, 0:1].astype(F32)
        eg[r, 7:8] += rb[r + REACH, 9:10].astype(F32)
        return carry

    lax.fori_loop(0, 16, edge_row, 0)
    halo_wait_recv(g, rb, br, SOUTH)

    def fold_in(r, row):
        eg[r] += row[1:9]
        eg[r, 0:1] += row[0:1]
        eg[r, 7:8] += row[9:10]

    @pl.when(g.lat > 0)
    def _():
        def one(k, carry):
            fold_in(k, rb[k].astype(F32))
            return carry

        lax.fori_loop(0, REACH, one, 0)

    halo_wait_recv(g, rb, br, NORTH)

    @pl.when(jnp.logical_not(g.north))
    def _():
        def one(k, carry):
            fold_in(10 + k, rb[22 + k].astype(F32))
            return carry

        lax.fori_loop(0, REACH, one, 0)

    @pl.when(g.north)
    def _():
        for k in range(REACH):
            row = rb[22 + k].astype(F32).reshape(80, 128).astype(BF16)
            fold_in(15 - k, jnp.dot(flip, row, preferred_element_type=F32).reshape(10, 8, 128))

    def last_row(r, carry):
        field_grad[r] = ((cotangent[r].astype(F32) + eg[r]) * sea[r]).astype(BF16)
        return carry

    lax.fori_loop(0, 16, last_row, 0, unroll=2)

    bulk_wait(gb1, g.planes - 1, ar_r.at[4])
    up_grad[:, 0:128] = gb1[0:per].astype(F32).reshape(128, 128) * factor
    up_grad[:, 128:256] = gb1[per : 2 * per].astype(F32).reshape(128, 128) * factor
    down_grad[...] = gb1[2 * per : 4 * per].astype(F32).reshape(256, 128) * factor

    @pl.when(owner)
    def _():
        bulk_wait(gb2, g.owners - 1, ar_r.at[5])

    @pl.when(jnp.logical_not(owner))
    def _():
        bulk_wait(gb2, g.owners, ar_r.at[5])

    small_sums = gb2[...].astype(F32).reshape(64, 128) * factor
    kernel_grad[...] = small_sums[0:TAPS]
    norm_grad[...] = small_sums[TAPS : TAPS + 2]

    halo_wait_send(g, ext, FWD_ROWS, FWD_COLS, fs)
    halo_wait_send(g, egs, BWD_ROWS, BWD_COLS, bs)
    fold_wait_send(g, ext, FWD_ROWS, FWD_COLS, fs, relay_f, rf)
    fold_wait_send(g, egs, BWD_ROWS, BWD_COLS, bs, relay_b, rb_s)
    bulk_wait(pay1, g.planes - 1, ar_s.at[0])
    bulk_wait(zb1, g.nlon - 1, ar_s.at[2])
    bulk_wait(gb1, g.planes - 1, ar_s.at[4])

    @pl.when(owner)
    def _():
        bulk_wait(pay2, g.owners - 1, ar_s.at[1])
        bulk_wait(zb2, g.nlon - 1, ar_s.at[3])
        bulk_wait(ra2, g.planes - 1, ar_s.at[5])

    @pl.when(jnp.logical_not(owner))
    def _():
        bulk_wait(pay2, g.owners, ar_s.at[1])


def write_out(*refs):
    sems = refs[-1]
    half = len(refs) // 2
    copies = [
        pltpu.make_async_copy(src, dst, sems.at[k])
        for k, (src, dst) in enumerate(zip(refs[:half], refs[half:-1]))
    ]
    for copy in copies:
        copy.start()
    for copy in copies:
        copy.wait()


def shards(sizes, field, cotangent, land_mask, kernel_taps, norm_gain, norm_shift, up_weight, down_weight):
    planes = sizes[1] * sizes[2]
    owners = min(8, planes)
    chunk, small = 512 // planes, 64 // owners
    tile = (16, 8, 8, 128)
    vmem = pl.BlockSpec(memory_space=pltpu.VMEM)
    hbm = pl.BlockSpec(memory_space=pltpu.HBM)
    dma = pltpu.SemaphoreType.DMA
    results = (
        jax.ShapeDtypeStruct(tile, BF16),
        jax.ShapeDtypeStruct(tile, BF16),
        jax.ShapeDtypeStruct((TAPS, 128), F32),
        jax.ShapeDtypeStruct((2, 128), F32),
        jax.ShapeDtypeStruct((128, 256), F32),
        jax.ShapeDtypeStruct((256, 128), F32),
    )
    held = pl.pallas_call(
        functools.partial(kernel, sizes),
        out_shape=results,
        in_specs=[hbm] * 8,
        out_specs=(vmem,) * 6,
        scratch_shapes=[
            pltpu.VMEM(tile, BF16),
            pltpu.VMEM(tile, BF16),
            pltpu.VMEM((16, 64), jnp.int32),
            pltpu.VMEM((TAPS, 128), F32),
            pltpu.VMEM((1, 128), F32),
            pltpu.VMEM((1, 128), F32),
            pltpu.VMEM((128, 256), BF16),
            pltpu.VMEM((256, 128), BF16),
            pltpu.VMEM((28, 10, 8, 128), BF16),
            pltpu.VMEM(tile, F32),
            pltpu.VMEM((4, 28, 10, 8, 128), F32),
            pltpu.VMEM((TAPS, 8, 128), F32),
            pltpu.VMEM((1024, 128), BF16),
            pltpu.VMEM((1024, 128), F32),
            pltpu.VMEM((1024, 128), BF16),
            pltpu.VMEM((1024, 256), BF16),
            pltpu.VMEM((1024, 256), BF16),
            pltpu.VMEM((4, 16, 9, 8, 128), F32),
            pltpu.VMEM((64, 8, 128), F32),
            pltpu.VMEM((128, 256), F32),
            pltpu.VMEM((256, 128), F32),
            pltpu.VMEM(tile, F32),
            pltpu.VMEM((28, 10, 8, 128), BF16),
            pltpu.VMEM((28, 10, 8, 128), BF16),
            pltpu.VMEM((planes, chunk, 128), BF16),
            pltpu.VMEM((planes, chunk, 128), BF16),
            pltpu.VMEM((sizes[0], chunk, 128), BF16),
            pltpu.VMEM((planes, chunk, 128), BF16),
            pltpu.VMEM((owners, small, 128), BF16),
            pltpu.VMEM((planes, small, 128), BF16),
            pltpu.VMEM((sizes[0], small, 128), BF16),
            pltpu.VMEM((owners, small, 128), BF16),
            pltpu.VMEM((2, 10, 8, 128), BF16),
            pltpu.VMEM((2, 10, 8, 128), BF16),
            dma((8,)),
            dma((9,)),
            dma((9,)),
            dma((9,)),
            dma((9,)),
            dma((6,)),
            dma((6,)),
            dma((7,)),
            dma((7,)),
            pltpu.SemaphoreType.REGULAR((2,)),
            pltpu.SemaphoreType.REGULAR((5,)),
        ],
        compiler_params=pltpu.CompilerParams(
            collective_id=0, has_side_effects=True, vmem_limit_bytes=48 * 1024 * 1024
        ),
        name="ocean_block",
    )(
        *(
            pltpu.with_memory_space_constraint(x, pltpu.HBM)
            for x in (
                field.reshape(tile),
                cotangent.reshape(tile),
                land_mask,
                kernel_taps,
                norm_gain.reshape(1, 128),
                norm_shift.reshape(1, 128),
                up_weight,
                down_weight,
            )
        )
    )
    out = pl.pallas_call(
        write_out,
        out_shape=results,
        in_specs=[vmem] * 6,
        out_specs=(hbm,) * 6,
        scratch_shapes=[dma((6,))],
        compiler_params=pltpu.CompilerParams(vmem_limit_bytes=8 * 1024 * 1024),
        name="write_out",
    )(*held)
    return (out[0].reshape(field.shape), out[1].reshape(field.shape)) + tuple(out[2:])


def solution(mesh):
    sizes = (mesh.shape["lon"], mesh.shape["lat"], mesh.shape["ens"])
    tiles = P("ens", "lat", "lon", None)
    in_specs = (tiles, tiles, P("lat", "lon"), P(), P(), P(), P(), P())
    out_specs = (tiles, tiles, P(), P(), P(), P())
    return jax.shard_map(
        functools.partial(shards, sizes),
        mesh=mesh,
        in_specs=in_specs,
        out_specs=out_specs,
        check_vma=False,
    )
```

```python
import functools
import math

import jax
import jax.numpy as jnp
from jax import lax
from jax.experimental import pallas as pl
from jax.experimental.pallas import tpu as pltpu
from jax.sharding import PartitionSpec as P

KERNEL = 7
REACH = 6
TAPS = KERNEL * KERNEL
MESH = pl.DeviceIdType.MESH
F32 = jnp.float32
BF16 = jnp.bfloat16
SLOPE = math.sqrt(2.0 / math.pi)
CUBIC = 0.044715

SOUTH, CENTER, NORTH = 0, 1, 2
WEST, MIDDLE, EAST = 0, 1, 2


def rdot(a, b):
    return lax.dot_general(a, b, (((1,), (1,)), ((), ())), preferred_element_type=F32)


def tdot(a, b):
    return lax.dot_general(a, b, (((0,), (0,)), ((), ())), preferred_element_type=F32)


def phases_of(blocks):
    count = blocks.shape[0]
    sub = lax.broadcasted_iota(jnp.int32, (count - 1, 8, 128), 1)
    out = []
    for shift in (2, 4, 6):
        rolled = pltpu.roll(blocks, 8 - shift, 1)
        out.append(jnp.where(sub < 8 - shift, rolled[: count - 1], rolled[1:]))
    return out


def region(ref, rows, cols):
    return ref.at[pl.ds(*rows), pl.ds(*cols)]


DST_ROWS = {SOUTH: (0, 6), CENTER: (6, 16), NORTH: (22, 6)}
DST_COLS = {WEST: (0, 1), MIDDLE: (1, 8), EAST: (9, 1)}
REGIONS = [(r, c) for r in range(3) for c in range(3) if (r, c) != (CENTER, MIDDLE)]


class Grid:
    def __init__(self, nlon, nlat, nens):
        self.nlon, self.nlat, self.nens = nlon, nlat, nens
        self.lon = lax.axis_index("lon")
        self.lat = lax.axis_index("lat")
        self.ens = lax.axis_index("ens")
        self.north = self.lat == nlat - 1
        self.plane = self.lat * nens + self.ens
        self.planes = nlat * nens
        if nlat == 8 and nens == 4:
            self.owner_at = [(lat, ens) for lat in (0, 2, 4, 6) for ens in (0, 2)]
            self.owner = (lax.rem(self.lat, 2) + lax.rem(self.ens, 2)) == 0
            self.owned = self.lat // 2 * 2 + self.ens // 2
        else:
            self.owner_at = [(p // nens, p % nens) for p in range(min(8, self.planes))]
            self.owner = self.plane < len(self.owner_at)
            self.owned = self.plane
        self.owners = len(self.owner_at)
        self.relays = ((nlat - 3, 2), (1, 2)) if nlat == 8 else ()
        self.relayed = sum(rows for _, rows in self.relays)
        across, along = nlat // 2, nens // 2 * 2
        y = self.ens // 2 * 2 + lax.rem(self.lat, 2)
        core = lax.rem(self.ens, 2)
        hop = lambda d: {"lon": lax.rem(self.lon + d + nlon, nlon)}
        x, low, high = self.lat // 2, lax.rem(self.lat, 2), self.ens // 2
        self.first = [hop(d) for d in (1, -1, 2, -2)]
        self.lon_rounds = [[hop(d), hop(-d)] for d in (2, 4) if 2 * d <= nlon]
        twin = {"ens": high * 2 + (1 - core)}
        beside = {"lat": x * 2 + (1 - low)}
        self.plane_rounds = [[twin], [beside]]
        if along == 4:
            self.plane_rounds.insert(1, [{"ens": (1 - high) * 2 + core}])
        if across == 4:
            ring = [{"lat": lax.rem(x + d, 4) * 2 + low} for d in (1, 3)]
            self.plane_rounds += [ring, ring]
        for near in self.plane_rounds[: 3 if along == 4 else 2] + self.plane_rounds[3:4]:
            self.first += near
        xs = [lax.rem(self.lat // 2 + d, across) for d in range(across)]
        ys = [lax.rem(y + d, along) for d in range(along)]
        steps = [(dx, dy, dc) for dx in range(across) for dy in range(along) for dc in range(2)][1:]
        steps.sort(key=lambda s: -min(s[0], across - s[0]) - min(s[1], along - s[1]))
        self.peers = []
        for dx, dy, dc in steps:
            lat = xs[dx] * 2 + lax.rem(ys[dy], 2)
            ens = ys[dy] // 2 * 2 + (1 - core if dc else core)
            self.peers.append((lat, ens))
        far = sorted(range(1, nlon), key=lambda k: -min(k, nlon - k))
        self.lons = [lax.rem(self.lon + k, nlon) for k in far]


def halo_start(g, src, dst, src_rows, src_cols, ssem, rsem, only_rows):
    for rr, cc in sorted(REGIONS, key=lambda rc: only_rows.index(rc[0]) if rc[0] in only_rows else 9):
        if rr not in only_rows:
            continue
        here = region(src, src_rows[rr], src_cols[cc])
        land_c = 2 - cc
        step = cc - 1
        east = lax.rem(g.lon + step + g.nlon, g.nlon)

        def send(lat, lon, land_r, here=here, rr=rr, cc=cc, land_c=land_c):
            pltpu.make_async_remote_copy(
                src_ref=here,
                dst_ref=region(dst, DST_ROWS[land_r], DST_COLS[land_c]),
                send_sem=ssem.at[rr * 3 + cc],
                recv_sem=rsem.at[land_r * 3 + land_c],
                device_id={"lon": lon, "lat": lat},
                device_id_type=MESH,
            ).start()

        if rr == CENTER:
            send(g.lat, east, CENTER)
        elif rr == SOUTH:

            @pl.when(g.lat > 0)
            def _(send=send, east=east):
                send(g.lat - 1, east, NORTH)

        else:

            @pl.when(jnp.logical_not(g.north))
            def _(send=send, east=east):
                send(g.lat + 1, east, SOUTH)


def across(g, step):
    return lax.rem(2 * g.nlon - 1 - g.lon - step, g.nlon)


def fold_sends(g, here, dst, dst_row, count, cols, ssem, rsem, first_row):
    for cc in (MIDDLE, EAST, WEST):
        lon = across(g, cc - 1)
        part = here.at[pl.ds(first_row, count), pl.ds(*cols[cc])]
        land = dst.at[pl.ds(dst_row, count), pl.ds(*DST_COLS[2 - cc])]
        arrived = rsem.at[NORTH * 3 + 2 - cc]

        def go(part=part, land=land, arrived=arrived, lon=lon, cc=cc):
            pltpu.make_async_remote_copy(
                src_ref=part,
                dst_ref=land,
                send_sem=ssem(cc),
                recv_sem=arrived,
                device_id={"lon": lon, "lat": g.nlat - 1},
                device_id_type=MESH,
            ).start()

        yield cc, lon, part, land, arrived, go


def relay_part(g, relay, src_cols, rows):
    low, high = src_cols[WEST][0], src_cols[EAST][0] + 1
    return relay.at[pl.ds(0, rows), pl.ds(low, high - low)]


def relay_send(g, src, src_rows, src_cols, relay, rsems):
    low, high = src_cols[WEST][0], src_cols[EAST][0] + 1
    first = sum(src_rows[NORTH]) - g.relayed
    for q, (lat, rows) in enumerate(g.relays):
        pltpu.make_async_remote_copy(
            src_ref=src.at[pl.ds(first, rows), pl.ds(low, high - low)],
            dst_ref=relay_part(g, relay, src_cols, rows),
            send_sem=rsems.at[q],
            recv_sem=rsems.at[3],
            device_id={"lat": lat},
            device_id_type=MESH,
        ).start()
        first += rows


def fold_own(g, src, dst, src_rows, src_cols, ssem, rsem):
    row, total = src_rows[NORTH]
    for cc, lon, part, land, arrived, go in fold_sends(
        g,
        src,
        dst,
        DST_ROWS[NORTH][0],
        total - g.relayed,
        src_cols,
        lambda cc: ssem.at[NORTH * 3 + cc],
        rsem,
        row,
    ):
        if cc == MIDDLE:
            go()
        else:
            pl.when(lon != g.lon)(go)

            @pl.when(lon == g.lon)
            def _(part=part, land=land, arrived=arrived):
                pltpu.make_async_copy(part, land, arrived).start()


def fold_pass_on(g, dst, src_cols, rsem, relay, rsems):
    first = DST_ROWS[NORTH][0] + DST_ROWS[NORTH][1] - g.relayed
    for lat, rows in g.relays:

        @pl.when(g.lat == lat)
        def _(first=first, rows=rows):
            part = relay_part(g, relay, src_cols, rows)
            pltpu.make_async_copy(part, part, rsems.at[3]).wait()
            for cc, lon, _, _, _, go in fold_sends(
                g, relay, dst, first, rows, src_cols, lambda cc: rsems.at[4 + cc], rsem, 0
            ):
                go()

        first += rows


def fold_wait_send(g, src, src_rows, src_cols, ssem, relay, rsems):
    row, total = src_rows[NORTH]
    own = total - g.relayed

    @pl.when(g.north)
    def _():
        for cc in range(3):
            part = src.at[pl.ds(row, own), pl.ds(*src_cols[cc])]
            wait = pltpu.make_async_copy(part, part, ssem.at[NORTH * 3 + cc]).wait
            if cc == MIDDLE:
                wait()
            else:
                pl.when(across(g, cc - 1) != g.lon)(wait)
        for q, (_, rows) in enumerate(g.relays):
            whole = relay_part(g, relay, src_cols, rows)
            pltpu.make_async_copy(whole, whole, rsems.at[q]).wait()

    for lat, rows in g.relays:

        @pl.when(g.lat == lat)
        def _(rows=rows):
            for cc in range(3):
                part = relay.at[pl.ds(0, rows), pl.ds(*src_cols[cc])]
                pltpu.make_async_copy(part, part, rsems.at[4 + cc]).wait()


def halo_wait_recv(g, dst, rsem, row):
    for cc in range(3):
        if (row, cc) == (CENTER, MIDDLE):
            continue
        part = region(dst, DST_ROWS[row], DST_COLS[cc])
        wait = pltpu.make_async_copy(part, part, rsem.at[row * 3 + cc]).wait
        if row == SOUTH:
            pl.when(g.lat > 0)(wait)
        else:
            wait()


def halo_wait_send(g, src, src_rows, src_cols, ssem):
    for rr, cc in REGIONS:
        here = region(src, src_rows[rr], src_cols[cc])
        wait = pltpu.make_async_copy(here, here, ssem.at[rr * 3 + cc]).wait
        if rr == CENTER:
            wait()
        elif rr == SOUTH:
            pl.when(g.lat > 0)(wait)
        else:
            pl.when(jnp.logical_not(g.north))(wait)


def plane_send(g, src_of, dst, ssem, rsem, slot=None):
    slot = g.plane if slot is None else slot
    for lat, ens in g.peers:
        pltpu.make_async_remote_copy(
            src_ref=src_of(lat * g.nens + ens),
            dst_ref=dst.at[slot],
            send_sem=ssem,
            recv_sem=rsem,
            device_id={"lat": lat, "ens": ens},
            device_id_type=MESH,
        ).start()


def owner_send(g, src, dst, ssem, rsem):
    for o, (lat, ens) in enumerate(g.owner_at):

        @pl.when(g.plane != lat * g.nens + ens)
        def _(o=o, lat=lat, ens=ens):
            pltpu.make_async_remote_copy(
                src_ref=src.at[o],
                dst_ref=dst.at[g.plane],
                send_sem=ssem,
                recv_sem=rsem,
                device_id={"lat": lat, "ens": ens},
                device_id_type=MESH,
            ).start()


def lon_send(g, buf, ssem, rsem):
    for lon in g.lons:
        pltpu.make_async_remote_copy(
            src_ref=buf.at[g.lon],
            dst_ref=buf.at[g.lon],
            send_sem=ssem,
            recv_sem=rsem,
            device_id={"lon": lon},
            device_id_type=MESH,
        ).start()


def bulk_wait(buf, count, sem):
    part = buf.at[pl.ds(0, count)]
    pltpu.make_async_copy(part, part, sem).wait()


FWD_ROWS = {SOUTH: (6, 6), CENTER: (6, 16), NORTH: (16, 6)}
FWD_COLS = {WEST: (1, 1), MIDDLE: (1, 8), EAST: (8, 1)}
BWD_ROWS = {SOUTH: (0, 6), CENTER: (6, 16), NORTH: (22, 6)}
BWD_COLS = {WEST: (0, 1), MIDDLE: (1, 8), EAST: (9, 1)}


def kernel(
    sizes,
    field_h, cotangent_h, mask_h, taps_h, gain_h, shift_h, up_h, down_h,
    output, field_grad, kernel_grad, norm_grad, up_grad, down_grad,
    field, cotangent, mask, taps, gain, shift, up, down,
    ext, sea, ep, kt, ups, mixed, normed, active, pregrad, mp, kacc, uacc, dacc, eg, egs, rb,
    pay1, ra1, zb1, gb1, pay2, ra2, zb2, gb2,
    relay_f, relay_b, ins, fs, fr, bs, br, ar_s, ar_r, rf, rb_s, lon_sem, plane_sem,
):
    g = Grid(*sizes)
    factor = 1.0 / math.sqrt(1024 * g.nlon * g.nlat * g.nens)
    owner = g.owner

    loads = {}
    for k, (name, src, dst) in enumerate(
        (
            ("mask", mask_h, mask),
            ("field", field_h, field),
            ("cotangent", cotangent_h, cotangent),
            ("taps", taps_h, taps),
            ("gain", gain_h, gain),
            ("shift", shift_h, shift),
            ("up", up_h, up),
            ("down", down_h, down),
        )
    ):
        loads[name] = pltpu.make_async_copy(src, dst, ins.at[k])
        loads[name].start()

    barrier = pltpu.get_barrier_semaphore()

    def greet(**where):
        pl.semaphore_signal(barrier, inc=1, device_id=where, device_id_type=MESH)

    for where in g.first:
        greet(**where)
    east = lax.rem(g.lon + 1, g.nlon)
    west = lax.rem(g.lon + g.nlon - 1, g.nlon)

    @pl.when(g.lat > 0)
    def _():
        for lon in (east, west, g.lon):
            greet(lat=g.lat - 1, lon=lon)

    @pl.when(g.lat < g.nlat - 1)
    def _():
        for lon in (east, west, g.lon):
            greet(lat=g.lat + 1, lon=lon)

    relay = jnp.int32(0)
    for lat, _ in g.relays:
        relay = relay + (g.lat == lat).astype(jnp.int32)

        @pl.when(g.north)
        def _(lat=lat):
            for where in g.first[:4]:
                greet(lat=lat, **where)

    def tell(rounds, sem, k):
        for where in rounds[k]:
            pl.semaphore_signal(sem.at[k], inc=1, device_id=where, device_id_type=MESH)

    def hear(rounds, sem, k):
        pl.semaphore_wait(sem.at[k], len(rounds[k]))

    eye = (
        lax.broadcasted_iota(jnp.int32, (64, 64), 0) == lax.broadcasted_iota(jnp.int32, (64, 64), 1)
    )
    ones = jnp.ones((64, 128), BF16)
    loads["mask"].wait()
    loads["field"].wait()
    for r in range(16):
        marks = jnp.broadcast_to(mask[r : r + 1, :].astype(F32), (64, 64))
        spread = jnp.where(eye, marks, 0.0).astype(BF16)
        wide = jnp.dot(spread, ones, preferred_element_type=F32).reshape(8, 8, 128)
        sea[r] = wide
        ext[r + REACH, 1:9] = (field[r].astype(F32) * wide).astype(BF16)

    sides = (g.lat > 0).astype(jnp.int32) + (g.lat < g.nlat - 1).astype(jnp.int32)
    pl.semaphore_wait(barrier, len(g.first) + 3 * sides + 4 * relay)
    tell(g.lon_rounds, lon_sem, 0)
    tell(g.plane_rounds, plane_sem, 0)

    @pl.when(g.north)
    def _():
        relay_send(g, ext, FWD_ROWS, FWD_COLS, relay_f, rf)

    halo_start(g, ext, ext, FWD_ROWS, FWD_COLS, fs, fr, (CENTER, NORTH, SOUTH))


    loads["cotangent"].wait()
    for name in ("taps", "gain", "shift", "up", "down"):
        loads[name].wait()

    def upstream_row(r, carry):
        wide = cotangent[r].astype(F32) * sea[r]
        ups[pl.ds(pl.multiple_of(r * 64, 64), 64), :] = wide.reshape(64, 128).astype(BF16)
        return carry

    lax.fori_loop(0, 16, upstream_row, 0, unroll=4)
    for t in range(TAPS):
        kt[t] = jnp.broadcast_to(taps[t : t + 1, :], (8, 128))
    kacc[...] = jnp.zeros_like(kacc)

    def widen_row(r, carry):
        blocks = ext[r].astype(F32)
        ep[0, r] = blocks
        for k, moved in enumerate(phases_of(blocks)):
            ep[k + 1, r, 0:9] = moved
        return carry

    hear(g.lon_rounds, lon_sem, 0)
    tell(g.lon_rounds, lon_sem, 1)
    hear(g.plane_rounds, plane_sem, 0)
    tell(g.plane_rounds, plane_sem, 1)
    halo_wait_recv(g, ext, fr, CENTER)
    lax.fori_loop(REACH, 16 + REACH, widen_row, 0)

    def conv_row(r, carry):
        total = jnp.zeros((8, 8, 128), F32)
        for i in range(KERNEL):
            for j in range(KERNEL):
                off = 2 + 2 * j
                ph, skip = (off % 8) // 2, off // 8
                total = total + kt[i * KERNEL + j][None] * ep[ph, r + 2 * i, skip : skip + 8]
        mixed[pl.ds(pl.multiple_of(r * 64, 64), 64), :] = total.reshape(64, 128)
        return carry

    gain_row = gain[...]
    shift_row = shift[...]

    def conv_pair(start, taps_i, more):
        def one(r, carry):
            cells = pl.ds(pl.multiple_of(r * 64, 64), 64)
            total = mixed[cells, :].reshape(8, 8, 128) if more else jnp.zeros((8, 8, 128), F32)
            for i in taps_i:
                for j in range(KERNEL):
                    off = 2 + 2 * j
                    ph, skip = (off % 8) // 2, off // 8
                    total = total + kt[i * KERNEL + j][None] * ep[ph, r + 2 * i, skip : skip + 8]
            mixed[cells, :] = total.reshape(64, 128)
            return carry

        lax.fori_loop(start, start + 2, one, 0)

    def group(first, many, conv=True):
        if conv:
            lax.fori_loop(first, first + many, conv_row, 0)
        cells = slice(64 * first, 64 * (first + many))
        rows = slice(first, first + many)
        x = mixed[cells, :]
        centered = x - jnp.mean(x, -1, keepdims=True)
        rstd = lax.rsqrt(jnp.mean(centered * centered, -1, keepdims=True) + 1e-06)
        unit = centered * rstd
        norm = (unit * gain_row + shift_row).astype(BF16)
        normed[cells, :] = norm
        pre = jnp.dot(norm, up[...], preferred_element_type=F32)
        square = pre * pre
        tanh_val = jnp.tanh(pre * (SLOPE + (SLOPE * CUBIC) * square))
        half = 0.5 + 0.5 * tanh_val
        gated = pre * half
        act = gated.astype(BF16)
        active[cells, :] = act
        product = jnp.dot(act, down[...], preferred_element_type=F32).reshape(many, 8, 8, 128)
        output[rows] = ((field[rows].astype(F32) + product) * sea[rows]).astype(BF16)
        act_grad = rdot(ups[cells, :], down[...])
        deriv = half + gated * (1.0 - tanh_val) * (SLOPE + (3.0 * SLOPE * CUBIC) * square)
        pre_grad = (act_grad * deriv).astype(BF16)
        pregrad[cells, :] = pre_grad
        nig = rdot(pre_grad, up[...])
        scaled = nig * gain_row
        kacc[TAPS] += jnp.sum((nig * unit).reshape(8 * many, 8, 128), 0)
        kacc[TAPS + 1] += jnp.sum(nig.reshape(8 * many, 8, 128), 0)
        mg = rstd * (
            scaled
            - jnp.mean(scaled, -1, keepdims=True)
            - unit * jnp.mean(scaled * unit, -1, keepdims=True)
        )
        mp[0, rows, 1:9] = mg.reshape(many, 8, 8, 128)

    zero_block = jnp.zeros((1, 8, 128), F32)

    def spread_row(r, carry):
        mp[0, r, 0:1] = zero_block
        blocks = jnp.concatenate([zero_block, mp[0, r, 1:9], zero_block], 0)
        for k, moved in enumerate(phases_of(blocks)):
            mp[k + 1, r] = moved
        return carry

    def tap_row(r, carry):
        grad = mp[0, r, 1:9]
        for i in range(KERNEL):
            for j in range(KERNEL):
                off = 2 + 2 * j
                ph, skip = (off % 8) // 2, off // 8
                kacc[i * KERNEL + j] += jnp.sum(grad * ep[ph, r + 2 * i, skip : skip + 8], 0)
        return carry

    crossing = jnp.logical_or(g.north, relay > 0)

    @pl.when(crossing)
    def _():
        hear(g.lon_rounds, lon_sem, 1)

    @pl.when(g.north)
    def _():
        fold_own(g, ext, ext, FWD_ROWS, FWD_COLS, fs, fr)

    fold_pass_on(g, ext, FWD_COLS, fr, relay_f, rf)
    group(6, 4)
    hear(g.plane_rounds, plane_sem, 1)
    tell(g.plane_rounds, plane_sem, 2)
    halo_wait_recv(g, ext, fr, SOUTH)

    @pl.when(g.lat == 0)
    def _():
        ext[0:REACH] = jnp.zeros((REACH, 10, 8, 128), BF16)

    lax.fori_loop(0, REACH, widen_row, 0)

    group(0, 6)
    hear(g.plane_rounds, plane_sem, 2)
    tell(g.plane_rounds, plane_sem, 3)
    lax.fori_loop(0, 10, tap_row, 0)
    hear(g.plane_rounds, plane_sem, 3)
    tell(g.plane_rounds, plane_sem, 4)
    lax.fori_loop(0, 10, spread_row, 0)
    uacc[...] = tdot(normed[0:640, :], pregrad[0:640, :])
    dacc[...] = tdot(active[0:640, :], ups[0:640, :])
    for m in range(3):
        conv_pair(10 + 2 * m, range(6 - m), False)
    halo_wait_recv(g, ext, fr, NORTH)

    flip = (
        lax.broadcasted_iota(jnp.int32, (80, 80), 0)
        + lax.broadcasted_iota(jnp.int32, (80, 80), 1)
        == 79
    ).astype(F32).astype(BF16)

    @pl.when(jnp.logical_not(g.north))
    def _():
        lax.fori_loop(16 + REACH, 16 + 2 * REACH, widen_row, 0)

    @pl.when(g.north)
    def _():
        for k in range(REACH):
            row = ext[16 + REACH + k].astype(F32).reshape(80, 128).astype(BF16)
            turned = jnp.dot(flip, row, preferred_element_type=F32).reshape(10, 8, 128)
            r = 16 + 2 * REACH - 1 - k
            ep[0, r] = turned
            for s, moved in enumerate(phases_of(turned)):
                ep[s + 1, r, 0:9] = moved

    for m in range(3):
        conv_pair(10 + 2 * m, range(6 - m, KERNEL), True)
    group(10, 6, False)
    def eg_row(p, first, last):
        lo = jnp.zeros((9, 8, 128), F32)
        hi = jnp.zeros((9, 8, 128), F32)
        for i in range(first, last + 1):
            for j in range(KERNEL):
                off = 14 - 2 * j
                ph, skip = (off % 8) // 2, off // 8
                term = kt[i * KERNEL + j][None] * mp[ph, p - 2 * i]
                if skip:
                    lo = lo + term
                else:
                    hi = hi + term
        return jnp.concatenate([lo, zero_block], 0) + jnp.concatenate([zero_block, hi], 0)

    def eg_halo(start, first, last):
        def one(p, carry):
            egs[p] = eg_row(p, first, last).astype(BF16)
            return carry

        lax.fori_loop(start, start + 2, one, 0)

    def eg_center(start, stop, first, last):
        def one(p, carry):
            value = eg_row(p, first, last)
            eg[p - REACH] = value[1:9]
            egs[p, 0:1] = value[0:1].astype(BF16)
            egs[p, 9:10] = value[9:10].astype(BF16)
            return carry

        lax.fori_loop(start, stop, one, 0)

    chunk = 512 // g.planes
    per = 128 // chunk
    up_part = (uacc[...] + tdot(normed[640:1024, :], pregrad[640:1024, :])).astype(BF16)
    pay1[0:per] = up_part[:, 0:128].reshape(per, chunk, 128)
    pay1[per : 2 * per] = up_part[:, 128:256].reshape(per, chunk, 128)
    down_part = (dacc[...] + tdot(active[640:1024, :], ups[640:1024, :])).astype(BF16)
    pay1[2 * per : 4 * per] = down_part.reshape(2 * per, chunk, 128)
    ra1[g.plane] = pay1[g.plane]
    hear(g.plane_rounds, plane_sem, 4)
    plane_send(g, lambda peer: pay1.at[peer], ra1, ar_s.at[0], ar_r.at[0])

    lax.fori_loop(10, 16, tap_row, 0)
    small = 64 // g.owners
    pay2[...] = jnp.sum(kacc[...], 1).reshape(g.owners, small, 128).astype(BF16)

    @pl.when(owner)
    def _():
        ra2[g.plane] = pay2[g.owned]

    owner_send(g, pay2, ra2, ar_s.at[1], ar_r.at[1])

    lax.fori_loop(10, 16, spread_row, 0)

    for m in range(3):
        eg_halo(22 + 2 * m, 4 + m, 6)
    halo_start(g, egs, rb, BWD_ROWS, BWD_COLS, bs, br, (NORTH,))

    @pl.when(g.north)
    def _():
        relay_send(g, egs, BWD_ROWS, BWD_COLS, relay_b, rb_s)
        fold_own(g, egs, rb, BWD_ROWS, BWD_COLS, bs, br)


    for m in range(3):
        eg_halo(2 * m, 0, m)
    halo_start(g, egs, rb, BWD_ROWS, BWD_COLS, bs, br, (SOUTH,))
    for m in range(3, 6):
        eg_center(2 * m, 2 * m + 2, 0, m)
    eg_center(12, 16, 0, 6)
    for m in range(3):
        eg_center(16 + 2 * m, 18 + 2 * m, 1 + m, 6)
    halo_start(g, egs, rb, BWD_ROWS, BWD_COLS, bs, br, (CENTER,))
    fold_pass_on(g, rb, BWD_COLS, br, relay_b, rb_s)

    @pl.when(jnp.logical_not(crossing))
    def _():
        hear(g.lon_rounds, lon_sem, 1)

    bulk_wait(ra1, g.planes - 1, ar_r.at[0])
    zb1[g.lon] = jnp.sum(ra1[...].astype(F32), 0).astype(BF16)
    lon_send(g, zb1, ar_s.at[2], ar_r.at[2])

    @pl.when(owner)
    def _():
        bulk_wait(ra2, g.planes - 1, ar_r.at[1])
        zb2[g.lon] = jnp.sum(ra2[...].astype(F32), 0).astype(BF16)
        lon_send(g, zb2, ar_s.at[3], ar_r.at[3])

    bulk_wait(zb1, g.nlon - 1, ar_r.at[2])
    gb1[g.plane] = jnp.sum(zb1[...].astype(F32), 0).astype(BF16)
    plane_send(g, lambda peer: gb1.at[g.plane], gb1, ar_s.at[4], ar_r.at[4])

    @pl.when(owner)
    def _():
        bulk_wait(zb2, g.nlon - 1, ar_r.at[3])
        gb2[g.owned] = jnp.sum(zb2[...].astype(F32), 0).astype(BF16)
        plane_send(g, lambda peer: gb2.at[g.owned], gb2, ar_s.at[5], ar_r.at[5], g.owned)

    halo_wait_recv(g, rb, br, CENTER)

    def edge_row(r, carry):
        eg[r, 0:1] += rb[r + REACH, 0:1].astype(F32)
        eg[r, 7:8] += rb[r + REACH, 9:10].astype(F32)
        return carry

    lax.fori_loop(0, 16, edge_row, 0)
    halo_wait_recv(g, rb, br, SOUTH)

    def fold_in(r, row):
        eg[r] += row[1:9]
        eg[r, 0:1] += row[0:1]
        eg[r, 7:8] += row[9:10]

    @pl.when(g.lat > 0)
    def _():
        def one(k, carry):
            fold_in(k, rb[k].astype(F32))
            return carry

        lax.fori_loop(0, REACH, one, 0)

    halo_wait_recv(g, rb, br, NORTH)

    @pl.when(jnp.logical_not(g.north))
    def _():
        def one(k, carry):
            fold_in(10 + k, rb[22 + k].astype(F32))
            return carry

        lax.fori_loop(0, REACH, one, 0)

    @pl.when(g.north)
    def _():
        for k in range(REACH):
            row = rb[22 + k].astype(F32).reshape(80, 128).astype(BF16)
            fold_in(15 - k, jnp.dot(flip, row, preferred_element_type=F32).reshape(10, 8, 128))

    def last_row(r, carry):
        field_grad[r] = ((cotangent[r].astype(F32) + eg[r]) * sea[r]).astype(BF16)
        return carry

    lax.fori_loop(0, 16, last_row, 0, unroll=2)

    bulk_wait(gb1, g.planes - 1, ar_r.at[4])
    up_grad[:, 0:128] = gb1[0:per].astype(F32).reshape(128, 128) * factor
    up_grad[:, 128:256] = gb1[per : 2 * per].astype(F32).reshape(128, 128) * factor
    down_grad[...] = gb1[2 * per : 4 * per].astype(F32).reshape(256, 128) * factor

    @pl.when(owner)
    def _():
        bulk_wait(gb2, g.owners - 1, ar_r.at[5])

    @pl.when(jnp.logical_not(owner))
    def _():
        bulk_wait(gb2, g.owners, ar_r.at[5])

    small_sums = gb2[...].astype(F32).reshape(64, 128) * factor
    kernel_grad[...] = small_sums[0:TAPS]
    norm_grad[...] = small_sums[TAPS : TAPS + 2]

    halo_wait_send(g, ext, FWD_ROWS, FWD_COLS, fs)
    halo_wait_send(g, egs, BWD_ROWS, BWD_COLS, bs)
    fold_wait_send(g, ext, FWD_ROWS, FWD_COLS, fs, relay_f, rf)
    fold_wait_send(g, egs, BWD_ROWS, BWD_COLS, bs, relay_b, rb_s)
    bulk_wait(pay1, g.planes - 1, ar_s.at[0])
    bulk_wait(zb1, g.nlon - 1, ar_s.at[2])
    bulk_wait(gb1, g.planes - 1, ar_s.at[4])

    @pl.when(owner)
    def _():
        bulk_wait(pay2, g.owners - 1, ar_s.at[1])
        bulk_wait(zb2, g.nlon - 1, ar_s.at[3])
        bulk_wait(ra2, g.planes - 1, ar_s.at[5])

    @pl.when(jnp.logical_not(owner))
    def _():
        bulk_wait(pay2, g.owners, ar_s.at[1])


def write_out(*refs):
    sems = refs[-1]
    half = len(refs) // 2
    copies = [
        pltpu.make_async_copy(src, dst, sems.at[k])
        for k, (src, dst) in enumerate(zip(refs[:half], refs[half:-1]))
    ]
    for copy in copies:
        copy.start()
    for copy in copies:
        copy.wait()


def shards(sizes, field, cotangent, land_mask, kernel_taps, norm_gain, norm_shift, up_weight, down_weight):
    planes = sizes[1] * sizes[2]
    owners = min(8, planes)
    chunk, small = 512 // planes, 64 // owners
    tile = (16, 8, 8, 128)
    vmem = pl.BlockSpec(memory_space=pltpu.VMEM)
    hbm = pl.BlockSpec(memory_space=pltpu.HBM)
    dma = pltpu.SemaphoreType.DMA
    results = (
        jax.ShapeDtypeStruct(tile, BF16),
        jax.ShapeDtypeStruct(tile, BF16),
        jax.ShapeDtypeStruct((TAPS, 128), F32),
        jax.ShapeDtypeStruct((2, 128), F32),
        jax.ShapeDtypeStruct((128, 256), F32),
        jax.ShapeDtypeStruct((256, 128), F32),
    )
    held = pl.pallas_call(
        functools.partial(kernel, sizes),
        out_shape=results,
        in_specs=[hbm] * 8,
        out_specs=(vmem,) * 6,
        scratch_shapes=[
            pltpu.VMEM(tile, BF16),
            pltpu.VMEM(tile, BF16),
            pltpu.VMEM((16, 64), jnp.int32),
            pltpu.VMEM((TAPS, 128), F32),
            pltpu.VMEM((1, 128), F32),
            pltpu.VMEM((1, 128), F32),
            pltpu.VMEM((128, 256), BF16),
            pltpu.VMEM((256, 128), BF16),
            pltpu.VMEM((28, 10, 8, 128), BF16),
            pltpu.VMEM(tile, F32),
            pltpu.VMEM((4, 28, 10, 8, 128), F32),
            pltpu.VMEM((TAPS, 8, 128), F32),
            pltpu.VMEM((1024, 128), BF16),
            pltpu.VMEM((1024, 128), F32),
            pltpu.VMEM((1024, 128), BF16),
            pltpu.VMEM((1024, 256), BF16),
            pltpu.VMEM((1024, 256), BF16),
            pltpu.VMEM((4, 16, 9, 8, 128), F32),
            pltpu.VMEM((64, 8, 128), F32),
            pltpu.VMEM((128, 256), F32),
            pltpu.VMEM((256, 128), F32),
            pltpu.VMEM(tile, F32),
            pltpu.VMEM((28, 10, 8, 128), BF16),
            pltpu.VMEM((28, 10, 8, 128), BF16),
            pltpu.VMEM((planes, chunk, 128), BF16),
            pltpu.VMEM((planes, chunk, 128), BF16),
            pltpu.VMEM((sizes[0], chunk, 128), BF16),
            pltpu.VMEM((planes, chunk, 128), BF16),
            pltpu.VMEM((owners, small, 128), BF16),
            pltpu.VMEM((planes, small, 128), BF16),
            pltpu.VMEM((sizes[0], small, 128), BF16),
            pltpu.VMEM((owners, small, 128), BF16),
            pltpu.VMEM((2, 10, 8, 128), BF16),
            pltpu.VMEM((2, 10, 8, 128), BF16),
            dma((8,)),
            dma((9,)),
            dma((9,)),
            dma((9,)),
            dma((9,)),
            dma((6,)),
            dma((6,)),
            dma((7,)),
            dma((7,)),
            pltpu.SemaphoreType.REGULAR((2,)),
            pltpu.SemaphoreType.REGULAR((5,)),
        ],
        compiler_params=pltpu.CompilerParams(
            collective_id=0, has_side_effects=True, vmem_limit_bytes=48 * 1024 * 1024
        ),
        name="ocean_block",
    )(
        *(
            pltpu.with_memory_space_constraint(x, pltpu.HBM)
            for x in (
                field.reshape(tile),
                cotangent.reshape(tile),
                land_mask,
                kernel_taps,
                norm_gain.reshape(1, 128),
                norm_shift.reshape(1, 128),
                up_weight,
                down_weight,
            )
        )
    )
    out = pl.pallas_call(
        write_out,
        out_shape=results,
        in_specs=[vmem] * 6,
        out_specs=(hbm,) * 6,
        scratch_shapes=[dma((6,))],
        compiler_params=pltpu.CompilerParams(vmem_limit_bytes=8 * 1024 * 1024),
        name="write_out",
    )(*held)
    return (out[0].reshape(field.shape), out[1].reshape(field.shape)) + tuple(out[2:])


def solution(mesh):
    sizes = (mesh.shape["lon"], mesh.shape["lat"], mesh.shape["ens"])
    tiles = P("ens", "lat", "lon", None)
    in_specs = (tiles, tiles, P("lat", "lon"), P(), P(), P(), P(), P())
    out_specs = (tiles, tiles, P(), P(), P(), P())
    return jax.shard_map(
        functools.partial(shards, sizes),
        mesh=mesh,
        in_specs=in_specs,
        out_specs=out_specs,
        check_vma=False,
    )
```

```python
import functools
import math

import jax
import jax.numpy as jnp
from jax import lax
from jax.experimental import pallas as pl
from jax.experimental.pallas import tpu as pltpu
from jax.sharding import PartitionSpec as P

KERNEL = 7
REACH = 6
TAPS = KERNEL * KERNEL
MESH = pl.DeviceIdType.MESH
F32 = jnp.float32
BF16 = jnp.bfloat16
SLOPE = math.sqrt(2.0 / math.pi)
CUBIC = 0.044715

SOUTH, CENTER, NORTH = 0, 1, 2
WEST, MIDDLE, EAST = 0, 1, 2


def rdot(a, b):
    return lax.dot_general(a, b, (((1,), (1,)), ((), ())), preferred_element_type=F32)


def tdot(a, b):
    return lax.dot_general(a, b, (((0,), (0,)), ((), ())), preferred_element_type=F32)


def phases_of(blocks):
    count = blocks.shape[0]
    sub = lax.broadcasted_iota(jnp.int32, (count - 1, 8, 128), 1)
    out = []
    for shift in (2, 4, 6):
        rolled = pltpu.roll(blocks, 8 - shift, 1)
        out.append(jnp.where(sub < 8 - shift, rolled[: count - 1], rolled[1:]))
    return out


def region(ref, rows, cols):
    return ref.at[pl.ds(*rows), pl.ds(*cols)]


DST_ROWS = {SOUTH: (0, 6), CENTER: (6, 16), NORTH: (22, 6)}
DST_COLS = {WEST: (0, 1), MIDDLE: (1, 8), EAST: (9, 1)}
REGIONS = [(r, c) for r in range(3) for c in range(3) if (r, c) != (CENTER, MIDDLE)]


class Grid:
    def __init__(self, nlon, nlat, nens):
        self.nlon, self.nlat, self.nens = nlon, nlat, nens
        self.lon = lax.axis_index("lon")
        self.lat = lax.axis_index("lat")
        self.ens = lax.axis_index("ens")
        self.north = self.lat == nlat - 1
        self.plane = self.lat * nens + self.ens
        self.planes = nlat * nens
        if nlat == 8 and nens == 4:
            self.owner_at = [(lat, ens) for lat in (0, 2, 4, 6) for ens in (0, 2)]
            self.owner = (lax.rem(self.lat, 2) + lax.rem(self.ens, 2)) == 0
            self.owned = self.lat // 2 * 2 + self.ens // 2
        else:
            self.owner_at = [(p // nens, p % nens) for p in range(min(8, self.planes))]
            self.owner = self.plane < len(self.owner_at)
            self.owned = self.plane
        self.owners = len(self.owner_at)
        self.relays = ((nlat - 3, 2), (1, 2)) if nlat == 8 else ()
        self.relayed = sum(rows for _, rows in self.relays)
        across, along = nlat // 2, nens // 2 * 2
        y = self.ens // 2 * 2 + lax.rem(self.lat, 2)
        core = lax.rem(self.ens, 2)
        hop = lambda d: {"lon": lax.rem(self.lon + d + nlon, nlon)}
        x, low, high = self.lat // 2, lax.rem(self.lat, 2), self.ens // 2
        self.first = [hop(d) for d in (1, -1, 2, -2)]
        self.lon_rounds = [[hop(d), hop(-d)] for d in (2, 4) if 2 * d <= nlon]
        twin = {"ens": high * 2 + (1 - core)}
        beside = {"lat": x * 2 + (1 - low)}
        self.plane_rounds = [[twin], [beside]]
        if along == 4:
            self.plane_rounds.insert(1, [{"ens": (1 - high) * 2 + core}])
        if across == 4:
            ring = [{"lat": lax.rem(x + d, 4) * 2 + low} for d in (1, 3)]
            self.plane_rounds += [ring, ring]
        for near in self.plane_rounds[: 3 if along == 4 else 2] + self.plane_rounds[3:4]:
            self.first += near
        xs = [lax.rem(self.lat // 2 + d, across) for d in range(across)]
        ys = [lax.rem(y + d, along) for d in range(along)]
        steps = [(dx, dy, dc) for dx in range(across) for dy in range(along) for dc in range(2)][1:]
        steps.sort(key=lambda s: -min(s[0], across - s[0]) - min(s[1], along - s[1]))
        self.peers = []
        for dx, dy, dc in steps:
            lat = xs[dx] * 2 + lax.rem(ys[dy], 2)
            ens = ys[dy] // 2 * 2 + (1 - core if dc else core)
            self.peers.append((lat, ens))
        far = sorted(range(1, nlon), key=lambda k: -min(k, nlon - k))
        self.lons = [lax.rem(self.lon + k, nlon) for k in far]


def halo_start(g, src, dst, src_rows, src_cols, ssem, rsem, only_rows):
    for rr, cc in sorted(REGIONS, key=lambda rc: only_rows.index(rc[0]) if rc[0] in only_rows else 9):
        if rr not in only_rows:
            continue
        here = region(src, src_rows[rr], src_cols[cc])
        land_c = 2 - cc
        step = cc - 1
        east = lax.rem(g.lon + step + g.nlon, g.nlon)

        def send(lat, lon, land_r, here=here, rr=rr, cc=cc, land_c=land_c):
            pltpu.make_async_remote_copy(
                src_ref=here,
                dst_ref=region(dst, DST_ROWS[land_r], DST_COLS[land_c]),
                send_sem=ssem.at[rr * 3 + cc],
                recv_sem=rsem.at[land_r * 3 + land_c],
                device_id={"lon": lon, "lat": lat},
                device_id_type=MESH,
            ).start()

        if rr == CENTER:
            send(g.lat, east, CENTER)
        elif rr == SOUTH:

            @pl.when(g.lat > 0)
            def _(send=send, east=east):
                send(g.lat - 1, east, NORTH)

        else:

            @pl.when(jnp.logical_not(g.north))
            def _(send=send, east=east):
                send(g.lat + 1, east, SOUTH)


def across(g, step):
    return lax.rem(2 * g.nlon - 1 - g.lon - step, g.nlon)


def fold_sends(g, here, dst, dst_row, count, cols, ssem, rsem, first_row):
    for cc in (MIDDLE, EAST, WEST):
        lon = across(g, cc - 1)
        part = here.at[pl.ds(first_row, count), pl.ds(*cols[cc])]
        land = dst.at[pl.ds(dst_row, count), pl.ds(*DST_COLS[2 - cc])]
        arrived = rsem.at[NORTH * 3 + 2 - cc]

        def go(part=part, land=land, arrived=arrived, lon=lon, cc=cc):
            pltpu.make_async_remote_copy(
                src_ref=part,
                dst_ref=land,
                send_sem=ssem(cc),
                recv_sem=arrived,
                device_id={"lon": lon, "lat": g.nlat - 1},
                device_id_type=MESH,
            ).start()

        yield cc, lon, part, land, arrived, go


def relay_part(g, relay, src_cols, rows):
    low, high = src_cols[WEST][0], src_cols[EAST][0] + 1
    return relay.at[pl.ds(0, rows), pl.ds(low, high - low)]


def relay_send(g, src, src_rows, src_cols, relay, rsems):
    low, high = src_cols[WEST][0], src_cols[EAST][0] + 1
    first = sum(src_rows[NORTH]) - g.relayed
    for q, (lat, rows) in enumerate(g.relays):
        pltpu.make_async_remote_copy(
            src_ref=src.at[pl.ds(first, rows), pl.ds(low, high - low)],
            dst_ref=relay_part(g, relay, src_cols, rows),
            send_sem=rsems.at[q],
            recv_sem=rsems.at[3],
            device_id={"lat": lat},
            device_id_type=MESH,
        ).start()
        first += rows


def fold_own(g, src, dst, src_rows, src_cols, ssem, rsem):
    row, total = src_rows[NORTH]
    for cc, lon, part, land, arrived, go in fold_sends(
        g,
        src,
        dst,
        DST_ROWS[NORTH][0],
        total - g.relayed,
        src_cols,
        lambda cc: ssem.at[NORTH * 3 + cc],
        rsem,
        row,
    ):
        if cc == MIDDLE:
            go()
        else:
            pl.when(lon != g.lon)(go)

            @pl.when(lon == g.lon)
            def _(part=part, land=land, arrived=arrived):
                pltpu.make_async_copy(part, land, arrived).start()


def fold_pass_on(g, dst, src_cols, rsem, relay, rsems):
    first = DST_ROWS[NORTH][0] + DST_ROWS[NORTH][1] - g.relayed
    for lat, rows in g.relays:

        @pl.when(g.lat == lat)
        def _(first=first, rows=rows):
            part = relay_part(g, relay, src_cols, rows)
            pltpu.make_async_copy(part, part, rsems.at[3]).wait()
            for cc, lon, _, _, _, go in fold_sends(
                g, relay, dst, first, rows, src_cols, lambda cc: rsems.at[4 + cc], rsem, 0
            ):
                go()

        first += rows


def fold_wait_send(g, src, src_rows, src_cols, ssem, relay, rsems):
    row, total = src_rows[NORTH]
    own = total - g.relayed

    @pl.when(g.north)
    def _():
        for cc in range(3):
            part = src.at[pl.ds(row, own), pl.ds(*src_cols[cc])]
            wait = pltpu.make_async_copy(part, part, ssem.at[NORTH * 3 + cc]).wait
            if cc == MIDDLE:
                wait()
            else:
                pl.when(across(g, cc - 1) != g.lon)(wait)
        for q, (_, rows) in enumerate(g.relays):
            whole = relay_part(g, relay, src_cols, rows)
            pltpu.make_async_copy(whole, whole, rsems.at[q]).wait()

    for lat, rows in g.relays:

        @pl.when(g.lat == lat)
        def _(rows=rows):
            for cc in range(3):
                part = relay.at[pl.ds(0, rows), pl.ds(*src_cols[cc])]
                pltpu.make_async_copy(part, part, rsems.at[4 + cc]).wait()


def halo_wait_recv(g, dst, rsem, row):
    for cc in range(3):
        if (row, cc) == (CENTER, MIDDLE):
            continue
        part = region(dst, DST_ROWS[row], DST_COLS[cc])
        wait = pltpu.make_async_copy(part, part, rsem.at[row * 3 + cc]).wait
        if row == SOUTH:
            pl.when(g.lat > 0)(wait)
        else:
            wait()


def halo_wait_send(g, src, src_rows, src_cols, ssem):
    for rr, cc in REGIONS:
        here = region(src, src_rows[rr], src_cols[cc])
        wait = pltpu.make_async_copy(here, here, ssem.at[rr * 3 + cc]).wait
        if rr == CENTER:
            wait()
        elif rr == SOUTH:
            pl.when(g.lat > 0)(wait)
        else:
            pl.when(jnp.logical_not(g.north))(wait)


def plane_send(g, src_of, dst, ssem, rsem, slot=None):
    slot = g.plane if slot is None else slot
    for lat, ens in g.peers:
        pltpu.make_async_remote_copy(
            src_ref=src_of(lat * g.nens + ens),
            dst_ref=dst.at[slot],
            send_sem=ssem,
            recv_sem=rsem,
            device_id={"lat": lat, "ens": ens},
            device_id_type=MESH,
        ).start()


def owner_send(g, src, dst, ssem, rsem):
    for o, (lat, ens) in enumerate(g.owner_at):

        @pl.when(g.plane != lat * g.nens + ens)
        def _(o=o, lat=lat, ens=ens):
            pltpu.make_async_remote_copy(
                src_ref=src.at[o],
                dst_ref=dst.at[g.plane],
                send_sem=ssem,
                recv_sem=rsem,
                device_id={"lat": lat, "ens": ens},
                device_id_type=MESH,
            ).start()


def lon_send(g, buf, ssem, rsem):
    for lon in g.lons:
        pltpu.make_async_remote_copy(
            src_ref=buf.at[g.lon],
            dst_ref=buf.at[g.lon],
            send_sem=ssem,
            recv_sem=rsem,
            device_id={"lon": lon},
            device_id_type=MESH,
        ).start()


def bulk_wait(buf, count, sem):
    part = buf.at[pl.ds(0, count)]
    pltpu.make_async_copy(part, part, sem).wait()


FWD_ROWS = {SOUTH: (6, 6), CENTER: (6, 16), NORTH: (16, 6)}
FWD_COLS = {WEST: (1, 1), MIDDLE: (1, 8), EAST: (8, 1)}
BWD_ROWS = {SOUTH: (0, 6), CENTER: (6, 16), NORTH: (22, 6)}
BWD_COLS = {WEST: (0, 1), MIDDLE: (1, 8), EAST: (9, 1)}


def kernel(
    sizes,
    field_h, cotangent_h, mask_h, taps_h, gain_h, shift_h, up_h, down_h,
    output, field_grad, kernel_grad, norm_grad, up_grad, down_grad,
    field, cotangent, mask, taps, gain, shift, up, down,
    ext, sea, ep, kt, ups, mixed, normed, active, pregrad, mp, kacc, uacc, dacc, eg, egs, rb,
    pay1, ra1, zb1, gb1, pay2, ra2, zb2, gb2,
    relay_f, relay_b, ins, fs, fr, bs, br, ar_s, ar_r, rf, rb_s, lon_sem, plane_sem,
):
    g = Grid(*sizes)
    factor = 1.0 / math.sqrt(1024 * g.nlon * g.nlat * g.nens)
    owner = g.owner

    loads = {}
    for k, (name, src, dst) in enumerate(
        (
            ("mask", mask_h, mask),
            ("field", field_h, field),
            ("cotangent", cotangent_h, cotangent),
            ("taps", taps_h, taps),
            ("gain", gain_h, gain),
            ("shift", shift_h, shift),
            ("up", up_h, up),
            ("down", down_h, down),
        )
    ):
        loads[name] = pltpu.make_async_copy(src, dst, ins.at[k])
        loads[name].start()

    barrier = pltpu.get_barrier_semaphore()

    def greet(**where):
        pl.semaphore_signal(barrier, inc=1, device_id=where, device_id_type=MESH)

    for where in g.first:
        greet(**where)
    east = lax.rem(g.lon + 1, g.nlon)
    west = lax.rem(g.lon + g.nlon - 1, g.nlon)

    @pl.when(g.lat > 0)
    def _():
        for lon in (east, west, g.lon):
            greet(lat=g.lat - 1, lon=lon)

    @pl.when(g.lat < g.nlat - 1)
    def _():
        for lon in (east, west, g.lon):
            greet(lat=g.lat + 1, lon=lon)

    relay = jnp.int32(0)
    for lat, _ in g.relays:
        relay = relay + (g.lat == lat).astype(jnp.int32)

        @pl.when(g.north)
        def _(lat=lat):
            for where in g.first[:4]:
                greet(lat=lat, **where)

    def tell(rounds, sem, k):
        for where in rounds[k]:
            pl.semaphore_signal(sem.at[k], inc=1, device_id=where, device_id_type=MESH)

    def hear(rounds, sem, k):
        pl.semaphore_wait(sem.at[k], len(rounds[k]))

    eye = (
        lax.broadcasted_iota(jnp.int32, (64, 64), 0) == lax.broadcasted_iota(jnp.int32, (64, 64), 1)
    )
    ones = jnp.ones((64, 128), BF16)
    loads["mask"].wait()
    loads["field"].wait()
    for r in range(16):
        marks = jnp.broadcast_to(mask[r : r + 1, :].astype(F32), (64, 64))
        spread = jnp.where(eye, marks, 0.0).astype(BF16)
        wide = jnp.dot(spread, ones, preferred_element_type=F32).reshape(8, 8, 128)
        sea[r] = wide
        ext[r + REACH, 1:9] = (field[r].astype(F32) * wide).astype(BF16)

    sides = (g.lat > 0).astype(jnp.int32) + (g.lat < g.nlat - 1).astype(jnp.int32)
    pl.semaphore_wait(barrier, len(g.first) + 3 * sides + 4 * relay)
    tell(g.lon_rounds, lon_sem, 0)
    tell(g.plane_rounds, plane_sem, 0)

    @pl.when(g.north)
    def _():
        relay_send(g, ext, FWD_ROWS, FWD_COLS, relay_f, rf)

    halo_start(g, ext, ext, FWD_ROWS, FWD_COLS, fs, fr, (CENTER, NORTH, SOUTH))


    loads["cotangent"].wait()
    for name in ("taps", "gain", "shift", "up", "down"):
        loads[name].wait()

    def upstream_row(r, carry):
        wide = cotangent[r].astype(F32) * sea[r]
        ups[pl.ds(pl.multiple_of(r * 64, 64), 64), :] = wide.reshape(64, 128).astype(BF16)
        return carry

    lax.fori_loop(0, 16, upstream_row, 0, unroll=4)
    for t in range(TAPS):
        kt[t] = jnp.broadcast_to(taps[t : t + 1, :], (8, 128))
    kacc[...] = jnp.zeros_like(kacc)

    def widen_row(r, carry):
        blocks = ext[r].astype(F32)
        ep[0, r] = blocks
        for k, moved in enumerate(phases_of(blocks)):
            ep[k + 1, r, 0:9] = moved
        return carry

    hear(g.lon_rounds, lon_sem, 0)
    tell(g.lon_rounds, lon_sem, 1)
    hear(g.plane_rounds, plane_sem, 0)
    tell(g.plane_rounds, plane_sem, 1)
    halo_wait_recv(g, ext, fr, CENTER)
    lax.fori_loop(REACH, 16 + REACH, widen_row, 0)

    def conv_row(r, carry):
        total = jnp.zeros((8, 8, 128), F32)
        for i in range(KERNEL):
            for j in range(KERNEL):
                off = 2 + 2 * j
                ph, skip = (off % 8) // 2, off // 8
                total = total + kt[i * KERNEL + j][None] * ep[ph, r + 2 * i, skip : skip + 8]
        mixed[pl.ds(pl.multiple_of(r * 64, 64), 64), :] = total.reshape(64, 128)
        return carry

    gain_row = gain[...]
    shift_row = shift[...]

    def conv_pair(start, taps_i, more):
        def one(r, carry):
            cells = pl.ds(pl.multiple_of(r * 64, 64), 64)
            total = mixed[cells, :].reshape(8, 8, 128) if more else jnp.zeros((8, 8, 128), F32)
            for i in taps_i:
                for j in range(KERNEL):
                    off = 2 + 2 * j
                    ph, skip = (off % 8) // 2, off // 8
                    total = total + kt[i * KERNEL + j][None] * ep[ph, r + 2 * i, skip : skip + 8]
            mixed[cells, :] = total.reshape(64, 128)
            return carry

        lax.fori_loop(start, start + 2, one, 0)

    def group(first, many, conv=True):
        if conv:
            lax.fori_loop(first, first + many, conv_row, 0)
        cells = slice(64 * first, 64 * (first + many))
        rows = slice(first, first + many)
        x = mixed[cells, :]
        centered = x - jnp.mean(x, -1, keepdims=True)
        rstd = lax.rsqrt(jnp.mean(centered * centered, -1, keepdims=True) + 1e-06)
        unit = centered * rstd
        norm = (unit * gain_row + shift_row).astype(BF16)
        normed[cells, :] = norm
        pre = jnp.dot(norm, up[...], preferred_element_type=F32)
        square = pre * pre
        tanh_val = jnp.tanh(pre * (SLOPE + (SLOPE * CUBIC) * square))
        half = 0.5 + 0.5 * tanh_val
        gated = pre * half
        act = gated.astype(BF16)
        active[cells, :] = act
        product = jnp.dot(act, down[...], preferred_element_type=F32).reshape(many, 8, 8, 128)
        output[rows] = ((field[rows].astype(F32) + product) * sea[rows]).astype(BF16)
        act_grad = rdot(ups[cells, :], down[...])
        deriv = half + gated * (1.0 - tanh_val) * (SLOPE + (3.0 * SLOPE * CUBIC) * square)
        pre_grad = (act_grad * deriv).astype(BF16)
        pregrad[cells, :] = pre_grad
        nig = rdot(pre_grad, up[...])
        scaled = nig * gain_row
        kacc[TAPS] += jnp.sum((nig * unit).reshape(8 * many, 8, 128), 0)
        kacc[TAPS + 1] += jnp.sum(nig.reshape(8 * many, 8, 128), 0)
        mg = rstd * (
            scaled
            - jnp.mean(scaled, -1, keepdims=True)
            - unit * jnp.mean(scaled * unit, -1, keepdims=True)
        )
        mp[0, rows, 1:9] = mg.reshape(many, 8, 8, 128)

    zero_block = jnp.zeros((1, 8, 128), F32)

    def spread_row(r, carry):
        mp[0, r, 0:1] = zero_block
        blocks = jnp.concatenate([zero_block, mp[0, r, 1:9], zero_block], 0)
        for k, moved in enumerate(phases_of(blocks)):
            mp[k + 1, r] = moved
        return carry

    def tap_row(r, carry):
        grad = mp[0, r, 1:9]
        for i in range(KERNEL):
            for j in range(KERNEL):
                off = 2 + 2 * j
                ph, skip = (off % 8) // 2, off // 8
                kacc[i * KERNEL + j] += jnp.sum(grad * ep[ph, r + 2 * i, skip : skip + 8], 0)
        return carry

    crossing = jnp.logical_or(g.north, relay > 0)

    @pl.when(crossing)
    def _():
        hear(g.lon_rounds, lon_sem, 1)

    @pl.when(g.north)
    def _():
        fold_own(g, ext, ext, FWD_ROWS, FWD_COLS, fs, fr)

    fold_pass_on(g, ext, FWD_COLS, fr, relay_f, rf)
    group(6, 4)
    hear(g.plane_rounds, plane_sem, 1)
    tell(g.plane_rounds, plane_sem, 2)
    halo_wait_recv(g, ext, fr, SOUTH)

    @pl.when(g.lat == 0)
    def _():
        ext[0:REACH] = jnp.zeros((REACH, 10, 8, 128), BF16)

    lax.fori_loop(0, REACH, widen_row, 0)

    group(0, 6)
    hear(g.plane_rounds, plane_sem, 2)
    tell(g.plane_rounds, plane_sem, 3)
    lax.fori_loop(0, 10, tap_row, 0)
    lax.fori_loop(0, 10, spread_row, 0)
    uacc[...] = tdot(normed[0:640, :], pregrad[0:640, :])
    dacc[...] = tdot(active[0:640, :], ups[0:640, :])
    for m in range(3):
        conv_pair(10 + 2 * m, range(6 - m), False)
    hear(g.plane_rounds, plane_sem, 3)
    tell(g.plane_rounds, plane_sem, 4)
    halo_wait_recv(g, ext, fr, NORTH)

    flip = (
        lax.broadcasted_iota(jnp.int32, (80, 80), 0)
        + lax.broadcasted_iota(jnp.int32, (80, 80), 1)
        == 79
    ).astype(F32).astype(BF16)

    @pl.when(jnp.logical_not(g.north))
    def _():
        lax.fori_loop(16 + REACH, 16 + 2 * REACH, widen_row, 0)

    @pl.when(g.north)
    def _():
        for k in range(REACH):
            row = ext[16 + REACH + k].astype(F32).reshape(80, 128).astype(BF16)
            turned = jnp.dot(flip, row, preferred_element_type=F32).reshape(10, 8, 128)
            r = 16 + 2 * REACH - 1 - k
            ep[0, r] = turned
            for s, moved in enumerate(phases_of(turned)):
                ep[s + 1, r, 0:9] = moved

    for m in range(3):
        conv_pair(10 + 2 * m, range(6 - m, KERNEL), True)
    group(10, 6, False)
    def eg_row(p, first, last):
        lo = jnp.zeros((9, 8, 128), F32)
        hi = jnp.zeros((9, 8, 128), F32)
        for i in range(first, last + 1):
            for j in range(KERNEL):
                off = 14 - 2 * j
                ph, skip = (off % 8) // 2, off // 8
                term = kt[i * KERNEL + j][None] * mp[ph, p - 2 * i]
                if skip:
                    lo = lo + term
                else:
                    hi = hi + term
        return jnp.concatenate([lo, zero_block], 0) + jnp.concatenate([zero_block, hi], 0)

    def eg_halo(start, first, last):
        def one(p, carry):
            egs[p] = eg_row(p, first, last).astype(BF16)
            return carry

        lax.fori_loop(start, start + 2, one, 0)

    def eg_center(start, stop, first, last):
        def one(p, carry):
            value = eg_row(p, first, last)
            eg[p - REACH] = value[1:9]
            egs[p, 0:1] = value[0:1].astype(BF16)
            egs[p, 9:10] = value[9:10].astype(BF16)
            return carry

        lax.fori_loop(start, stop, one, 0)

    chunk = 512 // g.planes
    per = 128 // chunk
    up_part = (uacc[...] + tdot(normed[640:1024, :], pregrad[640:1024, :])).astype(BF16)
    pay1[0:per] = up_part[:, 0:128].reshape(per, chunk, 128)
    pay1[per : 2 * per] = up_part[:, 128:256].reshape(per, chunk, 128)
    down_part = (dacc[...] + tdot(active[640:1024, :], ups[640:1024, :])).astype(BF16)
    pay1[2 * per : 4 * per] = down_part.reshape(2 * per, chunk, 128)
    ra1[g.plane] = pay1[g.plane]
    hear(g.plane_rounds, plane_sem, 4)
    plane_send(g, lambda peer: pay1.at[peer], ra1, ar_s.at[0], ar_r.at[0])

    lax.fori_loop(10, 16, tap_row, 0)
    small = 64 // g.owners
    pay2[...] = jnp.sum(kacc[...], 1).reshape(g.owners, small, 128).astype(BF16)

    @pl.when(owner)
    def _():
        ra2[g.plane] = pay2[g.owned]

    owner_send(g, pay2, ra2, ar_s.at[1], ar_r.at[1])

    lax.fori_loop(10, 16, spread_row, 0)

    for m in range(3):
        eg_halo(22 + 2 * m, 4 + m, 6)
    halo_start(g, egs, rb, BWD_ROWS, BWD_COLS, bs, br, (NORTH,))

    @pl.when(g.north)
    def _():
        relay_send(g, egs, BWD_ROWS, BWD_COLS, relay_b, rb_s)
        fold_own(g, egs, rb, BWD_ROWS, BWD_COLS, bs, br)


    for m in range(3):
        eg_halo(2 * m, 0, m)
    halo_start(g, egs, rb, BWD_ROWS, BWD_COLS, bs, br, (SOUTH,))
    for m in range(3, 6):
        eg_center(2 * m, 2 * m + 2, 0, m)
    eg_center(12, 16, 0, 6)
    for m in range(3):
        eg_center(16 + 2 * m, 18 + 2 * m, 1 + m, 6)
    halo_start(g, egs, rb, BWD_ROWS, BWD_COLS, bs, br, (CENTER,))
    fold_pass_on(g, rb, BWD_COLS, br, relay_b, rb_s)

    @pl.when(jnp.logical_not(crossing))
    def _():
        hear(g.lon_rounds, lon_sem, 1)

    bulk_wait(ra1, g.planes - 1, ar_r.at[0])
    zb1[g.lon] = jnp.sum(ra1[...].astype(F32), 0).astype(BF16)
    lon_send(g, zb1, ar_s.at[2], ar_r.at[2])

    @pl.when(owner)
    def _():
        bulk_wait(ra2, g.planes - 1, ar_r.at[1])
        zb2[g.lon] = jnp.sum(ra2[...].astype(F32), 0).astype(BF16)
        lon_send(g, zb2, ar_s.at[3], ar_r.at[3])

    bulk_wait(zb1, g.nlon - 1, ar_r.at[2])
    gb1[g.plane] = jnp.sum(zb1[...].astype(F32), 0).astype(BF16)
    plane_send(g, lambda peer: gb1.at[g.plane], gb1, ar_s.at[4], ar_r.at[4])

    @pl.when(owner)
    def _():
        bulk_wait(zb2, g.nlon - 1, ar_r.at[3])
        gb2[g.owned] = jnp.sum(zb2[...].astype(F32), 0).astype(BF16)
        plane_send(g, lambda peer: gb2.at[g.owned], gb2, ar_s.at[5], ar_r.at[5], g.owned)

    halo_wait_recv(g, rb, br, CENTER)

    def edge_row(r, carry):
        eg[r, 0:1] += rb[r + REACH, 0:1].astype(F32)
        eg[r, 7:8] += rb[r + REACH, 9:10].astype(F32)
        return carry

    lax.fori_loop(0, 16, edge_row, 0)
    halo_wait_recv(g, rb, br, SOUTH)

    def fold_in(r, row):
        eg[r] += row[1:9]
        eg[r, 0:1] += row[0:1]
        eg[r, 7:8] += row[9:10]

    @pl.when(g.lat > 0)
    def _():
        def one(k, carry):
            fold_in(k, rb[k].astype(F32))
            return carry

        lax.fori_loop(0, REACH, one, 0)

    halo_wait_recv(g, rb, br, NORTH)

    @pl.when(jnp.logical_not(g.north))
    def _():
        def one(k, carry):
            fold_in(10 + k, rb[22 + k].astype(F32))
            return carry

        lax.fori_loop(0, REACH, one, 0)

    @pl.when(g.north)
    def _():
        for k in range(REACH):
            row = rb[22 + k].astype(F32).reshape(80, 128).astype(BF16)
            fold_in(15 - k, jnp.dot(flip, row, preferred_element_type=F32).reshape(10, 8, 128))

    def last_row(r, carry):
        field_grad[r] = ((cotangent[r].astype(F32) + eg[r]) * sea[r]).astype(BF16)
        return carry

    lax.fori_loop(0, 16, last_row, 0, unroll=2)

    bulk_wait(gb1, g.planes - 1, ar_r.at[4])
    up_grad[:, 0:128] = gb1[0:per].astype(F32).reshape(128, 128) * factor
    up_grad[:, 128:256] = gb1[per : 2 * per].astype(F32).reshape(128, 128) * factor
    down_grad[...] = gb1[2 * per : 4 * per].astype(F32).reshape(256, 128) * factor

    @pl.when(owner)
    def _():
        bulk_wait(gb2, g.owners - 1, ar_r.at[5])

    @pl.when(jnp.logical_not(owner))
    def _():
        bulk_wait(gb2, g.owners, ar_r.at[5])

    small_sums = gb2[...].astype(F32).reshape(64, 128) * factor
    kernel_grad[...] = small_sums[0:TAPS]
    norm_grad[...] = small_sums[TAPS : TAPS + 2]

    halo_wait_send(g, ext, FWD_ROWS, FWD_COLS, fs)
    halo_wait_send(g, egs, BWD_ROWS, BWD_COLS, bs)
    fold_wait_send(g, ext, FWD_ROWS, FWD_COLS, fs, relay_f, rf)
    fold_wait_send(g, egs, BWD_ROWS, BWD_COLS, bs, relay_b, rb_s)
    bulk_wait(pay1, g.planes - 1, ar_s.at[0])
    bulk_wait(zb1, g.nlon - 1, ar_s.at[2])
    bulk_wait(gb1, g.planes - 1, ar_s.at[4])

    @pl.when(owner)
    def _():
        bulk_wait(pay2, g.owners - 1, ar_s.at[1])
        bulk_wait(zb2, g.nlon - 1, ar_s.at[3])
        bulk_wait(ra2, g.planes - 1, ar_s.at[5])

    @pl.when(jnp.logical_not(owner))
    def _():
        bulk_wait(pay2, g.owners, ar_s.at[1])


def write_out(*refs):
    sems = refs[-1]
    half = len(refs) // 2
    copies = [
        pltpu.make_async_copy(src, dst, sems.at[k])
        for k, (src, dst) in enumerate(zip(refs[:half], refs[half:-1]))
    ]
    for copy in copies:
        copy.start()
    for copy in copies:
        copy.wait()


def shards(sizes, field, cotangent, land_mask, kernel_taps, norm_gain, norm_shift, up_weight, down_weight):
    planes = sizes[1] * sizes[2]
    owners = min(8, planes)
    chunk, small = 512 // planes, 64 // owners
    tile = (16, 8, 8, 128)
    vmem = pl.BlockSpec(memory_space=pltpu.VMEM)
    hbm = pl.BlockSpec(memory_space=pltpu.HBM)
    dma = pltpu.SemaphoreType.DMA
    results = (
        jax.ShapeDtypeStruct(tile, BF16),
        jax.ShapeDtypeStruct(tile, BF16),
        jax.ShapeDtypeStruct((TAPS, 128), F32),
        jax.ShapeDtypeStruct((2, 128), F32),
        jax.ShapeDtypeStruct((128, 256), F32),
        jax.ShapeDtypeStruct((256, 128), F32),
    )
    held = pl.pallas_call(
        functools.partial(kernel, sizes),
        out_shape=results,
        in_specs=[hbm] * 8,
        out_specs=(vmem,) * 6,
        scratch_shapes=[
            pltpu.VMEM(tile, BF16),
            pltpu.VMEM(tile, BF16),
            pltpu.VMEM((16, 64), jnp.int32),
            pltpu.VMEM((TAPS, 128), F32),
            pltpu.VMEM((1, 128), F32),
            pltpu.VMEM((1, 128), F32),
            pltpu.VMEM((128, 256), BF16),
            pltpu.VMEM((256, 128), BF16),
            pltpu.VMEM((28, 10, 8, 128), BF16),
            pltpu.VMEM(tile, F32),
            pltpu.VMEM((4, 28, 10, 8, 128), F32),
            pltpu.VMEM((TAPS, 8, 128), F32),
            pltpu.VMEM((1024, 128), BF16),
            pltpu.VMEM((1024, 128), F32),
            pltpu.VMEM((1024, 128), BF16),
            pltpu.VMEM((1024, 256), BF16),
            pltpu.VMEM((1024, 256), BF16),
            pltpu.VMEM((4, 16, 9, 8, 128), F32),
            pltpu.VMEM((64, 8, 128), F32),
            pltpu.VMEM((128, 256), F32),
            pltpu.VMEM((256, 128), F32),
            pltpu.VMEM(tile, F32),
            pltpu.VMEM((28, 10, 8, 128), BF16),
            pltpu.VMEM((28, 10, 8, 128), BF16),
            pltpu.VMEM((planes, chunk, 128), BF16),
            pltpu.VMEM((planes, chunk, 128), BF16),
            pltpu.VMEM((sizes[0], chunk, 128), BF16),
            pltpu.VMEM((planes, chunk, 128), BF16),
            pltpu.VMEM((owners, small, 128), BF16),
            pltpu.VMEM((planes, small, 128), BF16),
            pltpu.VMEM((sizes[0], small, 128), BF16),
            pltpu.VMEM((owners, small, 128), BF16),
            pltpu.VMEM((2, 10, 8, 128), BF16),
            pltpu.VMEM((2, 10, 8, 128), BF16),
            dma((8,)),
            dma((9,)),
            dma((9,)),
            dma((9,)),
            dma((9,)),
            dma((6,)),
            dma((6,)),
            dma((7,)),
            dma((7,)),
            pltpu.SemaphoreType.REGULAR((2,)),
            pltpu.SemaphoreType.REGULAR((5,)),
        ],
        compiler_params=pltpu.CompilerParams(
            collective_id=0, has_side_effects=True, vmem_limit_bytes=48 * 1024 * 1024
        ),
        name="ocean_block",
    )(
        *(
            pltpu.with_memory_space_constraint(x, pltpu.HBM)
            for x in (
                field.reshape(tile),
                cotangent.reshape(tile),
                land_mask,
                kernel_taps,
                norm_gain.reshape(1, 128),
                norm_shift.reshape(1, 128),
                up_weight,
                down_weight,
            )
        )
    )
    out = pl.pallas_call(
        write_out,
        out_shape=results,
        in_specs=[vmem] * 6,
        out_specs=(hbm,) * 6,
        scratch_shapes=[dma((6,))],
        compiler_params=pltpu.CompilerParams(vmem_limit_bytes=8 * 1024 * 1024),
        name="write_out",
    )(*held)
    return (out[0].reshape(field.shape), out[1].reshape(field.shape)) + tuple(out[2:])


def solution(mesh):
    sizes = (mesh.shape["lon"], mesh.shape["lat"], mesh.shape["ens"])
    tiles = P("ens", "lat", "lon", None)
    in_specs = (tiles, tiles, P("lat", "lon"), P(), P(), P(), P(), P())
    out_specs = (tiles, tiles, P(), P(), P(), P())
    return jax.shard_map(
        functools.partial(shards, sizes),
        mesh=mesh,
        in_specs=in_specs,
        out_specs=out_specs,
        check_vma=False,
    )
```
